128 devices in a mesh: node: 16 (over x, y), head: 8 (over z, core).
Axes of the slice: x: 4, y: 4, z: 4, core: 2. Of those that a mesh axis runs over, the one named last changes fastest.
Arguments:
- features: bfloat16 [131072, 768], P(('node', 'head'))
- w_query: bfloat16 [768, 768], replicated
- w_key: bfloat16 [768, 768], replicated
- w_value: bfloat16 [768, 768], replicated, may hold values from -0.86328125 to 0.86328125
- w_out: bfloat16 [768, 768], replicated, may hold values from -0.21875 to 0.21875
- w_up: bfloat16 [768, 1536], replicated, may hold values from -0.21875 to 0.21875
- w_down: bfloat16 [1536, 768], replicated, may hold values from -0.21875 to 0.21875
- gain_attn: float32 [768], replicated, may hold values from 0.25 to 1.75
- gain_ffn: float32 [768], replicated, may hold values from 0.25 to 1.75
- send_list: int32 [16, 16, 16], P('node'), may hold values from 0 to 127
- edge_owner: int32 [2048, 8], P('node'), may hold values from 0 to 15
- edge_slot: int32 [2048, 8], P('node'), may hold values from 0 to 15
- edge_count: int32 [2048], P('node'), may hold values from 1 to 8, as said below
Outputs:
- layer_out: bfloat16 [131072, 768], P(('node', 'head'))
The draws below stay inside these ranges and needn't reach their ends.
Inputs may be any that keep to these rules, and one draw needn't show every extreme that they name: `edge_count`: at least one query block uses 1 entry; every query block of every fourth node group (0, 4, 8, ...) uses all 8.
All inputs are finite; a program needn't handle non-finite values.
Results may differ from the reference program's by a relative error of at most 0.0076.
Values may be sent and summed in bfloat16 or wider, within the bound.
No kernel may reach another device: no remote copies, remote signals or barrier semaphores. Data moves between devices by JAX's collectives and lax.ppermute only.
A program may use at most 128 MiB of HBM per device.

```python
import math
import jax
import jax.numpy as jnp
from jax import lax

D = 768
HEADS = 12
HDIM = 64
FF = 1536
BLOCK = 64
MAXK = 8
CAP = 16
GROUPS = 16
NODES = 131072
BPG = 128
QBLOCKS = 2048


def paired_weights(key):
    base = jax.random.normal(jax.random.fold_in(key, 11), (D, D), jnp.float32)
    other = jax.random.normal(jax.random.fold_in(key, 12), (D, D), jnp.float32)
    base = jnp.clip(base, -6.0, 6.0) / math.sqrt(D)
    other = jnp.clip(other, -6.0, 6.0) / math.sqrt(D)
    return (base, other)


def draw_w_query(key, part):
    base, other = paired_weights(key)
    return base.astype(jnp.bfloat16)


def draw_w_key(key, part):
    base, other = paired_weights(key)
    result = other
    return result.astype(jnp.bfloat16)


def draw_features(key, part):
    noise = jnp.clip(jax.random.normal(jax.random.fold_in(key, 21), (NODES, D), jnp.float32), -6.0, 6.0)
    result = noise
    return result.astype(jnp.bfloat16)


def draw_send_list(key, part):
    chosen = jax.random.randint(key, (GROUPS, GROUPS, CAP), 0, BPG, dtype=jnp.int32)
    chosen = chosen.at[0, 0, 0].set(BPG - 1)
    chosen = chosen.at[0, 0, 1].set(0)
    return chosen


def draw_edge_count(key, part):
    counts = jax.random.randint(key, (QBLOCKS,), 1, MAXK + 1, dtype=jnp.int32)
    group_ids = jnp.arange(QBLOCKS, dtype=jnp.int32) // BPG
    counts = jnp.where(group_ids % 4 == 0, MAXK, counts)
    counts = counts.at[BPG].set(1)
    return counts.astype(jnp.int32)


def with_ends(drawn, own_key, smallest, high):
    longest = drawn.shape.index(max(drawn.shape))
    spots = []
    for shift in (0, 1):
        where = [jax.random.randint(jax.random.fold_in(own_key, axis), (), 0, length) for axis, length in enumerate(drawn.shape)]
        where[longest] = (where[longest] + shift) % drawn.shape[longest]
        spots.append(tuple(where))
    return drawn.at[spots[0]].set(smallest).at[spots[1]].set(high)


def bell_draw(stream_key, dims, width, most, held_as=jnp.bfloat16):
    entries = jax.random.normal(stream_key, dims, jnp.float32) * width
    return jnp.minimum(jnp.maximum(entries, -most), most).astype(held_as)


def setup_inputs(seed: int = 0) -> dict:
    key_list = jax.random.split(jax.random.key(seed), 14)
    return {
        "features": draw_features(jax.random.fold_in(key_list[13], 71), 0),
        "w_query": draw_w_query(jax.random.fold_in(key_list[13], 71), 0),
        "w_key": draw_w_key(jax.random.fold_in(key_list[13], 71), 0),
        "w_value": bell_draw(key_list[3], (D, D), (4.0 / D ** 0.5), 0.86328125),
        "w_out": bell_draw(key_list[4], (D, D), D ** -0.5, 0.21875),
        "w_up": bell_draw(key_list[5], (D, FF), D ** -0.5, 0.21875),
        "w_down": bell_draw(key_list[6], (FF, D), (FF // 2) ** -0.5, 0.21875),
        "gain_attn": jnp.clip(1.0 + 0.15 * jax.random.normal(key_list[7], (D,), jnp.float32), 0.25, 1.75),
        "gain_ffn": jnp.clip(1.0 + 0.15 * jax.random.normal(key_list[8], (D,), jnp.float32), 0.25, 1.75),
        "send_list": draw_send_list(jax.random.fold_in(key_list[13], 71), 0),
        "edge_owner": with_ends(jax.random.randint(key_list[10], (QBLOCKS, MAXK), 0, GROUPS), jax.random.fold_in(key_list[10], 1), 0, GROUPS - 1).astype(jnp.int32),
        "edge_slot": with_ends(jax.random.randint(key_list[11], (QBLOCKS, MAXK), 0, CAP), jax.random.fold_in(key_list[11], 1), 0, CAP - 1).astype(jnp.int32),
        "edge_count": draw_edge_count(jax.random.fold_in(key_list[13], 71), 0),
    }


def normed(values, gain):
    center = values - lax.optimization_barrier(jnp.mean(values, axis=-1, keepdims=True))
    spread = lax.optimization_barrier(jnp.mean(center * center, axis=-1, keepdims=True))
    return center * lax.rsqrt(spread + 1e-05) * gain.astype(jnp.float32)

def reference(features, w_query, w_key, w_value, w_out, w_up, w_down, gain_attn, gain_ffn, send_list, edge_owner, edge_slot, edge_count):
    queries = jnp.dot(features, w_query, preferred_element_type=jnp.float32).astype(jnp.bfloat16)
    keys = jnp.dot(features, w_key, preferred_element_type=jnp.float32).astype(jnp.bfloat16)
    values = jnp.dot(features, w_value, preferred_element_type=jnp.float32).astype(jnp.bfloat16)
    blocks = jnp.arange(QBLOCKS, dtype=jnp.int32)
    reader = blocks // BPG
    picked = send_list[edge_owner, reader[:, None], edge_slot]
    kblock = (edge_owner * BPG + picked).astype(jnp.int32)
    listed = jnp.concatenate([blocks[:, None], kblock], axis=1)
    offsets = jnp.arange(BLOCK, dtype=jnp.int32)
    slot_ids = jnp.arange(MAXK + 1, dtype=jnp.int32)

    def one_block(args):
        block, block_list, count = args
        rows = (block_list[:, None] * BLOCK + offsets[None, :]).reshape(-1)
        query_rows = lax.dynamic_slice_in_dim(queries, (block * BLOCK).astype(jnp.int32), BLOCK, 0)
        query_rows = query_rows.astype(jnp.float32).reshape(BLOCK, HEADS, HDIM)
        key_rows = keys[rows].astype(jnp.float32).reshape(-1, HEADS, HDIM)
        value_rows = values[rows].astype(jnp.float32).reshape(-1, HEADS, HDIM)
        scores = jnp.einsum('qhd,khd->hqk', query_rows, key_rows) / math.sqrt(HDIM)
        valid = jnp.logical_or(slot_ids == 0, slot_ids - 1 < count)
        valid = jnp.repeat(valid, BLOCK)
        scores = jnp.where(valid[None, None, :], scores, -1e+30)
        top = lax.optimization_barrier(jnp.max(scores, axis=-1, keepdims=True))
        weights = jnp.exp(scores - top)
        probs = (weights / lax.optimization_barrier(jnp.sum(weights, axis=-1, keepdims=True))).astype(jnp.bfloat16)
        result = jnp.einsum('hqk,khd->qhd', probs.astype(jnp.float32), value_rows)
        return result.astype(jnp.bfloat16).reshape(BLOCK, D)
    attended = lax.map(one_block, (blocks, listed, edge_count)).reshape(NODES, D)
    mixed = features.astype(jnp.float32) + jnp.dot(attended, w_out, preferred_element_type=jnp.float32)
    first = normed(mixed, gain_attn).astype(jnp.bfloat16)
    hidden = jnp.maximum(jnp.dot(first, w_up, preferred_element_type=jnp.float32), 0.0).astype(jnp.bfloat16)
    total = first.astype(jnp.float32) + jnp.dot(hidden, w_down, preferred_element_type=jnp.float32)
    return normed(total, gain_ffn).astype(jnp.bfloat16)
```

```python
import functools
import math

import jax
import jax.numpy as jnp
from jax import lax
from jax.experimental import pallas as pl
from jax.experimental.pallas import tpu as pltpu
from jax.sharding import PartitionSpec as P

HDIM = 64
BLOCK = 64
MAXK = 8
CAP = 16
HALF = BLOCK // 2
LANES = 2 * HDIM
CHUNKS = 3
QUADS = 4
LOG2E = 1.4426950408889634
F32 = jnp.float32
BF16 = jnp.bfloat16
VMEM = pl.BlockSpec(memory_space=pltpu.VMEM)
SMEM = pl.BlockSpec(memory_space=pltpu.SMEM)
ANY = pl.BlockSpec(memory_space=pl.ANY)
LIMIT = 60 * 1024 * 1024


def low_lanes(rows):
    return lax.broadcasted_iota(jnp.int32, (rows, LANES), 1) < HDIM


def pack_pair(both):
    blocks = both.shape[0] // BLOCK
    split = both.reshape(blocks, 2, HALF, LANES)
    first = split[:, 0].reshape(blocks * HALF, LANES)
    second = split[:, 1].reshape(blocks * HALF, LANES)
    low = low_lanes(blocks * HALF)
    even = jnp.where(low, first, pltpu.roll(second, HDIM, 1))
    odd = jnp.where(low, pltpu.roll(first, HDIM, 1), second)
    return even.reshape(blocks, HALF, LANES), odd.reshape(blocks, HALF, LANES)


def unpack_pair(even, odd):
    blocks = even.shape[0]
    even = even.reshape(blocks * HALF, LANES).astype(F32)
    odd = odd.reshape(blocks * HALF, LANES).astype(F32)
    low = low_lanes(blocks * HALF)
    first = jnp.where(low, even, pltpu.roll(odd, HDIM, 1)).reshape(blocks, 1, HALF, LANES)
    second = jnp.where(low, pltpu.roll(even, HDIM, 1), odd).reshape(blocks, 1, HALF, LANES)
    return jnp.concatenate([first, second], axis=1).reshape(blocks * BLOCK, LANES)


def keys_values_kernel(feat_ref, key_ref, value_ref, out_ref):
    for half in range(2):
        rows = feat_ref[half * 512 : half * 512 + 512, :]
        for kind, w_ref in enumerate((key_ref, value_ref)):
            made = jnp.dot(rows, w_ref[...], preferred_element_type=F32)
            for pair in range(2):
                packed = pack_pair(made[:, pair * LANES : (pair + 1) * LANES])
                for side in range(2):
                    dest = 2 * (2 * pair + side) + kind
                    out_ref[dest, half * 8 : half * 8 + 8] = packed[side].astype(BF16)


def queries_kernel(feat_ref, query_ref, out_ref):
    for half in range(2):
        rows = feat_ref[half * 512 : half * 512 + 512, :]
        made = jnp.dot(rows, query_ref[...], preferred_element_type=F32)
        for pair in range(2):
            packed = pack_pair(made[:, pair * LANES : (pair + 1) * LANES])
            for side in range(2):
                out_ref[2 * (2 * pair + side) + half] = packed[side].astype(BF16)


def project_keys_values(features, w_key, w_value, chunk):
    rows, width = features.shape
    cols = QUADS * HDIM
    return pl.pallas_call(
        keys_values_kernel,
        grid=(1,),
        in_specs=[
            pl.BlockSpec((rows, width), lambda i: (0, 0)),
            pl.BlockSpec((width, cols), lambda i: (0, chunk)),
            pl.BlockSpec((width, cols), lambda i: (0, chunk)),
        ],
        out_specs=pl.BlockSpec((8, 16, HALF, LANES), lambda i: (0, 0, 0, 0)),
        out_shape=jax.ShapeDtypeStruct((8, 16, HALF, LANES), BF16),
        compiler_params=pltpu.CompilerParams(vmem_limit_bytes=LIMIT),
        cost_estimate=pl.CostEstimate(flops=4 * rows * width * cols, bytes_accessed=5 << 20, transcendentals=0),
        name="keys_values",
    )(features, w_key, w_value)


def project_queries(features, w_query, chunk):
    rows, width = features.shape
    cols = QUADS * HDIM
    return pl.pallas_call(
        queries_kernel,
        grid=(1,),
        in_specs=[
            pl.BlockSpec((rows, width), lambda i: (0, 0)),
            pl.BlockSpec((width, cols), lambda i: (0, chunk)),
        ],
        out_specs=pl.BlockSpec((8, 8, HALF, LANES), lambda i: (0, 0, 0, 0)),
        out_shape=jax.ShapeDtypeStruct((8, 8, HALF, LANES), BF16),
        compiler_params=pltpu.CompilerParams(vmem_limit_bytes=LIMIT),
        cost_estimate=pl.CostEstimate(flops=2 * rows * width * cols, bytes_accessed=3 << 20, transcendentals=0),
        name="queries",
    )(features, w_query)


def collect_kernel(list_ref, core_ref, held_ref, out_ref, swap_ref):
    def body(step, carry):
        for extra in range(8):
            slot = step * 8 + extra
            out_ref[slot] = held_ref[list_ref[slot]]
        return carry

    lax.fori_loop(0, out_ref.shape[0] // 8, body, 0)
    other = 1 - core_ref[0]
    for source in range(8):
        swap_ref[source] = held_ref[pl.ds(source * 16 + other * 8, 8)]


def collect(held, flat_list, core):
    slots = flat_list.shape[0]
    return pl.pallas_call(
        collect_kernel,
        in_specs=[SMEM, SMEM, VMEM],
        out_specs=[VMEM, VMEM],
        out_shape=[
            jax.ShapeDtypeStruct((slots, HALF, LANES), BF16),
            jax.ShapeDtypeStruct((8, 8, HALF, LANES), BF16),
        ],
        compiler_params=pltpu.CompilerParams(vmem_limit_bytes=LIMIT),
        cost_estimate=pl.CostEstimate(flops=0, bytes_accessed=4 << 20, transcendentals=0),
        name="collect",
    )(flat_list, core, held)


def attend_kernel(
    id_ref, count_ref, core_ref, query_ref, held_ref, swap_ref, mine_ref, other_ref,
    out_ref, keys, values, own_keys, own_values, sems,
):
    core = core_ref[0]

    def fetch(which, near, near_own, far, far_own):
        copies = [
            pltpu.make_async_copy(held_ref.at[:, which], near_own, sems.at[0]),
            pltpu.make_async_copy(swap_ref, far_own, sems.at[1]),
            pltpu.make_async_copy(mine_ref, near, sems.at[2]),
            pltpu.make_async_copy(other_ref, far, sems.at[3]),
        ]
        for copy in copies:
            copy.start()
        for copy in copies:
            copy.wait()

    @pl.when(core == 0)
    def _():
        fetch(0, keys, own_keys, values, own_values)

    @pl.when(core == 1)
    def _():
        fetch(1, values, own_values, keys, own_keys)

    low = low_lanes(HALF)
    lane = lax.broadcasted_iota(jnp.int32, (1, MAXK * HALF), 1)
    dims = (((1,), (1,)), ((), ()))

    def unit(source, place):
        block = source * 16 + core * 8 + place
        query = query_ref[source, place].astype(F32)
        turned = pltpu.roll(query, HDIM, 1)
        zero = jnp.zeros_like(query)
        left = jnp.concatenate(
            [
                jnp.where(low, query, zero),
                jnp.where(low, turned, zero),
                jnp.where(low, zero, turned),
                jnp.where(low, zero, query),
            ],
            axis=0,
        ).astype(BF16)
        slots = [id_ref[block * MAXK + entry] for entry in range(MAXK)]
        far_keys = jnp.concatenate([keys[slot] for slot in slots], axis=0)
        far = lax.dot_general(left, far_keys, dims, preferred_element_type=F32)
        near = lax.dot_general(left, own_keys[source, place], dims, preferred_element_type=F32)
        far = jnp.where(lane < count_ref[block] * HALF, far, -8e30)
        top = jnp.maximum(
            jnp.max(far, axis=1, keepdims=True), jnp.max(near, axis=1, keepdims=True)
        )
        top = jnp.maximum(top[:BLOCK], top[BLOCK:])
        top = jnp.concatenate([top, top], axis=0)
        scale = LOG2E / math.sqrt(HDIM)
        far = jnp.exp2((far - top) * scale)
        near = jnp.exp2((near - top) * scale)
        total = jnp.sum(far, axis=1, keepdims=True) + jnp.sum(near, axis=1, keepdims=True)
        total = total[:BLOCK] + total[BLOCK:]
        far_values = jnp.concatenate([values[slot] for slot in slots], axis=0)
        summed = jnp.dot(far.astype(BF16), far_values, preferred_element_type=F32)
        summed = summed + jnp.dot(
            near.astype(BF16), own_values[source, place], preferred_element_type=F32
        )
        straight = jnp.where(low, summed[:HALF], summed[3 * HALF :])
        crossed = jnp.where(low, summed[HALF : 2 * HALF], summed[2 * HALF : 3 * HALF])
        result = straight + pltpu.roll(crossed, HDIM, 1)
        share = 1.0 / total
        share = jnp.where(low, share[:HALF], share[HALF:])
        out_ref[source, place] = (result * share).astype(BF16)

    def body(step, carry):
        for extra in range(2):
            at = step * 2 + extra
            unit(at // 8, at % 8)
        return carry

    lax.fori_loop(0, 32, body, 0)


def attend(ids, counts, core, queries, held, swapped, mine, other):
    slots = mine.shape[0]
    return pl.pallas_call(
        attend_kernel,
        in_specs=[SMEM, SMEM, SMEM, VMEM, ANY, ANY, ANY, ANY],
        out_specs=VMEM,
        out_shape=jax.ShapeDtypeStruct((8, 8, HALF, LANES), BF16),
        scratch_shapes=[
            pltpu.VMEM((slots, HALF, LANES), BF16),
            pltpu.VMEM((slots, HALF, LANES), BF16),
            pltpu.VMEM((8, 8, HALF, LANES), BF16),
            pltpu.VMEM((8, 8, HALF, LANES), BF16),
            pltpu.SemaphoreType.DMA((4,)),
        ],
        compiler_params=pltpu.CompilerParams(vmem_limit_bytes=LIMIT),
        cost_estimate=pl.CostEstimate(
            flops=64 * 4 * 128 * 128 * 288, bytes_accessed=6 << 20, transcendentals=64 * 128 * 288
        ),
        name="attend",
    )(ids, counts, core, queries, held.reshape(8, 2, 8, HALF, LANES), swapped, mine, other)


def normed(values, gain):
    center = values - jnp.mean(values, axis=-1, keepdims=True)
    spread = jnp.mean(center * center, axis=-1, keepdims=True)
    return center * lax.rsqrt(spread + 1e-05) * gain


def finish_kernel(feat_ref, *refs):
    backs = refs[:CHUNKS]
    out_w_ref, up_ref, down_ref, gain_a_ref, gain_f_ref, result_ref = refs[CHUNKS:]
    mixed = feat_ref[...].astype(F32)
    for chunk, back in enumerate(backs):
        pieces = [unpack_pair(back[2 * pair, 0], back[2 * pair + 1, 0]) for pair in range(2)]
        attended = jnp.concatenate(pieces, axis=1).astype(BF16)
        mixed = mixed + jnp.dot(
            attended,
            out_w_ref[chunk * QUADS * HDIM : (chunk + 1) * QUADS * HDIM, :],
            preferred_element_type=F32,
        )
    first = normed(mixed, gain_a_ref[...]).astype(BF16)
    hidden = jnp.maximum(jnp.dot(first, up_ref[...], preferred_element_type=F32), 0.0).astype(BF16)
    total = first.astype(F32) + jnp.dot(hidden, down_ref[...], preferred_element_type=F32)
    result_ref[...] = normed(total, gain_f_ref[...]).astype(BF16)


def finish(features, backs, w_out, w_up, w_down, gain_attn, gain_ffn):
    rows, width = features.shape
    tile = rows // 2

    def once(shape):
        return pl.BlockSpec(shape, lambda i: (0,) * len(shape), pipeline_mode=pl.Buffered(1))

    return pl.pallas_call(
        finish_kernel,
        grid=(2,),
        in_specs=[pl.BlockSpec((tile, width), lambda i: (i, 0))]
        + [pl.BlockSpec((4, 1, 8, HALF, LANES), lambda i: (0, i, 0, 0, 0))] * CHUNKS
        + [
            once(w_out.shape),
            once(w_up.shape),
            once(w_down.shape),
            once((1, width)),
            once((1, width)),
        ],
        out_specs=pl.BlockSpec((tile, width), lambda i: (i, 0)),
        out_shape=jax.ShapeDtypeStruct((rows, width), BF16),
        compiler_params=pltpu.CompilerParams(vmem_limit_bytes=LIMIT),
        name="finish",
    )(
        features,
        *[back.reshape(4, 2, 8, HALF, LANES) for back in backs],
        w_out,
        w_up,
        w_down,
        gain_attn.reshape(1, width),
        gain_ffn.reshape(1, width),
    )


def per_device(
    features, w_query, w_key, w_value, w_out, w_up, w_down, gain_attn, gain_ffn,
    send_list, edge_owner, edge_slot, edge_count,
):
    core = (lax.axis_index("head") % 2).astype(jnp.int32).reshape(1)
    flat_list = send_list.reshape(-1)
    ids = (edge_owner * CAP + edge_slot).reshape(-1)
    across = functools.partial(lax.all_to_all, split_axis=0, concat_axis=0, tiled=True)
    swap = functools.partial(lax.ppermute, axis_name="head", perm=[(i, i ^ 1) for i in range(8)])
    helds = [across(project_keys_values(features, w_key, w_value, c), "head") for c in range(CHUNKS)]
    collected = [collect(held.reshape(128, HALF, LANES), flat_list, core) for held in helds]
    mines = [
        across(out.reshape(16, 16, HALF, LANES), "node").reshape(256, HALF, LANES)
        for out, _ in collected
    ]
    queries = [across(project_queries(features, w_query, c), "head") for c in range(CHUNKS)]
    backs = []
    for c in range(CHUNKS):
        swapped = swap(collected[c][1])
        other = swap(mines[c])
        done = attend(ids, edge_count, core, queries[c], helds[c], swapped, mines[c], other)
        backs.append(across(done, "head"))
    return finish(features, backs, w_out, w_up, w_down, gain_attn, gain_ffn)


def solution(mesh):
    return jax.shard_map(
        per_device,
        mesh=mesh,
        in_specs=(
            P(("node", "head"), None),
            P(), P(), P(), P(), P(), P(), P(), P(),
            P("node", None, None),
            P("node", None),
            P("node", None),
            P("node"),
        ),
        out_specs=P(("node", "head"), None),
        check_vma=False,
    )
```

```python
import functools
import math

import jax
import jax.numpy as jnp
from jax import lax
from jax.experimental import pallas as pl
from jax.experimental.pallas import tpu as pltpu
from jax.sharding import PartitionSpec as P


HDIM = 64
BLOCK = 64
MAXK = 8
CAP = 16
HALF = BLOCK // 2
LANES = 2 * HDIM
CHUNKS = 3
CHIPS = 4
COLS = CHIPS * HDIM
OWN = 16
SCALE = 1.4426950408889634 / math.sqrt(HDIM)
MASKED = -8e30
F32 = jnp.float32
BF16 = jnp.bfloat16
VMEM = pl.BlockSpec(memory_space=pltpu.VMEM)
SMEM = pl.BlockSpec(memory_space=pltpu.SMEM)
ANY = pl.BlockSpec(memory_space=pl.ANY)
LIMIT = 60 * 1024 * 1024
TILE = (HALF, LANES)


def low_lanes(rows):
    return lax.broadcasted_iota(jnp.int32, (rows, LANES), 1) < HDIM


def pack_pair(both):
    blocks = both.shape[0] // BLOCK
    split = both.reshape(blocks, 2, HALF, LANES)
    first = split[:, 0].reshape(blocks * HALF, LANES)
    second = split[:, 1].reshape(blocks * HALF, LANES)
    low = low_lanes(blocks * HALF)
    even = jnp.where(low, first, pltpu.roll(second, HDIM, 1))
    odd = jnp.where(low, pltpu.roll(first, HDIM, 1), second)
    return [part.reshape(blocks, HALF, LANES).astype(BF16) for part in (even, odd)]


def unpack_pair(even, odd):
    blocks = even.shape[0]
    even = even.reshape(blocks * HALF, LANES).astype(F32)
    odd = odd.reshape(blocks * HALF, LANES).astype(F32)
    low = low_lanes(blocks * HALF)
    first = jnp.where(low, even, pltpu.roll(odd, HDIM, 1)).reshape(blocks, 1, HALF, LANES)
    second = jnp.where(low, pltpu.roll(even, HDIM, 1), odd).reshape(blocks, 1, HALF, LANES)
    return jnp.concatenate([first, second], axis=1).reshape(blocks * BLOCK, LANES).astype(BF16)


def params():
    return pltpu.CompilerParams(vmem_limit_bytes=LIMIT)


def keys_values_kernel(chunk, place_ref, near_ref, far_ref, key_ref, value_ref, *refs):
    outs, (weight, packed, sem) = refs[:CHIPS], refs[CHIPS:]
    z, core = place_ref[0], place_ref[1]

    def fetch(source):
        copy = pltpu.make_async_copy(source.at[:, chunk * COLS : (chunk + 1) * COLS], weight, sem)
        copy.start()
        copy.wait()

    @pl.when(core == 0)
    def _():
        fetch(key_ref)

    @pl.when(core == 1)
    def _():
        fetch(value_ref)

    for owner, feat_ref in ((core, near_ref), (1 - core, far_ref)):
        for half in range(2):
            made = jnp.dot(
                feat_ref[half * 512 : half * 512 + 512, :], weight[...], preferred_element_type=F32
            )
            for pair in range(2):
                both = pack_pair(made[:, pair * LANES : (pair + 1) * LANES])
                for side in range(2):
                    packed[2 * pair + side, pl.ds(owner * OWN + half * 8, 8)] = both[side]
    for step in range(CHIPS):
        outs[step][...] = packed[lax.rem(z + step, CHIPS)]


def project_keys_values(place, near, far, w_key, w_value, chunk):
    rows, width = near.shape
    return pl.pallas_call(
        functools.partial(keys_values_kernel, chunk),
        in_specs=[SMEM, VMEM, VMEM, ANY, ANY],
        out_specs=[VMEM] * CHIPS,
        out_shape=[jax.ShapeDtypeStruct((2 * OWN,) + TILE, BF16)] * CHIPS,
        scratch_shapes=[
            pltpu.VMEM((width, COLS), BF16),
            pltpu.VMEM((CHIPS, 2 * OWN) + TILE, BF16),
            pltpu.SemaphoreType.DMA,
        ],
        compiler_params=params(),
        cost_estimate=pl.CostEstimate(
            flops=4 * rows * width * COLS, bytes_accessed=5 << 20, transcendentals=0
        ),
        name="keys_values",
    )(place, near, far, w_key, w_value)


def queries_kernel(place_ref, feat_ref, query_ref, *refs):
    outs, (packed,) = refs[:CHIPS], refs[CHIPS:]
    z = place_ref[0]
    for chunk in range(CHUNKS):
        for half in range(2):
            made = jnp.dot(
                feat_ref[half * 512 : half * 512 + 512, :],
                query_ref[:, chunk * COLS : (chunk + 1) * COLS],
                preferred_element_type=F32,
            )
            for pair in range(2):
                both = pack_pair(made[:, pair * LANES : (pair + 1) * LANES])
                for side in range(2):
                    packed[2 * pair + side, chunk, half * 8 : half * 8 + 8] = both[side]
    for step in range(CHIPS):
        outs[step][...] = packed[lax.rem(z + step, CHIPS)]


def project_queries(place, features, w_query):
    rows, width = features.shape
    return pl.pallas_call(
        queries_kernel,
        in_specs=[SMEM, VMEM, VMEM],
        out_specs=[VMEM] * CHIPS,
        out_shape=[jax.ShapeDtypeStruct((CHUNKS, OWN) + TILE, BF16)] * CHIPS,
        scratch_shapes=[pltpu.VMEM((CHIPS, CHUNKS, OWN) + TILE, BF16)],
        compiler_params=params(),
        cost_estimate=pl.CostEstimate(
            flops=2 * rows * width * width, bytes_accessed=5 << 20, transcendentals=0
        ),
        name="queries",
    )(place, features, w_query)


def collect_kernel(list_ref, place_ref, *refs):
    parts, (out_ref, own_ref, swap_ref, held) = refs[:CHIPS], refs[CHIPS:]
    z, core = place_ref[0], place_ref[1]
    for step in range(CHIPS):
        source = lax.rem(z + CHIPS - step, CHIPS)
        held[pl.ds(source * 2 * OWN, 2 * OWN)] = parts[step][...]

    def body(step, carry):
        for extra in range(8):
            slot = step * 8 + extra
            out_ref[slot] = held[list_ref[slot]]
        return carry

    lax.fori_loop(0, out_ref.shape[0] // 8, body, 0)
    for source in range(CHIPS):
        own_ref[source] = held[pl.ds(source * 2 * OWN + core * OWN, OWN)]
        swap_ref[source] = held[pl.ds(source * 2 * OWN + (1 - core) * OWN, OWN)]


def collect(flat_list, place, parts):
    slots = flat_list.shape[0]
    own = jax.ShapeDtypeStruct((CHIPS, OWN) + TILE, BF16)
    return pl.pallas_call(
        collect_kernel,
        in_specs=[SMEM, SMEM] + [VMEM] * CHIPS,
        out_specs=[VMEM] * 3,
        out_shape=[jax.ShapeDtypeStruct((slots,) + TILE, BF16), own, own],
        scratch_shapes=[pltpu.VMEM((CHIPS * 2 * OWN,) + TILE, BF16)],
        compiler_params=params(),
        cost_estimate=pl.CostEstimate(flops=0, bytes_accessed=5 << 20, transcendentals=0),
        name="collect",
    )(flat_list, place, *parts)


def attend_kernel(id_ref, count_ref, place_ref, *refs):
    parts, (own_ref, swap_ref, mine_ref, other_ref) = refs[:CHIPS], refs[CHIPS : CHIPS + 4]
    outs = refs[CHIPS + 4 : 2 * CHIPS + 4]
    queries, made, keys, values, own_keys, own_values, sems = refs[2 * CHIPS + 4 :]
    z, core = place_ref[0], place_ref[1]

    def fetch(near, near_own, far, far_own):
        copies = [
            pltpu.make_async_copy(own_ref, near_own, sems.at[0]),
            pltpu.make_async_copy(swap_ref, far_own, sems.at[1]),
            pltpu.make_async_copy(mine_ref, near, sems.at[2]),
            pltpu.make_async_copy(other_ref, far, sems.at[3]),
        ]
        for copy in copies:
            copy.start()
        for copy in copies:
            copy.wait()

    @pl.when(core == 0)
    def _():
        fetch(keys, own_keys, values, own_values)

    @pl.when(core == 1)
    def _():
        fetch(values, own_values, keys, own_keys)

    for step in range(CHIPS):
        queries[lax.rem(z + CHIPS - step, CHIPS)] = parts[step][0]

    low = low_lanes(HALF)
    lane = lax.broadcasted_iota(jnp.int32, (1, LANES), 1)
    dims = (((1,), (1,)), ((), ()))
    rows = 2 * BLOCK
    group = 8

    def attend_group(at, carry):
        source, first = at // 2, (at % 2) * group
        blocks = [source * 2 * OWN + core * OWN + first + k for k in range(group)]
        slots = [[id_ref[block * MAXK + entry] for entry in range(MAXK)] for block in blocks]
        left = []
        for k in range(group):
            query = queries[source, first + k].astype(F32)
            turned = pltpu.roll(query, HDIM, 1)
            zero = jnp.zeros_like(query)
            left.append(
                jnp.concatenate(
                    [
                        jnp.where(low, query, zero),
                        jnp.where(low, turned, zero),
                        jnp.where(low, zero, turned),
                        jnp.where(low, zero, query),
                    ],
                    axis=0,
                ).astype(BF16)
            )
        near = []
        for quad in range(group // 4):
            four = own_keys[source, pl.ds(first + 4 * quad, 4)].reshape(LANES, LANES)
            scores = lax.dot_general(
                jnp.concatenate(left[4 * quad : 4 * quad + 4], axis=0),
                four,
                dims,
                preferred_element_type=F32,
            )
            for j in range(4):
                near.append(
                    jnp.where(lane // HALF == j, scores[j * rows : (j + 1) * rows], MASKED)
                )
        far = []
        for k in range(group):
            far_keys = jnp.concatenate([keys[slot] for slot in slots[k]], axis=0)
            scores = lax.dot_general(left[k], far_keys, dims, preferred_element_type=F32)
            limit = count_ref[blocks[k]] * HALF
            far.append(
                [
                    jnp.where(lane < limit, scores[:, :LANES], MASKED),
                    jnp.where(lane + LANES < limit, scores[:, LANES:], MASKED),
                ]
            )
        tops = []
        for k in range(group):
            top = jnp.maximum(jnp.maximum(far[k][0], far[k][1]), near[k])
            top = jnp.max(jnp.maximum(top[:BLOCK], top[BLOCK:]), axis=1, keepdims=True)
            tops.append(jnp.concatenate([top, top], axis=0))
        far = [[jnp.exp2((part - tops[k]) * SCALE) for part in far[k]] for k in range(group)]
        near = [jnp.exp2((near[k] - tops[k]) * SCALE) for k in range(group)]
        summed = []
        for quad in range(group // 4):
            four = own_values[source, pl.ds(first + 4 * quad, 4)].reshape(LANES, LANES)
            weights = [near[4 * quad + j].astype(BF16) for j in range(4)]
            product = jnp.dot(
                jnp.concatenate(weights, axis=0), four, preferred_element_type=F32
            )
            summed += [product[j * rows : (j + 1) * rows] for j in range(4)]
        for k in range(group):
            far_values = jnp.concatenate([values[slot] for slot in slots[k]], axis=0)
            weights = jnp.concatenate([part.astype(BF16) for part in far[k]], axis=1)
            summed[k] = summed[k] + jnp.dot(weights, far_values, preferred_element_type=F32)
        for k in range(group):
            total = far[k][0] + far[k][1] + near[k]
            total = jnp.sum(total[:BLOCK] + total[BLOCK:], axis=1, keepdims=True)
            share = 1.0 / total
            share = jnp.where(low, share[:HALF], share[HALF:])
            straight = jnp.where(low, summed[k][:HALF], summed[k][3 * HALF :])
            crossed = jnp.where(low, summed[k][HALF : 2 * HALF], summed[k][2 * HALF : 3 * HALF])
            result = (straight + pltpu.roll(crossed, HDIM, 1)) * share
            made[source, first + k] = result.astype(BF16)
        return carry

    lax.fori_loop(0, CHIPS * OWN // group, attend_group, 0)
    for step in range(CHIPS):
        outs[step][...] = made[lax.rem(z + step, CHIPS)]


def attend(ids, counts, place, queries, own, swapped, mine, other, chunk):
    slots = mine.shape[0]
    blocks = pltpu.VMEM((CHIPS, OWN) + TILE, BF16)
    return pl.pallas_call(
        attend_kernel,
        grid=(1,),
        in_specs=[SMEM, SMEM, SMEM]
        + [pl.BlockSpec((1, OWN) + TILE, lambda i: (chunk, 0, 0, 0))] * CHIPS
        + [ANY] * 4,
        out_specs=[VMEM] * CHIPS,
        out_shape=[jax.ShapeDtypeStruct((OWN,) + TILE, BF16)] * CHIPS,
        scratch_shapes=[
            blocks,
            blocks,
            pltpu.VMEM((slots,) + TILE, BF16),
            pltpu.VMEM((slots,) + TILE, BF16),
            blocks,
            blocks,
            pltpu.SemaphoreType.DMA((4,)),
        ],
        compiler_params=params(),
        cost_estimate=pl.CostEstimate(
            flops=64 * 4 * 128 * 128 * 384, bytes_accessed=8 << 20, transcendentals=64 * 128 * 384
        ),
        name="attend",
    )(ids, counts, place, *queries, own, swapped, mine, other)


def normed(values, gain):
    center = values - jnp.mean(values, axis=-1, keepdims=True)
    spread = jnp.mean(center * center, axis=-1, keepdims=True)
    return center * lax.rsqrt(spread + 1e-05) * gain


def finish_kernel(place_ref, feat_ref, *refs):
    backs = refs[: CHUNKS * CHIPS]
    out_w_ref, up_ref, down_ref, gain_a_ref, gain_f_ref, result_ref = refs[CHUNKS * CHIPS :][:6]
    attended, out_w, up, down, sems = refs[CHUNKS * CHIPS + 6 :]
    copies = [
        pltpu.make_async_copy(out_w_ref, out_w, sems.at[0]),
        pltpu.make_async_copy(up_ref, up, sems.at[1]),
        pltpu.make_async_copy(down_ref, down, sems.at[2]),
    ]
    for copy in copies:
        copy.start()
    z = place_ref[0]
    for chunk in range(CHUNKS):
        for step in range(CHIPS):
            source = lax.rem(z + CHIPS - step, CHIPS)
            attended[chunk, source] = backs[chunk * CHIPS + step][...]
    rows = feat_ref.shape[0] // 2
    firsts = []
    copies[0].wait()
    for half in range(2):
        at = slice(half * rows, (half + 1) * rows)
        mixed = feat_ref[at, :].astype(F32)
        for chunk in range(CHUNKS):
            pieces = [
                unpack_pair(
                    attended[chunk, 2 * pair, half * 8 : half * 8 + 8],
                    attended[chunk, 2 * pair + 1, half * 8 : half * 8 + 8],
                )
                for pair in range(2)
            ]
            mixed = mixed + jnp.dot(
                jnp.concatenate(pieces, axis=1),
                out_w[chunk * COLS : (chunk + 1) * COLS, :],
                preferred_element_type=F32,
            )
        firsts.append(normed(mixed, gain_a_ref[...]).astype(BF16))
    copies[1].wait()
    copies[2].wait()
    for half in range(2):
        at = slice(half * rows, (half + 1) * rows)
        first = firsts[half]
        hidden = jnp.maximum(jnp.dot(first, up[...], preferred_element_type=F32), 0.0).astype(BF16)
        total = first.astype(F32) + jnp.dot(hidden, down[...], preferred_element_type=F32)
        result_ref[at, :] = normed(total, gain_f_ref[...]).astype(BF16)


def finish(place, features, backs, w_out, w_up, w_down, gain_attn, gain_ffn):
    rows, width = features.shape
    return pl.pallas_call(
        finish_kernel,
        in_specs=[SMEM, VMEM] + [VMEM] * (CHUNKS * CHIPS) + [ANY] * 3 + [VMEM] * 2,
        out_specs=VMEM,
        out_shape=jax.ShapeDtypeStruct((rows, width), BF16),
        scratch_shapes=[
            pltpu.VMEM((CHUNKS, CHIPS, OWN) + TILE, BF16),
            pltpu.VMEM(w_out.shape, BF16),
            pltpu.VMEM(w_up.shape, BF16),
            pltpu.VMEM(w_down.shape, BF16),
            pltpu.SemaphoreType.DMA((3,)),
        ],
        compiler_params=params(),
        name="finish",
    )(
        place,
        features,
        *[part for back in backs for part in back],
        w_out,
        w_up,
        w_down,
        gain_attn.reshape(1, width),
        gain_ffn.reshape(1, width),
    )


def swap(array):
    return lax.ppermute(array, "head", [(i, i ^ 1) for i in range(2 * CHIPS)])


def along_z(parts):
    moved = [parts[0]]
    for step in range(1, CHIPS):
        moved.append(
            lax.ppermute(
                parts[step], "head", [(i, (i + 2 * step) % (2 * CHIPS)) for i in range(2 * CHIPS)]
            )
        )
    return moved


def per_device(
    features, w_query, w_key, w_value, w_out, w_up, w_down, gain_attn, gain_ffn,
    send_list, edge_owner, edge_slot, edge_count,
):
    head = lax.axis_index("head").astype(jnp.int32)
    place = jnp.stack([head // 2, head % 2])
    groups = send_list.shape[1]
    flat_list = send_list.reshape(-1)
    ids = (edge_owner * CAP + edge_slot).reshape(-1)
    far = swap(features)
    collected = []
    for c in range(CHUNKS):
        parts = project_keys_values(place, features, far, w_key, w_value, c)
        parts = along_z(parts)
        collected.append(collect(flat_list, place, parts))
    queries = along_z(project_queries(place, features, w_query))
    mines = []
    for c in range(CHUNKS):
        sent = collected[c][0].reshape((groups, CAP) + TILE)
        got = lax.all_to_all(sent, "node", split_axis=0, concat_axis=0, tiled=True)
        mines.append(got.reshape((groups * CAP,) + TILE))
    backs = []
    for c in range(CHUNKS):
        swapped = swap(collected[c][2])
        other = swap(mines[c])
        done = attend(ids, edge_count, place, queries, collected[c][1], swapped, mines[c], other, c)
        backs.append(along_z(done))
    return finish(place, features, backs, w_out, w_up, w_down, gain_attn, gain_ffn)


def solution(mesh):
    return jax.shard_map(
        per_device,
        mesh=mesh,
        in_specs=(
            P(("node", "head"), None),
            P(), P(), P(), P(), P(), P(), P(), P(),
            P("node", None, None),
            P("node", None),
            P("node", None),
            P("node"),
        ),
        out_specs=P(("node", "head"), None),
        check_vma=False,
    )
```

```python
import functools
import math

import jax
import jax.numpy as jnp
from jax import lax
from jax.experimental import pallas as pl
from jax.experimental.pallas import tpu as pltpu
from jax.sharding import PartitionSpec as P


HDIM = 64
BLOCK = 64
MAXK = 8
CAP = 16
HALF = BLOCK // 2
LANES = 2 * HDIM
CHUNKS = 3
CHIPS = 4
COLS = CHIPS * HDIM
OWN = 16
SCALE = 1.4426950408889634 / math.sqrt(HDIM)
MASKED = -8e30
F32 = jnp.float32
BF16 = jnp.bfloat16
VMEM = pl.BlockSpec(memory_space=pltpu.VMEM)
SMEM = pl.BlockSpec(memory_space=pltpu.SMEM)
ANY = pl.BlockSpec(memory_space=pl.ANY)
TILE = (HALF, LANES)


def low_lanes(rows):
    return lax.broadcasted_iota(jnp.int32, (rows, LANES), 1) < HDIM


def pack_pair(both):
    blocks = both.shape[0] // BLOCK
    split = both.reshape(blocks, 2, HALF, LANES)
    first = split[:, 0].reshape(blocks * HALF, LANES)
    second = split[:, 1].reshape(blocks * HALF, LANES)
    low = low_lanes(blocks * HALF)
    even = jnp.where(low, first, pltpu.roll(second, HDIM, 1))
    odd = jnp.where(low, pltpu.roll(first, HDIM, 1), second)
    return [part.reshape(blocks, HALF, LANES).astype(BF16) for part in (even, odd)]


def unpack_pair(even, odd):
    blocks = even.shape[0]
    even = even.reshape(blocks * HALF, LANES).astype(F32)
    odd = odd.reshape(blocks * HALF, LANES).astype(F32)
    low = low_lanes(blocks * HALF)
    first = jnp.where(low, even, pltpu.roll(odd, HDIM, 1)).reshape(blocks, 1, HALF, LANES)
    second = jnp.where(low, pltpu.roll(even, HDIM, 1), odd).reshape(blocks, 1, HALF, LANES)
    return jnp.concatenate([first, second], axis=1).reshape(blocks * BLOCK, LANES).astype(BF16)


def params(mebibytes):
    return pltpu.CompilerParams(vmem_limit_bytes=mebibytes << 20)


def keys_values_kernel(chunk, place_ref, near_ref, far_ref, key_ref, value_ref, *refs):
    outs, (weight, packed, sem) = refs[:CHIPS], refs[CHIPS:]
    z, core = place_ref[0], place_ref[1]

    def fetch(source):
        copy = pltpu.make_async_copy(source.at[:, chunk * COLS : (chunk + 1) * COLS], weight, sem)
        copy.start()
        copy.wait()

    @pl.when(core == 0)
    def _():
        fetch(key_ref)

    @pl.when(core == 1)
    def _():
        fetch(value_ref)

    for owner, feat_ref in ((core, near_ref), (1 - core, far_ref)):
        for half in range(2):
            made = jnp.dot(
                feat_ref[half * 512 : half * 512 + 512, :], weight[...], preferred_element_type=F32
            )
            for pair in range(2):
                both = pack_pair(made[:, pair * LANES : (pair + 1) * LANES])
                for side in range(2):
                    packed[2 * pair + side, pl.ds(owner * OWN + half * 8, 8)] = both[side]
    for step in range(CHIPS):
        outs[step][...] = packed[lax.rem(z + step, CHIPS)]


def project_keys_values(place, near, far, w_key, w_value, chunk):
    rows, width = near.shape
    return pl.pallas_call(
        functools.partial(keys_values_kernel, chunk),
        in_specs=[SMEM, VMEM, VMEM, ANY, ANY],
        out_specs=[VMEM] * CHIPS,
        out_shape=[jax.ShapeDtypeStruct((2 * OWN,) + TILE, BF16)] * CHIPS,
        scratch_shapes=[
            pltpu.VMEM((width, COLS), BF16),
            pltpu.VMEM((CHIPS, 2 * OWN) + TILE, BF16),
            pltpu.SemaphoreType.DMA,
        ],
        compiler_params=params(24),
        cost_estimate=pl.CostEstimate(
            flops=4 * rows * width * COLS, bytes_accessed=5 << 20, transcendentals=0
        ),
        name="keys_values",
    )(place, near, far, w_key, w_value)


def queries_kernel(place_ref, feat_ref, query_ref, *refs):
    outs, (packed,) = refs[:CHIPS], refs[CHIPS:]
    z = place_ref[0]
    for chunk in range(CHUNKS):
        for half in range(2):
            made = jnp.dot(
                feat_ref[half * 512 : half * 512 + 512, :],
                query_ref[:, chunk * COLS : (chunk + 1) * COLS],
                preferred_element_type=F32,
            )
            for pair in range(2):
                both = pack_pair(made[:, pair * LANES : (pair + 1) * LANES])
                for side in range(2):
                    packed[2 * pair + side, chunk, half * 8 : half * 8 + 8] = both[side]
    for step in range(CHIPS):
        outs[step][...] = packed[lax.rem(z + step, CHIPS)]


def project_queries(place, features, w_query):
    rows, width = features.shape
    return pl.pallas_call(
        queries_kernel,
        in_specs=[SMEM, VMEM, VMEM],
        out_specs=[VMEM] * CHIPS,
        out_shape=[jax.ShapeDtypeStruct((CHUNKS, OWN) + TILE, BF16)] * CHIPS,
        scratch_shapes=[pltpu.VMEM((CHIPS, CHUNKS, OWN) + TILE, BF16)],
        compiler_params=params(24),
        cost_estimate=pl.CostEstimate(
            flops=2 * rows * width * width, bytes_accessed=5 << 20, transcendentals=0
        ),
        name="queries",
    )(place, features, w_query)


def collect_kernel(list_ref, place_ref, *refs):
    parts, (out_ref, own_ref, swap_ref, held) = refs[:CHIPS], refs[CHIPS:]
    z, core = place_ref[0], place_ref[1]
    for step in range(CHIPS):
        source = lax.rem(z + CHIPS - step, CHIPS)
        held[pl.ds(source * 2 * OWN, 2 * OWN)] = parts[step][...]

    def body(step, carry):
        for extra in range(CAP):
            out_ref[step * CAP + extra] = held[list_ref[0, step, extra]]
        return carry

    lax.fori_loop(0, out_ref.shape[0] // CAP, body, 0)
    for source in range(CHIPS):
        own_ref[source] = held[pl.ds(source * 2 * OWN + core * OWN, OWN)]
        swap_ref[source] = held[pl.ds(source * 2 * OWN + (1 - core) * OWN, OWN)]


def collect(send_list, place, parts):
    slots = send_list.shape[1] * send_list.shape[2]
    own = jax.ShapeDtypeStruct((CHIPS, OWN) + TILE, BF16)
    return pl.pallas_call(
        collect_kernel,
        in_specs=[SMEM, SMEM] + [VMEM] * CHIPS,
        out_specs=[VMEM] * 3,
        out_shape=[jax.ShapeDtypeStruct((slots,) + TILE, BF16), own, own],
        scratch_shapes=[pltpu.VMEM((CHIPS * 2 * OWN,) + TILE, BF16)],
        compiler_params=params(24),
        cost_estimate=pl.CostEstimate(flops=0, bytes_accessed=5 << 20, transcendentals=0),
        name="collect",
    )(send_list, place, *parts)


def attend_kernel(chunk, owner_ref, slot_ref, count_ref, place_ref, *refs):
    parts, (own_ref, swap_ref, mine_ref, other_ref) = refs[:CHIPS], refs[CHIPS : CHIPS + 4]
    outs = refs[CHIPS + 4 : 2 * CHIPS + 4]
    queries, made, keys, values, own_keys, own_values = refs[2 * CHIPS + 4 :]
    z, core = place_ref[0], place_ref[1]

    def place_in(near, near_own, far, far_own):
        def body(step, carry):
            at = pl.ds(step * 8, 8)
            near[at] = mine_ref[at]
            far[at] = other_ref[at]
            return carry

        lax.fori_loop(0, mine_ref.shape[0] // 8, body, 0)
        near_own[...] = own_ref[...]
        far_own[...] = swap_ref[...]

    @pl.when(core == 0)
    def _():
        place_in(keys, own_keys, values, own_values)

    @pl.when(core == 1)
    def _():
        place_in(values, own_values, keys, own_keys)

    for step in range(CHIPS):
        queries[lax.rem(z + CHIPS - step, CHIPS)] = parts[step][chunk]

    low = low_lanes(HALF)
    lane = lax.broadcasted_iota(jnp.int32, (1, LANES), 1)
    dims = (((1,), (1,)), ((), ()))
    rows = 2 * BLOCK
    group = 8

    def attend_group(at, carry):
        source, first = at // 2, (at % 2) * group
        blocks = [source * 2 * OWN + core * OWN + first + k for k in range(group)]
        slots = [
            [owner_ref[entry, block] * CAP + slot_ref[entry, block] for entry in range(MAXK)]
            for block in blocks
        ]
        left = []
        for k in range(group):
            query = queries[source, first + k].astype(F32)
            turned = pltpu.roll(query, HDIM, 1)
            zero = jnp.zeros_like(query)
            left.append(
                jnp.concatenate(
                    [
                        jnp.where(low, query, zero),
                        jnp.where(low, turned, zero),
                        jnp.where(low, zero, turned),
                        jnp.where(low, zero, query),
                    ],
                    axis=0,
                ).astype(BF16)
            )
        near = []
        for quad in range(group // 4):
            four = own_keys[source, pl.ds(first + 4 * quad, 4)].reshape(LANES, LANES)
            scores = lax.dot_general(
                jnp.concatenate(left[4 * quad : 4 * quad + 4], axis=0),
                four,
                dims,
                preferred_element_type=F32,
            )
            for j in range(4):
                near.append(
                    jnp.where(lane // HALF == j, scores[j * rows : (j + 1) * rows], MASKED)
                )
        far = []
        for k in range(group):
            far_keys = jnp.concatenate([keys[slot] for slot in slots[k]], axis=0)
            scores = lax.dot_general(left[k], far_keys, dims, preferred_element_type=F32)
            limit = count_ref[blocks[k]] * HALF
            far.append(
                [
                    jnp.where(lane < limit, scores[:, :LANES], MASKED),
                    jnp.where(lane + LANES < limit, scores[:, LANES:], MASKED),
                ]
            )
        tops = []
        for k in range(group):
            top = jnp.maximum(jnp.maximum(far[k][0], far[k][1]), near[k])
            top = jnp.max(jnp.maximum(top[:BLOCK], top[BLOCK:]), axis=1, keepdims=True)
            tops.append(jnp.concatenate([top, top], axis=0))
        far = [[jnp.exp2((part - tops[k]) * SCALE) for part in far[k]] for k in range(group)]
        near = [jnp.exp2((near[k] - tops[k]) * SCALE) for k in range(group)]
        summed = []
        for quad in range(group // 4):
            four = own_values[source, pl.ds(first + 4 * quad, 4)].reshape(LANES, LANES)
            weights = [near[4 * quad + j].astype(BF16) for j in range(4)]
            product = jnp.dot(
                jnp.concatenate(weights, axis=0), four, preferred_element_type=F32
            )
            summed += [product[j * rows : (j + 1) * rows] for j in range(4)]
        for k in range(group):
            far_values = jnp.concatenate([values[slot] for slot in slots[k]], axis=0)
            weights = jnp.concatenate([part.astype(BF16) for part in far[k]], axis=1)
            summed[k] = summed[k] + jnp.dot(weights, far_values, preferred_element_type=F32)
        for k in range(group):
            total = far[k][0] + far[k][1] + near[k]
            total = jnp.sum(total[:BLOCK] + total[BLOCK:], axis=1, keepdims=True)
            share = 1.0 / total
            share = jnp.where(low, share[:HALF], share[HALF:])
            straight = jnp.where(low, summed[k][:HALF], summed[k][3 * HALF :])
            crossed = jnp.where(low, summed[k][HALF : 2 * HALF], summed[k][2 * HALF : 3 * HALF])
            result = (straight + pltpu.roll(crossed, HDIM, 1)) * share
            made[source, first + k] = result.astype(BF16)
        return carry

    lax.fori_loop(0, CHIPS * OWN // group, attend_group, 0)
    for step in range(CHIPS):
        outs[step][...] = made[lax.rem(z + step, CHIPS)]


def attend(tables, place, queries, own, swapped, mine, other, chunk):
    slots = mine.shape[0]
    blocks = pltpu.VMEM((CHIPS, OWN) + TILE, BF16)
    return pl.pallas_call(
        functools.partial(attend_kernel, chunk),
        in_specs=[SMEM] * 4 + [VMEM] * (CHIPS + 4),
        out_specs=[VMEM] * CHIPS,
        out_shape=[jax.ShapeDtypeStruct((OWN,) + TILE, BF16)] * CHIPS,
        scratch_shapes=[
            blocks,
            blocks,
            pltpu.VMEM((slots,) + TILE, BF16),
            pltpu.VMEM((slots,) + TILE, BF16),
            blocks,
            blocks,
        ],
        compiler_params=params(28),
        cost_estimate=pl.CostEstimate(
            flops=64 * 4 * 128 * 128 * 384, bytes_accessed=8 << 20, transcendentals=64 * 128 * 384
        ),
        name="attend",
    )(*tables, place, *queries, own, swapped, mine, other)


def normed(values, gain):
    center = values - jnp.mean(values, axis=-1, keepdims=True)
    spread = jnp.mean(center * center, axis=-1, keepdims=True)
    return center * lax.rsqrt(spread + 1e-05) * gain


def mixed_rows(held, half, weight):
    at = slice(half * 8, half * 8 + 8)
    pieces = [unpack_pair(held[2 * pair, at], held[2 * pair + 1, at]) for pair in range(2)]
    return jnp.dot(jnp.concatenate(pieces, axis=1), weight, preferred_element_type=F32)


def gather_parts(place_ref, parts, held):
    z = place_ref[0]
    for step in range(CHIPS):
        held[lax.rem(z + CHIPS - step, CHIPS)] = parts[step][...]


def mix_kernel(place_ref, feat_ref, *refs):
    parts, (weight_ref, out_ref, held) = refs[: 2 * CHIPS], refs[2 * CHIPS :]
    rows = feat_ref.shape[0] // 2
    for chunk in range(2):
        gather_parts(place_ref, parts[chunk * CHIPS : (chunk + 1) * CHIPS], held.at[chunk])
    for half in range(2):
        at = slice(half * rows, (half + 1) * rows)
        mixed = feat_ref[at, :].astype(F32)
        for chunk in range(2):
            weight = weight_ref[chunk * COLS : (chunk + 1) * COLS, :]
            mixed = mixed + mixed_rows(held.at[chunk], half, weight)
        out_ref[at, :] = mixed


def mix(place, features, backs, w_out):
    rows, width = features.shape
    return pl.pallas_call(
        mix_kernel,
        in_specs=[SMEM, VMEM] + [VMEM] * (2 * CHIPS + 1),
        out_specs=VMEM,
        out_shape=jax.ShapeDtypeStruct((rows, width), F32),
        scratch_shapes=[pltpu.VMEM((2, CHIPS, OWN) + TILE, BF16)],
        compiler_params=params(24),
        cost_estimate=pl.CostEstimate(
            flops=4 * rows * COLS * width, bytes_accessed=7 << 20, transcendentals=0
        ),
        name="mix",
    )(place, features, *[part for back in backs for part in back], w_out)


def finish_kernel(place_ref, mixed_ref, *refs):
    parts, refs = refs[:CHIPS], refs[CHIPS:]
    out_w_ref, up_ref, down_ref, gain_a_ref, gain_f_ref, result_ref, held, up, down, sems = refs
    copies = [
        pltpu.make_async_copy(up_ref, up, sems.at[0]),
        pltpu.make_async_copy(down_ref, down, sems.at[1]),
    ]
    for copy in copies:
        copy.start()
    gather_parts(place_ref, parts, held)
    rows = mixed_ref.shape[0] // 2
    last = (CHUNKS - 1) * COLS
    firsts = []
    for half in range(2):
        at = slice(half * rows, (half + 1) * rows)
        mixed = mixed_ref[at, :] + mixed_rows(held, half, out_w_ref[last : last + COLS, :])
        firsts.append(normed(mixed, gain_a_ref[...]).astype(BF16))
    for copy in copies:
        copy.wait()
    for half in range(2):
        at = slice(half * rows, (half + 1) * rows)
        first = firsts[half]
        hidden = jnp.maximum(jnp.dot(first, up[...], preferred_element_type=F32), 0.0).astype(BF16)
        total = first.astype(F32) + jnp.dot(hidden, down[...], preferred_element_type=F32)
        result_ref[at, :] = normed(total, gain_f_ref[...]).astype(BF16)


def finish(place, mixed, back, w_out, w_up, w_down, gain_attn, gain_ffn):
    rows, width = mixed.shape
    return pl.pallas_call(
        finish_kernel,
        in_specs=[SMEM, VMEM] + [VMEM] * CHIPS + [VMEM, ANY, ANY, VMEM, VMEM],
        out_specs=VMEM,
        out_shape=jax.ShapeDtypeStruct((rows, width), BF16),
        scratch_shapes=[
            pltpu.VMEM((CHIPS, OWN) + TILE, BF16),
            pltpu.VMEM(w_up.shape, BF16),
            pltpu.VMEM(w_down.shape, BF16),
            pltpu.SemaphoreType.DMA((2,)),
        ],
        compiler_params=params(40),
        name="finish",
    )(
        place,
        mixed,
        *back,
        w_out,
        w_up,
        w_down,
        gain_attn.reshape(1, width),
        gain_ffn.reshape(1, width),
    )


def swap(array):
    return lax.ppermute(array, "head", [(i, i ^ 1) for i in range(2 * CHIPS)])


def along_z(parts):
    moved = [parts[0]]
    for step in range(1, CHIPS):
        moved.append(
            lax.ppermute(
                parts[step], "head", [(i, (i + 2 * step) % (2 * CHIPS)) for i in range(2 * CHIPS)]
            )
        )
    return moved


def per_device(
    features, w_query, w_key, w_value, w_out, w_up, w_down, gain_attn, gain_ffn,
    send_list, edge_owner, edge_slot, edge_count,
):
    head = lax.axis_index("head").astype(jnp.int32)
    place = jnp.stack([head // 2, head % 2])
    groups = send_list.shape[1]
    owners, slots = edge_owner.T, edge_slot.T
    far = swap(features)
    collected = []
    for c in range(CHUNKS):
        parts = project_keys_values(place, features, far, w_key, w_value, c)
        parts = along_z(parts)
        collected.append(collect(send_list, place, parts))
    queries = along_z(project_queries(place, features, w_query))
    mines = []
    for c in range(CHUNKS):
        sent = collected[c][0].reshape((groups, CAP) + TILE)
        got = lax.all_to_all(sent, "node", split_axis=0, concat_axis=0, tiled=True)
        mines.append(got.reshape((groups * CAP,) + TILE))
    backs = []
    for c in range(CHUNKS):
        swapped = swap(collected[c][2])
        other = swap(mines[c])
        tables = (owners, slots, edge_count)
        done = attend(
            tables, place, queries, collected[c][1], swapped, mines[c], other, c
        )
        backs.append(along_z(done))
    mixed = mix(place, features, backs[:2], w_out)
    return finish(place, mixed, backs[2], w_out, w_up, w_down, gain_attn, gain_ffn)


def solution(mesh):
    return jax.shard_map(
        per_device,
        mesh=mesh,
        in_specs=(
            P(("node", "head"), None),
            P(), P(), P(), P(), P(), P(), P(), P(),
            P("node", None, None),
            P("node", None),
            P("node", None),
            P("node"),
        ),
        out_specs=P(("node", "head"), None),
        check_vma=False,
    )
```

```python
import functools
import math

import jax
import jax.numpy as jnp
from jax import lax
from jax.experimental import pallas as pl
from jax.experimental.pallas import tpu as pltpu
from jax.sharding import PartitionSpec as P


HDIM = 64
BLOCK = 64
MAXK = 8
CAP = 16
HALF = BLOCK // 2
LANES = 2 * HDIM
CHUNKS = 3
CHIPS = 4
COLS = CHIPS * HDIM
OWN = 16
SCALE = 1.4426950408889634 / math.sqrt(HDIM)
MASKED = -8e30
F32 = jnp.float32
BF16 = jnp.bfloat16
VMEM = pl.BlockSpec(memory_space=pltpu.VMEM)
SMEM = pl.BlockSpec(memory_space=pltpu.SMEM)
HBM = pl.BlockSpec(memory_space=pltpu.HBM)
TILE = (HALF, LANES)


def low_lanes(rows):
    return lax.broadcasted_iota(jnp.int32, (rows, LANES), 1) < HDIM


def pack_pair(both):
    blocks = both.shape[0] // BLOCK
    split = both.reshape(blocks, 2, HALF, LANES)
    first = split[:, 0].reshape(blocks * HALF, LANES)
    second = split[:, 1].reshape(blocks * HALF, LANES)
    low = low_lanes(blocks * HALF)
    even = jnp.where(low, first, pltpu.roll(second, HDIM, 1))
    odd = jnp.where(low, pltpu.roll(first, HDIM, 1), second)
    return [part.reshape(blocks, HALF, LANES).astype(BF16) for part in (even, odd)]


def unpack_pair(even, odd):
    blocks = even.shape[0]
    even = even.reshape(blocks * HALF, LANES).astype(F32)
    odd = odd.reshape(blocks * HALF, LANES).astype(F32)
    low = low_lanes(blocks * HALF)
    first = jnp.where(low, even, pltpu.roll(odd, HDIM, 1)).reshape(blocks, 1, HALF, LANES)
    second = jnp.where(low, pltpu.roll(even, HDIM, 1), odd).reshape(blocks, 1, HALF, LANES)
    return jnp.concatenate([first, second], axis=1).reshape(blocks * BLOCK, LANES).astype(BF16)


def params(room):
    return pltpu.CompilerParams(vmem_limit_bytes=67_043_328 - room)


def fetch_weight(chunk, core, key_ref, value_ref, weight, sem):
    def fetch(source):
        copy = pltpu.make_async_copy(source.at[:, chunk * COLS : (chunk + 1) * COLS], weight, sem)
        copy.start()
        copy.wait()

    @pl.when(core == 0)
    def _():
        fetch(key_ref)

    @pl.when(core == 1)
    def _():
        fetch(value_ref)


def pack_rows(feat_ref, weight, packed, first):
    for half in range(2):
        made = jnp.dot(
            feat_ref[half * 512 : half * 512 + 512, :], weight[...], preferred_element_type=F32
        )
        for pair in range(2):
            both = pack_pair(made[:, pair * LANES : (pair + 1) * LANES])
            for side in range(2):
                packed[2 * pair + side, pl.ds(first + half * 8, 8)] = both[side]


def near_kernel(place_ref, near_ref, key_ref, value_ref, weight, packed, sem):
    fetch_weight(0, place_ref[1], key_ref, value_ref, weight, sem)
    pack_rows(near_ref, weight, packed, 0)


def project_near(place, near, w_key, w_value):
    rows, width = near.shape
    return pl.pallas_call(
        near_kernel,
        in_specs=[SMEM, VMEM, HBM, HBM],
        out_specs=[VMEM] * 2,
        out_shape=[
            jax.ShapeDtypeStruct((width, COLS), BF16),
            jax.ShapeDtypeStruct((CHIPS, OWN) + TILE, BF16),
        ],
        scratch_shapes=[pltpu.SemaphoreType.DMA],
        compiler_params=params(0),
        cost_estimate=pl.CostEstimate(
            flops=2 * rows * width * COLS, bytes_accessed=3 << 20, transcendentals=0
        ),
        name="near_keys_values",
    )(place, near, w_key, w_value)


def far_kernel(place_ref, far_ref, weight, near_packed, *refs):
    outs, (packed,) = refs[:CHIPS], refs[CHIPS:]
    z, core = place_ref[0], place_ref[1]
    pack_rows(far_ref, weight, packed, 0)
    for step in range(CHIPS):
        dest = lax.rem(z + step, CHIPS)
        outs[step][pl.ds(core * OWN, OWN)] = near_packed[dest]
        outs[step][pl.ds((1 - core) * OWN, OWN)] = packed[dest]


def project_far(place, far, weight, near_packed):
    rows, width = far.shape
    return pl.pallas_call(
        far_kernel,
        in_specs=[SMEM] + [VMEM] * 3,
        out_specs=[VMEM] * CHIPS,
        out_shape=[jax.ShapeDtypeStruct((2 * OWN,) + TILE, BF16)] * CHIPS,
        scratch_shapes=[pltpu.VMEM((CHIPS, OWN) + TILE, BF16)],
        compiler_params=params(0),
        cost_estimate=pl.CostEstimate(
            flops=2 * rows * width * COLS, bytes_accessed=3 << 20, transcendentals=0
        ),
        name="far_keys_values",
    )(place, far, weight, near_packed)


def keys_values_kernel(chunk, place_ref, near_ref, far_ref, key_ref, value_ref, *refs):
    outs, (weight, packed, sem) = refs[:CHIPS], refs[CHIPS:]
    z, core = place_ref[0], place_ref[1]
    fetch_weight(chunk, core, key_ref, value_ref, weight, sem)
    pack_rows(near_ref, weight, packed, core * OWN)
    pack_rows(far_ref, weight, packed, (1 - core) * OWN)
    for step in range(CHIPS):
        outs[step][...] = packed[lax.rem(z + step, CHIPS)]


def project_keys_values(place, near, far, w_key, w_value, chunk):
    rows, width = near.shape
    return pl.pallas_call(
        functools.partial(keys_values_kernel, chunk),
        in_specs=[SMEM, VMEM, VMEM, HBM, HBM],
        out_specs=[VMEM] * CHIPS,
        out_shape=[jax.ShapeDtypeStruct((2 * OWN,) + TILE, BF16)] * CHIPS,
        scratch_shapes=[
            pltpu.VMEM((width, COLS), BF16),
            pltpu.VMEM((CHIPS, 2 * OWN) + TILE, BF16),
            pltpu.SemaphoreType.DMA,
        ],
        compiler_params=params(0),
        cost_estimate=pl.CostEstimate(
            flops=4 * rows * width * COLS, bytes_accessed=5 << 20, transcendentals=0
        ),
        name="keys_values",
    )(place, near, far, w_key, w_value)


def queries_kernel(place_ref, feat_ref, query_ref, *refs):
    outs, (packed,) = refs[:CHIPS], refs[CHIPS:]
    z = place_ref[0]
    for chunk in range(CHUNKS):
        for half in range(2):
            made = jnp.dot(
                feat_ref[half * 512 : half * 512 + 512, :],
                query_ref[:, chunk * COLS : (chunk + 1) * COLS],
                preferred_element_type=F32,
            )
            for pair in range(2):
                both = pack_pair(made[:, pair * LANES : (pair + 1) * LANES])
                for side in range(2):
                    packed[2 * pair + side, chunk, half * 8 : half * 8 + 8] = both[side]
    for step in range(CHIPS):
        outs[step][...] = packed[lax.rem(z + step, CHIPS)]


def project_queries(place, features, w_query):
    rows, width = features.shape
    return pl.pallas_call(
        queries_kernel,
        in_specs=[SMEM, VMEM, VMEM],
        out_specs=[VMEM] * CHIPS,
        out_shape=[jax.ShapeDtypeStruct((CHUNKS, OWN) + TILE, BF16)] * CHIPS,
        scratch_shapes=[pltpu.VMEM((CHIPS, CHUNKS, OWN) + TILE, BF16)],
        compiler_params=params(0),
        cost_estimate=pl.CostEstimate(
            flops=2 * rows * width * width, bytes_accessed=5 << 20, transcendentals=0
        ),
        name="queries",
    )(place, features, w_query)


def collect_kernel(list_ref, place_ref, *refs):
    parts, (out_ref, own_ref, swap_ref, held, picked, sems) = refs[:CHIPS], refs[CHIPS:]
    z, core = place_ref[0], place_ref[1]
    for step in range(CHIPS):
        source = lax.rem(z + CHIPS - step, CHIPS)
        held[pl.ds(source * 2 * OWN, 2 * OWN)] = parts[step][...]
    quarter = picked.shape[0] // CAP // 4

    def body(step, carry):
        for extra in range(CAP):
            picked[step * CAP + extra] = held[list_ref[0, step, extra]]
        return carry

    copies = []
    for part in range(4):
        lax.fori_loop(part * quarter, (part + 1) * quarter, body, 0)
        at = pl.ds(part * quarter * CAP, quarter * CAP)
        copies.append(pltpu.make_async_copy(picked.at[at], out_ref.at[at], sems.at[part]))
        copies[-1].start()
    for source in range(CHIPS):
        for which, target in enumerate((own_ref, swap_ref)):
            side = core if which == 0 else 1 - core
            at = pl.ds(source * 2 * OWN + side * OWN, OWN)
            copies.append(
                pltpu.make_async_copy(
                    held.at[at], target.at[source], sems.at[4 + 2 * source + which]
                )
            )
            copies[-1].start()
    for copy in copies:
        copy.wait()


def collect(send_list, place, parts):
    slots = send_list.shape[1] * send_list.shape[2]
    own = jax.ShapeDtypeStruct((CHIPS, OWN) + TILE, BF16)
    return pl.pallas_call(
        collect_kernel,
        in_specs=[SMEM, SMEM] + [VMEM] * CHIPS,
        out_specs=[HBM] * 3,
        out_shape=[jax.ShapeDtypeStruct((slots,) + TILE, BF16), own, own],
        scratch_shapes=[
            pltpu.VMEM((CHIPS * 2 * OWN,) + TILE, BF16),
            pltpu.VMEM((slots,) + TILE, BF16),
            pltpu.SemaphoreType.DMA((4 + 2 * CHIPS,)),
        ],
        compiler_params=params(0),
        cost_estimate=pl.CostEstimate(flops=0, bytes_accessed=5 << 20, transcendentals=0),
        name="collect",
    )(send_list, place, *parts)


def attend_kernel(chunk, owner_ref, slot_ref, count_ref, place_ref, *refs):
    parts, (own_ref, swap_ref, mine_ref, other_ref) = refs[:CHIPS], refs[CHIPS : CHIPS + 4]
    outs = refs[CHIPS + 4 : 2 * CHIPS + 4]
    queries, made, keys, values, own_keys, own_values, sems = refs[2 * CHIPS + 4 :]
    z, core = place_ref[0], place_ref[1]

    def place_in(near, near_own, far, far_own):
        copies = [
            pltpu.make_async_copy(mine_ref, near, sems.at[0]),
            pltpu.make_async_copy(other_ref, far, sems.at[1]),
            pltpu.make_async_copy(own_ref, near_own, sems.at[2]),
            pltpu.make_async_copy(swap_ref, far_own, sems.at[3]),
        ]
        for copy in copies:
            copy.start()
        for copy in copies:
            copy.wait()

    @pl.when(core == 0)
    def _():
        place_in(keys, own_keys, values, own_values)

    @pl.when(core == 1)
    def _():
        place_in(values, own_values, keys, own_keys)

    for step in range(CHIPS):
        queries[lax.rem(z + CHIPS - step, CHIPS)] = parts[step][chunk]

    low = low_lanes(HALF)
    lane = lax.broadcasted_iota(jnp.int32, (1, LANES), 1)
    dims = (((1,), (1,)), ((), ()))
    rows = 2 * BLOCK
    group = 8

    def attend_group(at, carry):
        source, first = at // 2, (at % 2) * group
        blocks = [source * 2 * OWN + core * OWN + first + k for k in range(group)]
        slots = [
            [owner_ref[entry, block] * CAP + slot_ref[entry, block] for entry in range(MAXK)]
            for block in blocks
        ]
        left = []
        for k in range(group):
            query = queries[source, first + k].astype(F32)
            turned = pltpu.roll(query, HDIM, 1)
            zero = jnp.zeros_like(query)
            left.append(
                jnp.concatenate(
                    [
                        jnp.where(low, query, zero),
                        jnp.where(low, turned, zero),
                        jnp.where(low, zero, turned),
                        jnp.where(low, zero, query),
                    ],
                    axis=0,
                ).astype(BF16)
            )
        near = []
        for quad in range(group // 4):
            four = own_keys[source, pl.ds(first + 4 * quad, 4)].reshape(LANES, LANES)
            scores = lax.dot_general(
                jnp.concatenate(left[4 * quad : 4 * quad + 4], axis=0),
                four,
                dims,
                preferred_element_type=F32,
            )
            for j in range(4):
                near.append(
                    jnp.where(lane // HALF == j, scores[j * rows : (j + 1) * rows], MASKED)
                )
        far = []
        for k in range(group):
            far_keys = jnp.concatenate([keys[slot] for slot in slots[k]], axis=0)
            scores = lax.dot_general(left[k], far_keys, dims, preferred_element_type=F32)
            limit = count_ref[blocks[k]] * HALF
            far.append(
                [
                    jnp.where(lane < limit, scores[:, :LANES], MASKED),
                    jnp.where(lane + LANES < limit, scores[:, LANES:], MASKED),
                ]
            )
        tops = []
        for k in range(group):
            top = jnp.maximum(jnp.maximum(far[k][0], far[k][1]), near[k])
            top = jnp.max(jnp.maximum(top[:BLOCK], top[BLOCK:]), axis=1, keepdims=True)
            tops.append(jnp.concatenate([top, top], axis=0))
        far = [[jnp.exp2((part - tops[k]) * SCALE) for part in far[k]] for k in range(group)]
        near = [jnp.exp2((near[k] - tops[k]) * SCALE) for k in range(group)]
        summed = []
        for quad in range(group // 4):
            four = own_values[source, pl.ds(first + 4 * quad, 4)].reshape(LANES, LANES)
            weights = [near[4 * quad + j].astype(BF16) for j in range(4)]
            product = jnp.dot(
                jnp.concatenate(weights, axis=0), four, preferred_element_type=F32
            )
            summed += [product[j * rows : (j + 1) * rows] for j in range(4)]
        for k in range(group):
            far_values = jnp.concatenate([values[slot] for slot in slots[k]], axis=0)
            weights = jnp.concatenate([part.astype(BF16) for part in far[k]], axis=1)
            summed[k] = summed[k] + jnp.dot(weights, far_values, preferred_element_type=F32)
        for k in range(group):
            total = far[k][0] + far[k][1] + near[k]
            total = jnp.sum(total[:BLOCK] + total[BLOCK:], axis=1, keepdims=True)
            share = 1.0 / total
            share = jnp.where(low, share[:HALF], share[HALF:])
            straight = jnp.where(low, summed[k][:HALF], summed[k][3 * HALF :])
            crossed = jnp.where(low, summed[k][HALF : 2 * HALF], summed[k][2 * HALF : 3 * HALF])
            result = (straight + pltpu.roll(crossed, HDIM, 1)) * share
            made[source, first + k] = result.astype(BF16)
        return carry

    lax.fori_loop(0, CHIPS * OWN // group, attend_group, 0)
    for step in range(CHIPS):
        outs[step][...] = made[lax.rem(z + step, CHIPS)]


def attend(tables, place, queries, own, swapped, mine, other, chunk):
    slots = mine.shape[0]
    blocks = pltpu.VMEM((CHIPS, OWN) + TILE, BF16)
    return pl.pallas_call(
        functools.partial(attend_kernel, chunk),
        in_specs=[SMEM] * 4 + [VMEM] * CHIPS + [HBM] * 4,
        out_specs=[VMEM] * CHIPS,
        out_shape=[jax.ShapeDtypeStruct((OWN,) + TILE, BF16)] * CHIPS,
        scratch_shapes=[
            blocks,
            blocks,
            pltpu.VMEM((slots,) + TILE, BF16),
            pltpu.VMEM((slots,) + TILE, BF16),
            blocks,
            blocks,
            pltpu.SemaphoreType.DMA((4,)),
        ],
        compiler_params=params(0),
        cost_estimate=pl.CostEstimate(
            flops=64 * 4 * 128 * 128 * 384, bytes_accessed=8 << 20, transcendentals=64 * 128 * 384
        ),
        name="attend",
    )(*tables, place, *queries, own, swapped, mine, other)


def normed(values, gain):
    center = values - jnp.mean(values, axis=-1, keepdims=True)
    spread = jnp.mean(center * center, axis=-1, keepdims=True)
    return center * lax.rsqrt(spread + 1e-05) * gain


def mixed_rows(held, half, weight):
    at = slice(half * 8, half * 8 + 8)
    pieces = [unpack_pair(held[2 * pair, at], held[2 * pair + 1, at]) for pair in range(2)]
    return jnp.dot(jnp.concatenate(pieces, axis=1), weight, preferred_element_type=F32)


def gather_parts(place_ref, parts, held):
    z = place_ref[0]
    for step in range(CHIPS):
        held[lax.rem(z + CHIPS - step, CHIPS)] = parts[step][...]


def mix_kernel(place_ref, feat_ref, *refs):
    parts, (weight_ref, out_ref, held, made, sems) = refs[: 2 * CHIPS], refs[2 * CHIPS :]
    copies = []
    rows = feat_ref.shape[0] // 2
    for chunk in range(2):
        gather_parts(place_ref, parts[chunk * CHIPS : (chunk + 1) * CHIPS], held.at[chunk])
    for half in range(2):
        at = slice(half * rows, (half + 1) * rows)
        mixed = feat_ref[at, :].astype(F32)
        for chunk in range(2):
            weight = weight_ref[chunk * COLS : (chunk + 1) * COLS, :]
            mixed = mixed + mixed_rows(held.at[chunk], half, weight)
        made[at, :] = mixed
        copies.append(pltpu.make_async_copy(made.at[at], out_ref.at[at], sems.at[half]))
        copies[-1].start()
    for copy in copies:
        copy.wait()


def mix(place, features, backs, w_out):
    rows, width = features.shape
    return pl.pallas_call(
        mix_kernel,
        in_specs=[SMEM, VMEM] + [VMEM] * (2 * CHIPS + 1),
        out_specs=HBM,
        out_shape=jax.ShapeDtypeStruct((rows, width), F32),
        scratch_shapes=[
            pltpu.VMEM((2, CHIPS, OWN) + TILE, BF16),
            pltpu.VMEM((rows, width), F32),
            pltpu.SemaphoreType.DMA((2,)),
        ],
        compiler_params=params(0),
        cost_estimate=pl.CostEstimate(
            flops=4 * rows * COLS * width, bytes_accessed=7 << 20, transcendentals=0
        ),
        name="mix",
    )(place, features, *[part for back in backs for part in back], w_out)


def finish_kernel(place_ref, mixed_ref, *refs):
    parts, refs = refs[:CHIPS], refs[CHIPS:]
    out_w_ref, up_ref, down_ref, gain_a_ref, gain_f_ref, result_ref, *scratch = refs
    held, early, out_w, up, down, sems = scratch
    rows = mixed_ref.shape[0] // 2
    halves = [slice(half * rows, (half + 1) * rows) for half in range(2)]
    copies = [
        pltpu.make_async_copy(out_w_ref.at[(CHUNKS - 1) * COLS :], out_w, sems.at[0]),
        pltpu.make_async_copy(mixed_ref.at[halves[0]], early.at[halves[0]], sems.at[1]),
        pltpu.make_async_copy(mixed_ref.at[halves[1]], early.at[halves[1]], sems.at[2]),
        pltpu.make_async_copy(up_ref, up, sems.at[3]),
        pltpu.make_async_copy(down_ref, down, sems.at[4]),
    ]
    for copy in copies:
        copy.start()
    gather_parts(place_ref, parts, held)
    copies[0].wait()
    firsts = []
    for half, at in enumerate(halves):
        added = mixed_rows(held, half, out_w[...])
        copies[1 + half].wait()
        firsts.append(normed(early[at, :] + added, gain_a_ref[...]).astype(BF16))
    for half, at in enumerate(halves):
        first = firsts[half]
        if half == 0:
            copies[3].wait()
        hidden = jnp.maximum(jnp.dot(first, up[...], preferred_element_type=F32), 0.0).astype(BF16)
        if half == 0:
            copies[4].wait()
        total = first.astype(F32) + jnp.dot(hidden, down[...], preferred_element_type=F32)
        result_ref[at, :] = normed(total, gain_f_ref[...]).astype(BF16)


def finish(place, mixed, back, w_out, w_up, w_down, gain_attn, gain_ffn):
    rows, width = mixed.shape
    return pl.pallas_call(
        finish_kernel,
        in_specs=[SMEM, HBM] + [VMEM] * CHIPS + [HBM, HBM, HBM, VMEM, VMEM],
        out_specs=VMEM,
        out_shape=jax.ShapeDtypeStruct((rows, width), BF16),
        scratch_shapes=[
            pltpu.VMEM((CHIPS, OWN) + TILE, BF16),
            pltpu.VMEM((rows, width), F32),
            pltpu.VMEM((COLS, width), BF16),
            pltpu.VMEM(w_up.shape, BF16),
            pltpu.VMEM(w_down.shape, BF16),
            pltpu.SemaphoreType.DMA((5,)),
        ],
        compiler_params=params(0),
        name="finish",
    )(
        place,
        mixed,
        *back,
        w_out,
        w_up,
        w_down,
        gain_attn.reshape(1, width),
        gain_ffn.reshape(1, width),
    )


def swap(array):
    return lax.ppermute(array, "head", [(i, i ^ 1) for i in range(2 * CHIPS)])


def along_z(parts):
    moved = list(parts)
    for step in (2, 1, 3):
        moved[step] = lax.ppermute(
            parts[step], "head", [(i, (i + 2 * step) % (2 * CHIPS)) for i in range(2 * CHIPS)]
        )
    return moved


def per_device(
    features, w_query, w_key, w_value, w_out, w_up, w_down, gain_attn, gain_ffn,
    send_list, edge_owner, edge_slot, edge_count,
):
    head = lax.axis_index("head").astype(jnp.int32)
    place = jnp.stack([head // 2, head % 2])
    groups = send_list.shape[1]
    owners, slots = edge_owner.T, edge_slot.T
    far = swap(features)
    weight, near_packed = project_near(place, features, w_key, w_value)
    collected = []
    for c in range(CHUNKS):
        if c == 0:
            parts = project_far(place, far, weight, near_packed)
        else:
            parts = project_keys_values(place, features, far, w_key, w_value, c)
        parts = along_z(parts)
        collected.append(collect(send_list, place, parts))
    queries = along_z(project_queries(place, features, w_query))
    mines = []
    for c in range(CHUNKS):
        sent = collected[c][0].reshape((groups, CAP) + TILE)
        got = lax.all_to_all(sent, "node", split_axis=0, concat_axis=0, tiled=True)
        mines.append(got.reshape((groups * CAP,) + TILE))
    backs = []
    for c in range(CHUNKS):
        swapped = swap(collected[c][2])
        other = swap(mines[c])
        tables = (owners, slots, edge_count)
        done = attend(
            tables, place, queries, collected[c][1], swapped, mines[c], other, c
        )
        backs.append(along_z(done))
    mixed = mix(place, features, backs[:2], w_out)
    return finish(place, mixed, backs[2], w_out, w_up, w_down, gain_attn, gain_ffn)


def solution(mesh):
    return jax.shard_map(
        per_device,
        mesh=mesh,
        in_specs=(
            P(("node", "head"), None),
            P(), P(), P(), P(), P(), P(), P(), P(),
            P("node", None, None),
            P("node", None),
            P("node", None),
            P("node"),
        ),
        out_specs=P(("node", "head"), None),
        check_vma=False,
    )
```

```python
import functools
import math

import jax
import jax.numpy as jnp
from jax import lax
from jax.experimental import pallas as pl
from jax.experimental.pallas import tpu as pltpu
from jax.sharding import PartitionSpec as P


HDIM = 64
BLOCK = 64
MAXK = 8
CAP = 16
HALF = BLOCK // 2
LANES = 2 * HDIM
CHUNKS = 3
CHIPS = 4
COLS = CHIPS * HDIM
OWN = 16
SCALE = 1.4426950408889634 / math.sqrt(HDIM)
MASKED = -8e30
F32 = jnp.float32
BF16 = jnp.bfloat16
VMEM = pl.BlockSpec(memory_space=pltpu.VMEM)
SMEM = pl.BlockSpec(memory_space=pltpu.SMEM)
HBM = pl.BlockSpec(memory_space=pltpu.HBM)
TILE = (HALF, LANES)


def low_lanes(rows):
    return lax.broadcasted_iota(jnp.int32, (rows, LANES), 1) < HDIM


def pack_pair(both):
    blocks = both.shape[0] // BLOCK
    split = both.reshape(blocks, 2, HALF, LANES)
    first = split[:, 0].reshape(blocks * HALF, LANES)
    second = split[:, 1].reshape(blocks * HALF, LANES)
    low = low_lanes(blocks * HALF)
    even = jnp.where(low, first, pltpu.roll(second, HDIM, 1))
    odd = jnp.where(low, pltpu.roll(first, HDIM, 1), second)
    return [part.reshape(blocks, HALF, LANES).astype(BF16) for part in (even, odd)]


def unpack_pair(even, odd):
    blocks = even.shape[0]
    even = even.reshape(blocks * HALF, LANES).astype(F32)
    odd = odd.reshape(blocks * HALF, LANES).astype(F32)
    low = low_lanes(blocks * HALF)
    first = jnp.where(low, even, pltpu.roll(odd, HDIM, 1)).reshape(blocks, 1, HALF, LANES)
    second = jnp.where(low, pltpu.roll(even, HDIM, 1), odd).reshape(blocks, 1, HALF, LANES)
    return jnp.concatenate([first, second], axis=1).reshape(blocks * BLOCK, LANES).astype(BF16)


def params(room):
    return pltpu.CompilerParams(vmem_limit_bytes=67_043_328 - room)


def fetch_weight(chunk, core, key_ref, value_ref, weight, sem):
    def fetch(source):
        copy = pltpu.make_async_copy(source.at[:, chunk * COLS : (chunk + 1) * COLS], weight, sem)
        copy.start()
        copy.wait()

    @pl.when(core == 0)
    def _():
        fetch(key_ref)

    @pl.when(core == 1)
    def _():
        fetch(value_ref)


def pack_rows(feat_ref, weight, packed, first):
    for half in range(2):
        made = jnp.dot(
            feat_ref[half * 512 : half * 512 + 512, :], weight[...], preferred_element_type=F32
        )
        for pair in range(2):
            both = pack_pair(made[:, pair * LANES : (pair + 1) * LANES])
            for side in range(2):
                packed[2 * pair + side, pl.ds(first + half * 8, 8)] = both[side]


def first_kernel(feat_ref, key_ref, value_ref, *refs):
    out_ref, feats, weights, made, sems, done = refs
    halves = [slice(half * 512, half * 512 + 512) for half in range(2)]
    fetches = [
        pltpu.make_async_copy(key_ref.at[:, :COLS], weights.at[0], sems.at[0]),
        pltpu.make_async_copy(feat_ref.at[halves[0]], feats.at[halves[0]], sems.at[1]),
        pltpu.make_async_copy(feat_ref.at[halves[1]], feats.at[halves[1]], sems.at[2]),
        pltpu.make_async_copy(value_ref.at[:, :COLS], weights.at[1], sems.at[3]),
    ]
    for copy in fetches:
        copy.start()
    copies = []
    fetches[0].wait()
    for kind in range(2):
        if kind == 1:
            fetches[3].wait()
        for half, at in enumerate(halves):
            if kind == 0:
                fetches[1 + half].wait()
            rows = jnp.dot(feats[at, :], weights[kind], preferred_element_type=F32)
            for pair in range(2):
                both = pack_pair(rows[:, pair * LANES : (pair + 1) * LANES])
                for side in range(2):
                    dest = 2 * (2 * pair + side) + kind
                    made[dest, half * 8 : half * 8 + 8] = both[side]
        for z in range(CHIPS):
            dest = 2 * z + kind
            copies.append(pltpu.make_async_copy(made.at[dest], out_ref.at[dest], done.at[dest]))
            copies[-1].start()
    for copy in copies:
        copy.wait()


def project_first(features, w_key, w_value):
    rows, width = features.shape
    return pl.pallas_call(
        first_kernel,
        in_specs=[HBM] * 3,
        out_specs=HBM,
        out_shape=jax.ShapeDtypeStruct((2 * CHIPS, OWN) + TILE, BF16),
        scratch_shapes=[
            pltpu.VMEM((rows, width), BF16),
            pltpu.VMEM((2, width, COLS), BF16),
            pltpu.VMEM((2 * CHIPS, OWN) + TILE, BF16),
            pltpu.SemaphoreType.DMA((4,)),
            pltpu.SemaphoreType.DMA((2 * CHIPS,)),
        ],
        compiler_params=params(0),
        cost_estimate=pl.CostEstimate(
            flops=4 * rows * width * COLS, bytes_accessed=4 << 20, transcendentals=0
        ),
        name="first_keys_values",
    )(features, w_key, w_value)


def keys_values_kernel(chunk, place_ref, near_ref, far_ref, key_ref, value_ref, *refs):
    outs, (weight, packed, sem) = refs[:CHIPS], refs[CHIPS:]
    z, core = place_ref[0], place_ref[1]
    fetch_weight(chunk, core, key_ref, value_ref, weight, sem)
    pack_rows(near_ref, weight, packed, core * OWN)
    pack_rows(far_ref, weight, packed, (1 - core) * OWN)
    for step in range(CHIPS):
        outs[step][...] = packed[lax.rem(z + step, CHIPS)]


def project_keys_values(place, near, far, w_key, w_value, chunk):
    rows, width = near.shape
    return pl.pallas_call(
        functools.partial(keys_values_kernel, chunk),
        in_specs=[SMEM, VMEM, VMEM, HBM, HBM],
        out_specs=[VMEM] * CHIPS,
        out_shape=[jax.ShapeDtypeStruct((2 * OWN,) + TILE, BF16)] * CHIPS,
        scratch_shapes=[
            pltpu.VMEM((width, COLS), BF16),
            pltpu.VMEM((CHIPS, 2 * OWN) + TILE, BF16),
            pltpu.SemaphoreType.DMA,
        ],
        compiler_params=params(0),
        cost_estimate=pl.CostEstimate(
            flops=4 * rows * width * COLS, bytes_accessed=5 << 20, transcendentals=0
        ),
        name="keys_values",
    )(place, near, far, w_key, w_value)


def queries_kernel(place_ref, feat_ref, query_ref, *refs):
    outs, (packed,) = refs[:CHIPS], refs[CHIPS:]
    z = place_ref[0]
    for chunk in range(CHUNKS):
        for half in range(2):
            made = jnp.dot(
                feat_ref[half * 512 : half * 512 + 512, :],
                query_ref[:, chunk * COLS : (chunk + 1) * COLS],
                preferred_element_type=F32,
            )
            for pair in range(2):
                both = pack_pair(made[:, pair * LANES : (pair + 1) * LANES])
                for side in range(2):
                    packed[2 * pair + side, chunk, half * 8 : half * 8 + 8] = both[side]
    for step in range(CHIPS):
        outs[step][...] = packed[lax.rem(z + step, CHIPS)]


def project_queries(place, features, w_query):
    rows, width = features.shape
    return pl.pallas_call(
        queries_kernel,
        in_specs=[SMEM, VMEM, VMEM],
        out_specs=[VMEM] * CHIPS,
        out_shape=[jax.ShapeDtypeStruct((CHUNKS, OWN) + TILE, BF16)] * CHIPS,
        scratch_shapes=[pltpu.VMEM((CHIPS, CHUNKS, OWN) + TILE, BF16)],
        compiler_params=params(0),
        cost_estimate=pl.CostEstimate(
            flops=2 * rows * width * width, bytes_accessed=5 << 20, transcendentals=0
        ),
        name="queries",
    )(place, features, w_query)


def collect_kernel(count, list_ref, place_ref, *refs):
    parts, (out_ref, own_ref, swap_ref, *scratch) = refs[:count], refs[count:]
    z, core = place_ref[0], place_ref[1]
    held, picked, arrive, sems = scratch
    if count == 1:
        copies = [pltpu.make_async_copy(parts[0], held, arrive.at[0])]
    else:
        copies = []
        for step in range(CHIPS):
            at = pl.ds(lax.rem(z + CHIPS - step, CHIPS) * 2 * OWN, 2 * OWN)
            copies.append(pltpu.make_async_copy(parts[step], held.at[at], arrive.at[step]))
    for copy in copies:
        copy.start()
    for copy in copies:
        copy.wait()
    copies = []
    for source in range(CHIPS):
        for which, target in enumerate((own_ref, swap_ref)):
            side = core if which == 0 else 1 - core
            at = pl.ds(source * 2 * OWN + side * OWN, OWN)
            copies.append(
                pltpu.make_async_copy(
                    held.at[at], target.at[source], sems.at[4 + 2 * source + which]
                )
            )
            copies[-1].start()
    quarter = picked.shape[0] // CAP // 4

    def body(step, carry):
        for extra in range(CAP):
            picked[step * CAP + extra] = held[list_ref[0, step, extra]]
        return carry

    for part in range(4):
        lax.fori_loop(part * quarter, (part + 1) * quarter, body, 0)
        at = pl.ds(part * quarter * CAP, quarter * CAP)
        copies.append(pltpu.make_async_copy(picked.at[at], out_ref.at[at], sems.at[part]))
        copies[-1].start()
    for copy in copies:
        copy.wait()


def collect(send_list, place, parts):
    slots = send_list.shape[1] * send_list.shape[2]
    own = jax.ShapeDtypeStruct((CHIPS, OWN) + TILE, BF16)
    return pl.pallas_call(
        functools.partial(collect_kernel, len(parts)),
        in_specs=[SMEM, SMEM] + [HBM] * len(parts),
        out_specs=[HBM] * 3,
        out_shape=[jax.ShapeDtypeStruct((slots,) + TILE, BF16), own, own],
        scratch_shapes=[
            pltpu.VMEM((CHIPS * 2 * OWN,) + TILE, BF16),
            pltpu.VMEM((slots,) + TILE, BF16),
            pltpu.SemaphoreType.DMA((CHIPS,)),
            pltpu.SemaphoreType.DMA((4 + 2 * CHIPS,)),
        ],
        compiler_params=params(0),
        cost_estimate=pl.CostEstimate(flops=0, bytes_accessed=5 << 20, transcendentals=0),
        name="collect",
    )(send_list, place, *parts)


def attend_kernel(chunk, owner_ref, slot_ref, count_ref, place_ref, *refs):
    parts, (own_ref, swap_ref, mine_ref, other_ref) = refs[:CHIPS], refs[CHIPS : CHIPS + 4]
    outs = refs[CHIPS + 4 : 2 * CHIPS + 4]
    queries, made, keys, values, own_keys, own_values, asked, sems, done = refs[2 * CHIPS + 4 :]
    z, core = place_ref[0], place_ref[1]

    asking = []
    for step in range(CHIPS):
        source = lax.rem(z + CHIPS - step, CHIPS)
        asking.append(
            pltpu.make_async_copy(parts[step].at[chunk], queries.at[source], asked.at[step])
        )
        asking[-1].start()

    def place_in(near, near_own, far, far_own):
        copies = [
            pltpu.make_async_copy(mine_ref, near, sems.at[0]),
            pltpu.make_async_copy(other_ref, far, sems.at[1]),
            pltpu.make_async_copy(own_ref, near_own, sems.at[2]),
            pltpu.make_async_copy(swap_ref, far_own, sems.at[3]),
        ]
        for copy in copies:
            copy.start()
        for copy in copies:
            copy.wait()

    @pl.when(core == 0)
    def _():
        place_in(keys, own_keys, values, own_values)

    @pl.when(core == 1)
    def _():
        place_in(values, own_values, keys, own_keys)

    for copy in asking:
        copy.wait()

    low = low_lanes(HALF)
    lane = lax.broadcasted_iota(jnp.int32, (1, LANES), 1)
    dims = (((1,), (1,)), ((), ()))
    rows = 2 * BLOCK
    group = 8

    def attend_group(at, carry):
        ahead = lax.rem(at // 2 + 1, CHIPS)
        source, first = lax.rem(z + ahead, CHIPS), (at % 2) * group
        blocks = [source * 2 * OWN + core * OWN + first + k for k in range(group)]
        slots = [
            [owner_ref[entry, block] * CAP + slot_ref[entry, block] for entry in range(MAXK)]
            for block in blocks
        ]
        left = []
        for k in range(group):
            query = queries[source, first + k].astype(F32)
            turned = pltpu.roll(query, HDIM, 1)
            zero = jnp.zeros_like(query)
            left.append(
                jnp.concatenate(
                    [
                        jnp.where(low, query, zero),
                        jnp.where(low, turned, zero),
                        jnp.where(low, zero, turned),
                        jnp.where(low, zero, query),
                    ],
                    axis=0,
                ).astype(BF16)
            )
        near = []
        for quad in range(group // 4):
            four = own_keys[source, pl.ds(first + 4 * quad, 4)].reshape(LANES, LANES)
            scores = lax.dot_general(
                jnp.concatenate(left[4 * quad : 4 * quad + 4], axis=0),
                four,
                dims,
                preferred_element_type=F32,
            )
            for j in range(4):
                near.append(
                    jnp.where(lane // HALF == j, scores[j * rows : (j + 1) * rows], MASKED)
                )
        far = []
        for k in range(group):
            far_keys = jnp.concatenate([keys[slot] for slot in slots[k]], axis=0)
            scores = lax.dot_general(left[k], far_keys, dims, preferred_element_type=F32)
            limit = count_ref[blocks[k]] * HALF
            far.append(
                [
                    jnp.where(lane < limit, scores[:, :LANES], MASKED),
                    jnp.where(lane + LANES < limit, scores[:, LANES:], MASKED),
                ]
            )
        tops = []
        for k in range(group):
            top = jnp.maximum(jnp.maximum(far[k][0], far[k][1]), near[k])
            top = jnp.max(jnp.maximum(top[:BLOCK], top[BLOCK:]), axis=1, keepdims=True)
            tops.append(jnp.concatenate([top, top], axis=0))
        far = [[jnp.exp2((part - tops[k]) * SCALE) for part in far[k]] for k in range(group)]
        near = [jnp.exp2((near[k] - tops[k]) * SCALE) for k in range(group)]
        summed = []
        for quad in range(group // 4):
            four = own_values[source, pl.ds(first + 4 * quad, 4)].reshape(LANES, LANES)
            weights = [near[4 * quad + j].astype(BF16) for j in range(4)]
            product = jnp.dot(
                jnp.concatenate(weights, axis=0), four, preferred_element_type=F32
            )
            summed += [product[j * rows : (j + 1) * rows] for j in range(4)]
        for k in range(group):
            far_values = jnp.concatenate([values[slot] for slot in slots[k]], axis=0)
            weights = jnp.concatenate([part.astype(BF16) for part in far[k]], axis=1)
            summed[k] = summed[k] + jnp.dot(weights, far_values, preferred_element_type=F32)
        for k in range(group):
            total = far[k][0] + far[k][1] + near[k]
            total = jnp.sum(total[:BLOCK] + total[BLOCK:], axis=1, keepdims=True)
            share = 1.0 / total
            share = jnp.where(low, share[:HALF], share[HALF:])
            straight = jnp.where(low, summed[k][:HALF], summed[k][3 * HALF :])
            crossed = jnp.where(low, summed[k][HALF : 2 * HALF], summed[k][2 * HALF : 3 * HALF])
            result = (straight + pltpu.roll(crossed, HDIM, 1)) * share
            made[source, first + k] = result.astype(BF16)
        for step in range(CHIPS):

            @pl.when(jnp.logical_and(at % 2 == 1, ahead == step))
            def _():
                pltpu.make_async_copy(made.at[source], outs[step], done.at[step]).start()

        return carry

    lax.fori_loop(0, CHIPS * OWN // group, attend_group, 0)
    for step in range(CHIPS):
        source = lax.rem(z + step, CHIPS)
        pltpu.make_async_copy(made.at[source], outs[step], done.at[step]).wait()


def attend(tables, place, queries, own, swapped, mine, other, chunk):
    slots = mine.shape[0]
    blocks = pltpu.VMEM((CHIPS, OWN) + TILE, BF16)
    return pl.pallas_call(
        functools.partial(attend_kernel, chunk),
        in_specs=[SMEM] * 4 + [HBM] * (CHIPS + 4),
        out_specs=[HBM] * CHIPS,
        out_shape=[jax.ShapeDtypeStruct((OWN,) + TILE, BF16)] * CHIPS,
        scratch_shapes=[
            blocks,
            blocks,
            pltpu.VMEM((slots,) + TILE, BF16),
            pltpu.VMEM((slots,) + TILE, BF16),
            blocks,
            blocks,
            pltpu.SemaphoreType.DMA((CHIPS,)),
            pltpu.SemaphoreType.DMA((4,)),
            pltpu.SemaphoreType.DMA((CHIPS,)),
        ],
        compiler_params=params(0),
        cost_estimate=pl.CostEstimate(
            flops=64 * 4 * 128 * 128 * 384, bytes_accessed=8 << 20, transcendentals=64 * 128 * 384
        ),
        name="attend",
    )(*tables, place, *queries, own, swapped, mine, other)


def normed(values, gain):
    center = values - jnp.mean(values, axis=-1, keepdims=True)
    spread = jnp.mean(center * center, axis=-1, keepdims=True)
    return center * lax.rsqrt(spread + 1e-05) * gain


def mixed_rows(held, half, weight):
    at = slice(half * 8, half * 8 + 8)
    pieces = [unpack_pair(held[2 * pair, at], held[2 * pair + 1, at]) for pair in range(2)]
    return jnp.dot(jnp.concatenate(pieces, axis=1), weight, preferred_element_type=F32)


def gather_parts(place_ref, parts, held, sems):
    copies = []
    for step in range(CHIPS):
        source = lax.rem(place_ref[0] + CHIPS - step, CHIPS)
        copies.append(pltpu.make_async_copy(parts[step], held.at[source], sems.at[step]))
        copies[-1].start()
    return copies


def mix_kernel(place_ref, feat_ref, *refs):
    parts, (weight_ref, out_ref, held, weight, made, arrive, sems) = refs[:CHIPS], refs[CHIPS:]
    rows = feat_ref.shape[0] // 2
    fetch = pltpu.make_async_copy(weight_ref.at[:COLS], weight, sems.at[0])
    fetch.start()
    for copy in gather_parts(place_ref, parts, held, arrive):
        copy.wait()
    fetch.wait()
    copies = []
    for half in range(2):
        at = slice(half * rows, (half + 1) * rows)
        made[at, :] = feat_ref[at, :].astype(F32) + mixed_rows(held, half, weight[...])
        copies.append(pltpu.make_async_copy(made.at[at], out_ref.at[at], sems.at[1 + half]))
        copies[-1].start()
    for copy in copies:
        copy.wait()


def mix(place, features, back, w_out):
    rows, width = features.shape
    return pl.pallas_call(
        mix_kernel,
        in_specs=[SMEM, VMEM] + [HBM] * (CHIPS + 1),
        out_specs=HBM,
        out_shape=jax.ShapeDtypeStruct((rows, width), F32),
        scratch_shapes=[
            pltpu.VMEM((CHIPS, OWN) + TILE, BF16),
            pltpu.VMEM((COLS, width), BF16),
            pltpu.VMEM((rows, width), F32),
            pltpu.SemaphoreType.DMA((CHIPS,)),
            pltpu.SemaphoreType.DMA((3,)),
        ],
        compiler_params=params(0),
        cost_estimate=pl.CostEstimate(
            flops=2 * rows * COLS * width, bytes_accessed=6 << 20, transcendentals=0
        ),
        name="mix",
    )(place, features, *back, w_out)


def finish_kernel(place_ref, mixed_ref, *refs):
    late = CHUNKS - 1
    parts, refs = refs[: late * CHIPS], refs[late * CHIPS :]
    out_w_ref, up_ref, down_ref, gain_a_ref, gain_f_ref, result_ref, *scratch = refs
    held, early, out_w, up, down, made, arrive, sems = scratch
    rows = mixed_ref.shape[0] // 2
    halves = [slice(half * rows, (half + 1) * rows) for half in range(2)]
    copies = [
        pltpu.make_async_copy(out_w_ref.at[COLS:], out_w, sems.at[0]),
        pltpu.make_async_copy(mixed_ref.at[halves[0]], early.at[halves[0]], sems.at[1]),
        pltpu.make_async_copy(mixed_ref.at[halves[1]], early.at[halves[1]], sems.at[2]),
        pltpu.make_async_copy(up_ref, up, sems.at[3]),
        pltpu.make_async_copy(down_ref, down, sems.at[4]),
    ]
    arriving = []
    for which in range(late):
        some = parts[which * CHIPS : (which + 1) * CHIPS]
        arriving += gather_parts(place_ref, some, held.at[which], arrive.at[which])
    for copy in copies:
        copy.start()
    for copy in arriving:
        copy.wait()
    copies[0].wait()
    firsts = []
    for half, at in enumerate(halves):
        added = mixed_rows(held.at[0], half, out_w[:COLS, :])
        added = added + mixed_rows(held.at[1], half, out_w[COLS:, :])
        copies[1 + half].wait()
        firsts.append(normed(early[at, :] + added, gain_a_ref[...]).astype(BF16))
    for half, at in enumerate(halves):
        first = firsts[half]
        if half == 0:
            copies[3].wait()
        hidden = jnp.maximum(jnp.dot(first, up[...], preferred_element_type=F32), 0.0).astype(BF16)
        if half == 0:
            copies[4].wait()
        total = first.astype(F32) + jnp.dot(hidden, down[...], preferred_element_type=F32)
        made[at, :] = normed(total, gain_f_ref[...]).astype(BF16)
        copies.append(pltpu.make_async_copy(made.at[at], result_ref.at[at], sems.at[5 + half]))
        copies[-1].start()
    for copy in copies[5:]:
        copy.wait()


def finish(place, mixed, backs, w_out, w_up, w_down, gain_attn, gain_ffn):
    rows, width = mixed.shape
    return pl.pallas_call(
        finish_kernel,
        in_specs=[SMEM] + [HBM] * (2 * CHIPS + 4) + [VMEM, VMEM],
        out_specs=HBM,
        out_shape=jax.ShapeDtypeStruct((rows, width), BF16),
        scratch_shapes=[
            pltpu.VMEM((CHUNKS - 1, CHIPS, OWN) + TILE, BF16),
            pltpu.VMEM((rows, width), F32),
            pltpu.VMEM((2 * COLS, width), BF16),
            pltpu.VMEM(w_up.shape, BF16),
            pltpu.VMEM(w_down.shape, BF16),
            pltpu.VMEM((rows, width), BF16),
            pltpu.SemaphoreType.DMA((CHUNKS - 1, CHIPS)),
            pltpu.SemaphoreType.DMA((7,)),
        ],
        compiler_params=params(0),
        name="finish",
    )(
        place,
        mixed,
        *[part for back in backs for part in back],
        w_out,
        w_up,
        w_down,
        gain_attn.reshape(1, width),
        gain_ffn.reshape(1, width),
    )


def swap(array):
    return lax.ppermute(array, "head", [(i, i ^ 1) for i in range(2 * CHIPS)])


def along_z(parts):
    moved = list(parts)
    for step in (2, 1, 3):
        moved[step] = lax.ppermute(
            parts[step], "head", [(i, (i + 2 * step) % (2 * CHIPS)) for i in range(2 * CHIPS)]
        )
    return moved


def per_device(
    features, w_query, w_key, w_value, w_out, w_up, w_down, gain_attn, gain_ffn,
    send_list, edge_owner, edge_slot, edge_count,
):
    head = lax.axis_index("head").astype(jnp.int32)
    place = jnp.stack([head // 2, head % 2])
    groups = send_list.shape[1]
    owners, slots = edge_owner.T, edge_slot.T
    far = swap(features)
    collected = []
    for c in range(CHUNKS):
        if c == 0:
            whole = project_first(features, w_key, w_value)
            whole = lax.all_to_all(whole, "head", split_axis=0, concat_axis=0, tiled=True)
            parts = [whole.reshape((-1,) + TILE)]
        else:
            parts = project_keys_values(place, features, far, w_key, w_value, c)
            parts = along_z(parts)
        collected.append(collect(send_list, place, parts))
    queries = along_z(project_queries(place, features, w_query))
    mines = []
    for c in range(CHUNKS):
        sent = collected[c][0].reshape((groups, CAP) + TILE)
        got = lax.all_to_all(sent, "node", split_axis=0, concat_axis=0, tiled=True)
        mines.append(got.reshape((groups * CAP,) + TILE))
    backs = []
    for c in range(CHUNKS):
        swapped = swap(collected[c][2])
        other = swap(mines[c])
        tables = (owners, slots, edge_count)
        done = attend(
            tables, place, queries, collected[c][1], swapped, mines[c], other, c
        )
        backs.append(along_z(done))
    mixed = mix(place, features, backs[0], w_out)
    return finish(place, mixed, backs[1:], w_out, w_up, w_down, gain_attn, gain_ffn)


def solution(mesh):
    return jax.shard_map(
        per_device,
        mesh=mesh,
        in_specs=(
            P(("node", "head"), None),
            P(), P(), P(), P(), P(), P(), P(), P(),
            P("node", None, None),
            P("node", None),
            P("node", None),
            P("node"),
        ),
        out_specs=P(("node", "head"), None),
        check_vma=False,
    )
```

```python
import functools
import math

import jax
import jax.numpy as jnp
from jax import lax
from jax.experimental import pallas as pl
from jax.experimental.pallas import tpu as pltpu
from jax.sharding import PartitionSpec as P


HDIM = 64
BLOCK = 64
MAXK = 8
CAP = 16
HALF = BLOCK // 2
LANES = 2 * HDIM
CHUNKS = 3
CHIPS = 4
COLS = CHIPS * HDIM
OWN = 16
SCALE = 1.4426950408889634 / math.sqrt(HDIM)
MASKED = -8e30
F32 = jnp.float32
BF16 = jnp.bfloat16
VMEM = pl.BlockSpec(memory_space=pltpu.VMEM)
SMEM = pl.BlockSpec(memory_space=pltpu.SMEM)
HBM = pl.BlockSpec(memory_space=pltpu.HBM)
TILE = (HALF, LANES)


def low_lanes(rows):
    return lax.broadcasted_iota(jnp.int32, (rows, LANES), 1) < HDIM


def pack_pair(both):
    blocks = both.shape[0] // BLOCK
    split = both.reshape(blocks, 2, HALF, LANES)
    first = split[:, 0].reshape(blocks * HALF, LANES)
    second = split[:, 1].reshape(blocks * HALF, LANES)
    low = low_lanes(blocks * HALF)
    even = jnp.where(low, first, pltpu.roll(second, HDIM, 1))
    odd = jnp.where(low, pltpu.roll(first, HDIM, 1), second)
    return [part.reshape(blocks, HALF, LANES).astype(BF16) for part in (even, odd)]


def unpack_pair(even, odd):
    blocks = even.shape[0]
    even = even.reshape(blocks * HALF, LANES).astype(F32)
    odd = odd.reshape(blocks * HALF, LANES).astype(F32)
    low = low_lanes(blocks * HALF)
    first = jnp.where(low, even, pltpu.roll(odd, HDIM, 1)).reshape(blocks, 1, HALF, LANES)
    second = jnp.where(low, pltpu.roll(even, HDIM, 1), odd).reshape(blocks, 1, HALF, LANES)
    return jnp.concatenate([first, second], axis=1).reshape(blocks * BLOCK, LANES).astype(BF16)


def params(room):
    return pltpu.CompilerParams(vmem_limit_bytes=67_043_328 - room)


def fetch_weight(chunk, core, key_ref, value_ref, weight, sem):
    def fetch(source):
        copy = pltpu.make_async_copy(source.at[:, chunk * COLS : (chunk + 1) * COLS], weight, sem)
        copy.start()
        copy.wait()

    @pl.when(core == 0)
    def _():
        fetch(key_ref)

    @pl.when(core == 1)
    def _():
        fetch(value_ref)


def pack_rows(feat_ref, weight, packed, first):
    for half in range(2):
        made = jnp.dot(
            feat_ref[half * 512 : half * 512 + 512, :], weight[...], preferred_element_type=F32
        )
        for pair in range(2):
            both = pack_pair(made[:, pair * LANES : (pair + 1) * LANES])
            for side in range(2):
                packed[2 * pair + side, pl.ds(first + half * 8, 8)] = both[side]


def first_kernel(feat_ref, key_ref, value_ref, *refs):
    out_ref, feats, weights, made, sems, done = refs
    halves = [slice(half * 512, half * 512 + 512) for half in range(2)]
    fetches = [
        pltpu.make_async_copy(key_ref.at[:, :COLS], weights.at[0], sems.at[0]),
        pltpu.make_async_copy(feat_ref.at[halves[0]], feats.at[halves[0]], sems.at[1]),
        pltpu.make_async_copy(feat_ref.at[halves[1]], feats.at[halves[1]], sems.at[2]),
        pltpu.make_async_copy(value_ref.at[:, :COLS], weights.at[1], sems.at[3]),
    ]
    for copy in fetches:
        copy.start()
    copies = []
    fetches[0].wait()
    for kind in range(2):
        if kind == 1:
            fetches[3].wait()
        for half, at in enumerate(halves):
            if kind == 0:
                fetches[1 + half].wait()
            rows = jnp.dot(feats[at, :], weights[kind], preferred_element_type=F32)
            for pair in range(2):
                both = pack_pair(rows[:, pair * LANES : (pair + 1) * LANES])
                for side in range(2):
                    dest = 2 * (2 * pair + side) + kind
                    made[dest, half * 8 : half * 8 + 8] = both[side]
        for z in range(CHIPS):
            dest = 2 * z + kind
            copies.append(pltpu.make_async_copy(made.at[dest], out_ref.at[dest], done.at[dest]))
            copies[-1].start()
    for copy in copies:
        copy.wait()


def project_first(features, w_key, w_value):
    rows, width = features.shape
    return pl.pallas_call(
        first_kernel,
        in_specs=[HBM] * 3,
        out_specs=HBM,
        out_shape=jax.ShapeDtypeStruct((2 * CHIPS, OWN) + TILE, BF16),
        scratch_shapes=[
            pltpu.VMEM((rows, width), BF16),
            pltpu.VMEM((2, width, COLS), BF16),
            pltpu.VMEM((2 * CHIPS, OWN) + TILE, BF16),
            pltpu.SemaphoreType.DMA((4,)),
            pltpu.SemaphoreType.DMA((2 * CHIPS,)),
        ],
        compiler_params=params(0),
        cost_estimate=pl.CostEstimate(
            flops=4 * rows * width * COLS, bytes_accessed=4 << 20, transcendentals=0
        ),
        name="first_keys_values",
    )(features, w_key, w_value)


def keys_values_kernel(chunk, place_ref, near_ref, far_ref, key_ref, value_ref, *refs):
    outs, (weight, packed, sem) = refs[:CHIPS], refs[CHIPS:]
    z, core = place_ref[0], place_ref[1]
    fetch_weight(chunk, core, key_ref, value_ref, weight, sem)
    pack_rows(near_ref, weight, packed, core * OWN)
    pack_rows(far_ref, weight, packed, (1 - core) * OWN)
    for step in range(CHIPS):
        outs[step][...] = packed[lax.rem(z + step, CHIPS)]


def project_keys_values(place, near, far, w_key, w_value, chunk):
    rows, width = near.shape
    return pl.pallas_call(
        functools.partial(keys_values_kernel, chunk),
        in_specs=[SMEM, VMEM, VMEM, HBM, HBM],
        out_specs=[VMEM] * CHIPS,
        out_shape=[jax.ShapeDtypeStruct((2 * OWN,) + TILE, BF16)] * CHIPS,
        scratch_shapes=[
            pltpu.VMEM((width, COLS), BF16),
            pltpu.VMEM((CHIPS, 2 * OWN) + TILE, BF16),
            pltpu.SemaphoreType.DMA,
        ],
        compiler_params=params(0),
        cost_estimate=pl.CostEstimate(
            flops=4 * rows * width * COLS, bytes_accessed=5 << 20, transcendentals=0
        ),
        name="keys_values",
    )(place, near, far, w_key, w_value)


def queries_kernel(place_ref, feat_ref, query_ref, *refs):
    outs, (packed,) = refs[:CHIPS], refs[CHIPS:]
    z = place_ref[0]
    for chunk in range(CHUNKS):
        for half in range(2):
            made = jnp.dot(
                feat_ref[half * 512 : half * 512 + 512, :],
                query_ref[:, chunk * COLS : (chunk + 1) * COLS],
                preferred_element_type=F32,
            )
            for pair in range(2):
                both = pack_pair(made[:, pair * LANES : (pair + 1) * LANES])
                for side in range(2):
                    packed[2 * pair + side, chunk, half * 8 : half * 8 + 8] = both[side]
    for step in range(CHIPS):
        outs[step][...] = packed[lax.rem(z + step, CHIPS)]


def project_queries(place, features, w_query):
    rows, width = features.shape
    return pl.pallas_call(
        queries_kernel,
        in_specs=[SMEM, VMEM, VMEM],
        out_specs=[VMEM] * CHIPS,
        out_shape=[jax.ShapeDtypeStruct((CHUNKS, OWN) + TILE, BF16)] * CHIPS,
        scratch_shapes=[pltpu.VMEM((CHIPS, CHUNKS, OWN) + TILE, BF16)],
        compiler_params=params(0),
        cost_estimate=pl.CostEstimate(
            flops=2 * rows * width * width, bytes_accessed=5 << 20, transcendentals=0
        ),
        name="queries",
    )(place, features, w_query)


def collect_kernel(count, list_ref, place_ref, *refs):
    parts, (out_ref, own_ref, swap_ref, *scratch) = refs[:count], refs[count:]
    z, core = place_ref[0], place_ref[1]
    if count == 1:
        held, (picked, sems) = parts[0], scratch
    else:
        held, picked, sems = scratch
        for step in range(CHIPS):
            source = lax.rem(z + CHIPS - step, CHIPS)
            held[pl.ds(source * 2 * OWN, 2 * OWN)] = parts[step][...]
    quarter = picked.shape[0] // CAP // 4

    def body(step, carry):
        for extra in range(CAP):
            picked[step * CAP + extra] = held[list_ref[0, step, extra]]
        return carry

    copies = []
    for part in range(4):
        lax.fori_loop(part * quarter, (part + 1) * quarter, body, 0)
        at = pl.ds(part * quarter * CAP, quarter * CAP)
        copies.append(pltpu.make_async_copy(picked.at[at], out_ref.at[at], sems.at[part]))
        copies[-1].start()
    for source in range(CHIPS):
        for which, target in enumerate((own_ref, swap_ref)):
            side = core if which == 0 else 1 - core
            at = pl.ds(source * 2 * OWN + side * OWN, OWN)
            copies.append(
                pltpu.make_async_copy(
                    held.at[at], target.at[source], sems.at[4 + 2 * source + which]
                )
            )
            copies[-1].start()
    for copy in copies:
        copy.wait()


def collect(send_list, place, parts):
    slots = send_list.shape[1] * send_list.shape[2]
    own = jax.ShapeDtypeStruct((CHIPS, OWN) + TILE, BF16)
    return pl.pallas_call(
        functools.partial(collect_kernel, len(parts)),
        in_specs=[SMEM, SMEM] + [VMEM] * len(parts),
        out_specs=[HBM] * 3,
        out_shape=[jax.ShapeDtypeStruct((slots,) + TILE, BF16), own, own],
        scratch_shapes=[pltpu.VMEM((CHIPS * 2 * OWN,) + TILE, BF16)] * (len(parts) > 1)
        + [pltpu.VMEM((slots,) + TILE, BF16), pltpu.SemaphoreType.DMA((4 + 2 * CHIPS,))],
        compiler_params=params(0),
        cost_estimate=pl.CostEstimate(flops=0, bytes_accessed=5 << 20, transcendentals=0),
        name="collect",
    )(send_list, place, *parts)


def attend_kernel(chunk, owner_ref, slot_ref, count_ref, place_ref, *refs):
    parts, (own_ref, swap_ref, mine_ref, other_ref) = refs[:CHIPS], refs[CHIPS : CHIPS + 4]
    outs = refs[CHIPS + 4 : 2 * CHIPS + 4]
    queries, made, keys, values, own_keys, own_values, asked, sems, done = refs[2 * CHIPS + 4 :]
    z, core = place_ref[0], place_ref[1]

    asking = []
    for step in range(CHIPS):
        source = lax.rem(z + CHIPS - step, CHIPS)
        asking.append(
            pltpu.make_async_copy(parts[step].at[chunk], queries.at[source], asked.at[step])
        )
        asking[-1].start()

    def place_in(near, near_own, far, far_own):
        copies = [
            pltpu.make_async_copy(mine_ref, near, sems.at[0]),
            pltpu.make_async_copy(other_ref, far, sems.at[1]),
            pltpu.make_async_copy(own_ref, near_own, sems.at[2]),
            pltpu.make_async_copy(swap_ref, far_own, sems.at[3]),
        ]
        for copy in copies:
            copy.start()
        for copy in copies:
            copy.wait()

    @pl.when(core == 0)
    def _():
        place_in(keys, own_keys, values, own_values)

    @pl.when(core == 1)
    def _():
        place_in(values, own_values, keys, own_keys)

    for copy in asking:
        copy.wait()

    low = low_lanes(HALF)
    lane = lax.broadcasted_iota(jnp.int32, (1, LANES), 1)
    dims = (((1,), (1,)), ((), ()))
    rows = 2 * BLOCK
    group = 8

    def attend_group(at, carry):
        ahead = lax.rem(at // 2 + 1, CHIPS)
        source, first = lax.rem(z + ahead, CHIPS), (at % 2) * group
        blocks = [source * 2 * OWN + core * OWN + first + k for k in range(group)]
        slots = [
            [owner_ref[entry, block] * CAP + slot_ref[entry, block] for entry in range(MAXK)]
            for block in blocks
        ]
        left = []
        for k in range(group):
            query = queries[source, first + k].astype(F32)
            turned = pltpu.roll(query, HDIM, 1)
            zero = jnp.zeros_like(query)
            left.append(
                jnp.concatenate(
                    [
                        jnp.where(low, query, zero),
                        jnp.where(low, turned, zero),
                        jnp.where(low, zero, turned),
                        jnp.where(low, zero, query),
                    ],
                    axis=0,
                ).astype(BF16)
            )
        near = []
        for quad in range(group // 4):
            four = own_keys[source, pl.ds(first + 4 * quad, 4)].reshape(LANES, LANES)
            scores = lax.dot_general(
                jnp.concatenate(left[4 * quad : 4 * quad + 4], axis=0),
                four,
                dims,
                preferred_element_type=F32,
            )
            for j in range(4):
                near.append(
                    jnp.where(lane // HALF == j, scores[j * rows : (j + 1) * rows], MASKED)
                )
        far = []
        for k in range(group):
            far_keys = jnp.concatenate([keys[slot] for slot in slots[k]], axis=0)
            scores = lax.dot_general(left[k], far_keys, dims, preferred_element_type=F32)
            limit = count_ref[blocks[k]] * HALF
            far.append(
                [
                    jnp.where(lane < limit, scores[:, :LANES], MASKED),
                    jnp.where(lane + LANES < limit, scores[:, LANES:], MASKED),
                ]
            )
        tops = []
        for k in range(group):
            top = jnp.maximum(jnp.maximum(far[k][0], far[k][1]), near[k])
            top = jnp.max(jnp.maximum(top[:BLOCK], top[BLOCK:]), axis=1, keepdims=True)
            tops.append(jnp.concatenate([top, top], axis=0))
        far = [[jnp.exp2((part - tops[k]) * SCALE) for part in far[k]] for k in range(group)]
        near = [jnp.exp2((near[k] - tops[k]) * SCALE) for k in range(group)]
        summed = []
        for quad in range(group // 4):
            four = own_values[source, pl.ds(first + 4 * quad, 4)].reshape(LANES, LANES)
            weights = [near[4 * quad + j].astype(BF16) for j in range(4)]
            product = jnp.dot(
                jnp.concatenate(weights, axis=0), four, preferred_element_type=F32
            )
            summed += [product[j * rows : (j + 1) * rows] for j in range(4)]
        for k in range(group):
            far_values = jnp.concatenate([values[slot] for slot in slots[k]], axis=0)
            weights = jnp.concatenate([part.astype(BF16) for part in far[k]], axis=1)
            summed[k] = summed[k] + jnp.dot(weights, far_values, preferred_element_type=F32)
        for k in range(group):
            total = far[k][0] + far[k][1] + near[k]
            total = jnp.sum(total[:BLOCK] + total[BLOCK:], axis=1, keepdims=True)
            share = 1.0 / total
            share = jnp.where(low, share[:HALF], share[HALF:])
            straight = jnp.where(low, summed[k][:HALF], summed[k][3 * HALF :])
            crossed = jnp.where(low, summed[k][HALF : 2 * HALF], summed[k][2 * HALF : 3 * HALF])
            result = (straight + pltpu.roll(crossed, HDIM, 1)) * share
            made[source, first + k] = result.astype(BF16)
        for step in range(CHIPS):

            @pl.when(jnp.logical_and(at % 2 == 1, ahead == step))
            def _():
                pltpu.make_async_copy(made.at[source], outs[step], done.at[step]).start()

        return carry

    lax.fori_loop(0, CHIPS * OWN // group, attend_group, 0)
    for step in range(CHIPS):
        source = lax.rem(z + step, CHIPS)
        pltpu.make_async_copy(made.at[source], outs[step], done.at[step]).wait()


def attend(tables, place, queries, own, swapped, mine, other, chunk):
    slots = mine.shape[0]
    blocks = pltpu.VMEM((CHIPS, OWN) + TILE, BF16)
    return pl.pallas_call(
        functools.partial(attend_kernel, chunk),
        in_specs=[SMEM] * 4 + [HBM] * (CHIPS + 4),
        out_specs=[HBM] * CHIPS,
        out_shape=[jax.ShapeDtypeStruct((OWN,) + TILE, BF16)] * CHIPS,
        scratch_shapes=[
            blocks,
            blocks,
            pltpu.VMEM((slots,) + TILE, BF16),
            pltpu.VMEM((slots,) + TILE, BF16),
            blocks,
            blocks,
            pltpu.SemaphoreType.DMA((CHIPS,)),
            pltpu.SemaphoreType.DMA((4,)),
            pltpu.SemaphoreType.DMA((CHIPS,)),
        ],
        compiler_params=params(0),
        cost_estimate=pl.CostEstimate(
            flops=64 * 4 * 128 * 128 * 384, bytes_accessed=8 << 20, transcendentals=64 * 128 * 384
        ),
        name="attend",
    )(*tables, place, *queries, own, swapped, mine, other)


def normed(values, gain):
    center = values - jnp.mean(values, axis=-1, keepdims=True)
    spread = jnp.mean(center * center, axis=-1, keepdims=True)
    return center * lax.rsqrt(spread + 1e-05) * gain


def mixed_rows(held, half, weight):
    at = slice(half * 8, half * 8 + 8)
    pieces = [unpack_pair(held[2 * pair, at], held[2 * pair + 1, at]) for pair in range(2)]
    return jnp.dot(jnp.concatenate(pieces, axis=1), weight, preferred_element_type=F32)


def gather_parts(place_ref, parts, held, sems):
    copies = []
    for step in range(CHIPS):
        source = lax.rem(place_ref[0] + CHIPS - step, CHIPS)
        copies.append(pltpu.make_async_copy(parts[step], held.at[source], sems.at[step]))
        copies[-1].start()
    return copies


def gains_kernel(attn_ref, ffn_ref, out_ref):
    out_ref[0, :] = attn_ref[...]
    out_ref[1, :] = ffn_ref[...]


def stack_gains(gain_attn, gain_ffn):
    return pl.pallas_call(
        gains_kernel,
        in_specs=[VMEM, VMEM],
        out_specs=VMEM,
        out_shape=jax.ShapeDtypeStruct((2,) + gain_attn.shape, F32),
        compiler_params=params(0),
        name="gains",
    )(gain_attn, gain_ffn)


def finish_kernel(place_ref, feat_ref, *refs):
    parts, refs = refs[: CHUNKS * CHIPS], refs[CHUNKS * CHIPS :]
    out_w_ref, up_ref, down_ref, gain_ref, result_ref, *scratch = refs
    held, feats, out_w, up, down, made, arrive, sems = scratch
    rows = feat_ref.shape[0] // 2
    halves = [slice(half * rows, (half + 1) * rows) for half in range(2)]
    arriving = []
    for which in range(CHUNKS):
        some = parts[which * CHIPS : (which + 1) * CHIPS]
        arriving += gather_parts(place_ref, some, held.at[which], arrive.at[which])
    copies = [
        pltpu.make_async_copy(out_w_ref, out_w, sems.at[0]),
        pltpu.make_async_copy(feat_ref.at[halves[0]], feats.at[halves[0]], sems.at[1]),
        pltpu.make_async_copy(feat_ref.at[halves[1]], feats.at[halves[1]], sems.at[2]),
        pltpu.make_async_copy(up_ref, up, sems.at[3]),
        pltpu.make_async_copy(down_ref, down, sems.at[4]),
    ]
    for copy in copies:
        copy.start()
    for copy in arriving:
        copy.wait()
    copies[0].wait()
    firsts = []
    for half, at in enumerate(halves):
        added = mixed_rows(held.at[0], half, out_w[:COLS, :])
        for which in range(1, CHUNKS):
            weight = out_w[which * COLS : (which + 1) * COLS, :]
            added = added + mixed_rows(held.at[which], half, weight)
        copies[1 + half].wait()
        mixed = feats[at, :].astype(F32) + added
        firsts.append(normed(mixed, gain_ref[0:1, :]).astype(BF16))
    for half, at in enumerate(halves):
        first = firsts[half]
        if half == 0:
            copies[3].wait()
        hidden = jnp.maximum(jnp.dot(first, up[...], preferred_element_type=F32), 0.0).astype(BF16)
        if half == 0:
            copies[4].wait()
        total = first.astype(F32) + jnp.dot(hidden, down[...], preferred_element_type=F32)
        made[at, :] = normed(total, gain_ref[1:2, :]).astype(BF16)
        copies.append(pltpu.make_async_copy(made.at[at], result_ref.at[at], sems.at[5 + half]))
        copies[-1].start()
    for copy in copies[5:]:
        copy.wait()


def finish(place, features, backs, w_out, w_up, w_down, gains):
    rows, width = features.shape
    return pl.pallas_call(
        finish_kernel,
        in_specs=[SMEM] + [HBM] * (CHUNKS * CHIPS + 4) + [VMEM],
        out_specs=HBM,
        out_shape=jax.ShapeDtypeStruct((rows, width), BF16),
        scratch_shapes=[
            pltpu.VMEM((CHUNKS, CHIPS, OWN) + TILE, BF16),
            pltpu.VMEM((rows, width), BF16),
            pltpu.VMEM(w_out.shape, BF16),
            pltpu.VMEM(w_up.shape, BF16),
            pltpu.VMEM(w_down.shape, BF16),
            pltpu.VMEM((rows, width), BF16),
            pltpu.SemaphoreType.DMA((CHUNKS, CHIPS)),
            pltpu.SemaphoreType.DMA((7,)),
        ],
        compiler_params=params(0),
        name="finish",
    )(place, features, *[part for back in backs for part in back], w_out, w_up, w_down, gains)


def swap(array):
    return lax.ppermute(array, "head", [(i, i ^ 1) for i in range(2 * CHIPS)])


def along_z(parts):
    moved = list(parts)
    for step in (2, 1, 3):
        moved[step] = lax.ppermute(
            parts[step], "head", [(i, (i + 2 * step) % (2 * CHIPS)) for i in range(2 * CHIPS)]
        )
    return moved


def per_device(
    features, w_query, w_key, w_value, w_out, w_up, w_down, gain_attn, gain_ffn,
    send_list, edge_owner, edge_slot, edge_count,
):
    head = lax.axis_index("head").astype(jnp.int32)
    place = jnp.stack([head // 2, head % 2])
    groups = send_list.shape[1]
    owners, slots = edge_owner.T, edge_slot.T
    far = swap(features)
    collected = []
    for c in range(CHUNKS):
        if c == 0:
            whole = project_first(features, w_key, w_value)
            whole = lax.all_to_all(whole, "head", split_axis=0, concat_axis=0, tiled=True)
            parts = [whole.reshape((-1,) + TILE)]
        else:
            parts = project_keys_values(place, features, far, w_key, w_value, c)
            parts = along_z(parts)
        collected.append(collect(send_list, place, parts))
    queries = along_z(project_queries(place, features, w_query))
    mines = []
    for c in range(CHUNKS):
        sent = collected[c][0].reshape((groups, CAP) + TILE)
        got = lax.all_to_all(sent, "node", split_axis=0, concat_axis=0, tiled=True)
        mines.append(got.reshape((groups * CAP,) + TILE))
    backs = []
    for c in range(CHUNKS):
        swapped = swap(collected[c][2])
        other = swap(mines[c])
        tables = (owners, slots, edge_count)
        done = attend(
            tables, place, queries, collected[c][1], swapped, mines[c], other, c
        )
        backs.append(along_z(done))
    gains = stack_gains(gain_attn, gain_ffn)
    return finish(place, features, backs, w_out, w_up, w_down, gains)


def solution(mesh):
    return jax.shard_map(
        per_device,
        mesh=mesh,
        in_specs=(
            P(("node", "head"), None),
            P(), P(), P(), P(), P(), P(), P(), P(),
            P("node", None, None),
            P("node", None),
            P("node", None),
            P("node"),
        ),
        out_specs=P(("node", "head"), None),
        check_vma=False,
    )
```

```python
import functools
import math

import jax
import jax.numpy as jnp
from jax import lax
from jax.experimental import pallas as pl
from jax.experimental.pallas import tpu as pltpu
from jax.sharding import PartitionSpec as P


HDIM = 64
BLOCK = 64
MAXK = 8
CAP = 16
HALF = BLOCK // 2
LANES = 2 * HDIM
CHUNKS = 3
CHIPS = 4
COLS = CHIPS * HDIM
OWN = 16
SCALE = 1.4426950408889634 / math.sqrt(HDIM)
MASKED = -8e30
F32 = jnp.float32
BF16 = jnp.bfloat16
VMEM = pl.BlockSpec(memory_space=pltpu.VMEM)
SMEM = pl.BlockSpec(memory_space=pltpu.SMEM)
HBM = pl.BlockSpec(memory_space=pltpu.HBM)
TILE = (HALF, LANES)


def low_lanes(rows):
    return lax.broadcasted_iota(jnp.int32, (rows, LANES), 1) < HDIM


def pack_pair(both):
    blocks = both.shape[0] // BLOCK
    split = both.reshape(blocks, 2, HALF, LANES)
    first = split[:, 0].reshape(blocks * HALF, LANES)
    second = split[:, 1].reshape(blocks * HALF, LANES)
    low = low_lanes(blocks * HALF)
    even = jnp.where(low, first, pltpu.roll(second, HDIM, 1))
    odd = jnp.where(low, pltpu.roll(first, HDIM, 1), second)
    return [part.reshape(blocks, HALF, LANES).astype(BF16) for part in (even, odd)]


def unpack_pair(even, odd):
    blocks = even.shape[0]
    even = even.reshape(blocks * HALF, LANES).astype(F32)
    odd = odd.reshape(blocks * HALF, LANES).astype(F32)
    low = low_lanes(blocks * HALF)
    first = jnp.where(low, even, pltpu.roll(odd, HDIM, 1)).reshape(blocks, 1, HALF, LANES)
    second = jnp.where(low, pltpu.roll(even, HDIM, 1), odd).reshape(blocks, 1, HALF, LANES)
    return jnp.concatenate([first, second], axis=1).reshape(blocks * BLOCK, LANES).astype(BF16)


def params(room):
    return pltpu.CompilerParams(vmem_limit_bytes=67_043_328 - room)


def fetch_weight(chunk, core, key_ref, value_ref, weight, sem):
    def fetch(source):
        copy = pltpu.make_async_copy(source.at[:, chunk * COLS : (chunk + 1) * COLS], weight, sem)
        copy.start()
        copy.wait()

    @pl.when(core == 0)
    def _():
        fetch(key_ref)

    @pl.when(core == 1)
    def _():
        fetch(value_ref)


def pack_rows(feat_ref, weight, packed, first):
    for half in range(2):
        made = jnp.dot(
            feat_ref[half * 512 : half * 512 + 512, :], weight[...], preferred_element_type=F32
        )
        for pair in range(2):
            both = pack_pair(made[:, pair * LANES : (pair + 1) * LANES])
            for side in range(2):
                packed[2 * pair + side, pl.ds(first + half * 8, 8)] = both[side]


def first_kernel(feat_ref, key_ref, value_ref, *refs):
    out_ref, feats, weights, made, sems, done = refs
    halves = [slice(half * 512, half * 512 + 512) for half in range(2)]
    fetches = [
        pltpu.make_async_copy(key_ref.at[:, :COLS], weights.at[0], sems.at[0]),
        pltpu.make_async_copy(feat_ref.at[halves[0]], feats.at[halves[0]], sems.at[1]),
        pltpu.make_async_copy(feat_ref.at[halves[1]], feats.at[halves[1]], sems.at[2]),
        pltpu.make_async_copy(value_ref.at[:, :COLS], weights.at[1], sems.at[3]),
    ]
    for copy in fetches:
        copy.start()
    copies = []
    fetches[0].wait()
    for kind in range(2):
        if kind == 1:
            fetches[3].wait()
        for half, at in enumerate(halves):
            if kind == 0:
                fetches[1 + half].wait()
            rows = jnp.dot(feats[at, :], weights[kind], preferred_element_type=F32)
            for pair in range(2):
                both = pack_pair(rows[:, pair * LANES : (pair + 1) * LANES])
                for side in range(2):
                    dest = 2 * (2 * pair + side) + kind
                    made[dest, half * 8 : half * 8 + 8] = both[side]
        for z in range(CHIPS):
            dest = 2 * z + kind
            copies.append(pltpu.make_async_copy(made.at[dest], out_ref.at[dest], done.at[dest]))
            copies[-1].start()
    for copy in copies:
        copy.wait()


def project_first(features, w_key, w_value):
    rows, width = features.shape
    return pl.pallas_call(
        first_kernel,
        in_specs=[HBM] * 3,
        out_specs=HBM,
        out_shape=jax.ShapeDtypeStruct((2 * CHIPS, OWN) + TILE, BF16),
        scratch_shapes=[
            pltpu.VMEM((rows, width), BF16),
            pltpu.VMEM((2, width, COLS), BF16),
            pltpu.VMEM((2 * CHIPS, OWN) + TILE, BF16),
            pltpu.SemaphoreType.DMA((4,)),
            pltpu.SemaphoreType.DMA((2 * CHIPS,)),
        ],
        compiler_params=params(0),
        cost_estimate=pl.CostEstimate(
            flops=4 * rows * width * COLS, bytes_accessed=4 << 20, transcendentals=0
        ),
        name="first_keys_values",
    )(features, w_key, w_value)


def keys_values_kernel(chunk, place_ref, near_ref, far_ref, key_ref, value_ref, *refs):
    outs, (weight, packed, sem) = refs[:CHIPS], refs[CHIPS:]
    z, core = place_ref[0], place_ref[1]
    fetch_weight(chunk, core, key_ref, value_ref, weight, sem)
    pack_rows(near_ref, weight, packed, core * OWN)
    pack_rows(far_ref, weight, packed, (1 - core) * OWN)
    for step in range(CHIPS):
        outs[step][...] = packed[lax.rem(z + step, CHIPS)]


def project_keys_values(place, near, far, w_key, w_value, chunk):
    rows, width = near.shape
    return pl.pallas_call(
        functools.partial(keys_values_kernel, chunk),
        in_specs=[SMEM, VMEM, VMEM, HBM, HBM],
        out_specs=[VMEM] * CHIPS,
        out_shape=[jax.ShapeDtypeStruct((2 * OWN,) + TILE, BF16)] * CHIPS,
        scratch_shapes=[
            pltpu.VMEM((width, COLS), BF16),
            pltpu.VMEM((CHIPS, 2 * OWN) + TILE, BF16),
            pltpu.SemaphoreType.DMA,
        ],
        compiler_params=params(0),
        cost_estimate=pl.CostEstimate(
            flops=4 * rows * width * COLS, bytes_accessed=5 << 20, transcendentals=0
        ),
        name="keys_values",
    )(place, near, far, w_key, w_value)


def queries_kernel(place_ref, feat_ref, query_ref, *refs):
    outs, (packed,) = refs[:CHIPS], refs[CHIPS:]
    z = place_ref[0]
    for chunk in range(CHUNKS):
        for half in range(2):
            made = jnp.dot(
                feat_ref[half * 512 : half * 512 + 512, :],
                query_ref[:, chunk * COLS : (chunk + 1) * COLS],
                preferred_element_type=F32,
            )
            for pair in range(2):
                both = pack_pair(made[:, pair * LANES : (pair + 1) * LANES])
                for side in range(2):
                    packed[2 * pair + side, chunk, half * 8 : half * 8 + 8] = both[side]
    for step in range(CHIPS):
        outs[step][...] = packed[lax.rem(z + step, CHIPS)]


def project_queries(place, features, w_query):
    rows, width = features.shape
    return pl.pallas_call(
        queries_kernel,
        in_specs=[SMEM, VMEM, VMEM],
        out_specs=[VMEM] * CHIPS,
        out_shape=[jax.ShapeDtypeStruct((CHUNKS, OWN) + TILE, BF16)] * CHIPS,
        scratch_shapes=[pltpu.VMEM((CHIPS, CHUNKS, OWN) + TILE, BF16)],
        compiler_params=params(0),
        cost_estimate=pl.CostEstimate(
            flops=2 * rows * width * width, bytes_accessed=5 << 20, transcendentals=0
        ),
        name="queries",
    )(place, features, w_query)


def collect_kernel(count, list_ref, place_ref, *refs):
    parts, (out_ref, own_ref, swap_ref, *scratch) = refs[:count], refs[count:]
    z, core = place_ref[0], place_ref[1]
    if count == 1:
        held, (picked, sems) = parts[0], scratch
    else:
        held, picked, sems = scratch
        for step in range(CHIPS):
            source = lax.rem(z + CHIPS - step, CHIPS)
            held[pl.ds(source * 2 * OWN, 2 * OWN)] = parts[step][...]
    quarter = picked.shape[0] // CAP // 4

    def body(step, carry):
        for extra in range(CAP):
            picked[step * CAP + extra] = held[list_ref[0, step, extra]]
        return carry

    copies = []
    for part in range(4):
        lax.fori_loop(part * quarter, (part + 1) * quarter, body, 0)
        at = pl.ds(part * quarter * CAP, quarter * CAP)
        copies.append(pltpu.make_async_copy(picked.at[at], out_ref.at[at], sems.at[part]))
        copies[-1].start()
    for source in range(CHIPS):
        for which, target in enumerate((own_ref, swap_ref)):
            side = core if which == 0 else 1 - core
            at = pl.ds(source * 2 * OWN + side * OWN, OWN)
            copies.append(
                pltpu.make_async_copy(
                    held.at[at], target.at[source], sems.at[4 + 2 * source + which]
                )
            )
            copies[-1].start()
    for copy in copies:
        copy.wait()


def collect(send_list, place, parts):
    slots = send_list.shape[1] * send_list.shape[2]
    own = jax.ShapeDtypeStruct((CHIPS, OWN) + TILE, BF16)
    return pl.pallas_call(
        functools.partial(collect_kernel, len(parts)),
        in_specs=[SMEM, SMEM] + [VMEM] * len(parts),
        out_specs=[HBM] * 3,
        out_shape=[jax.ShapeDtypeStruct((slots,) + TILE, BF16), own, own],
        scratch_shapes=[pltpu.VMEM((CHIPS * 2 * OWN,) + TILE, BF16)] * (len(parts) > 1)
        + [pltpu.VMEM((slots,) + TILE, BF16), pltpu.SemaphoreType.DMA((4 + 2 * CHIPS,))],
        compiler_params=params(0),
        cost_estimate=pl.CostEstimate(flops=0, bytes_accessed=5 << 20, transcendentals=0),
        name="collect",
    )(send_list, place, *parts)


def attend_kernel(chunk, carried, owner_ref, slot_ref, count_ref, place_ref, *refs):
    parts, (own_ref, swap_ref, mine_ref, other_ref) = refs[:CHIPS], refs[CHIPS : CHIPS + 4]
    befores, refs = refs[CHIPS + 4 : CHIPS + 4 + carried], refs[CHIPS + 4 + carried :]
    outs, refs = refs[:CHIPS], refs[CHIPS:]
    queries, made, keys, values, own_keys, own_values, asked, sems, done = refs[:9]
    z, core = place_ref[0], place_ref[1]

    asking = []
    for step in range(CHIPS):
        source = lax.rem(z + CHIPS - step, CHIPS)
        asking.append(
            pltpu.make_async_copy(parts[step].at[chunk], queries.at[source], asked.at[step])
        )
        asking[-1].start()

    def place_in(near, near_own, far, far_own):
        copies = [
            pltpu.make_async_copy(mine_ref, near, sems.at[0]),
            pltpu.make_async_copy(other_ref, far, sems.at[1]),
            pltpu.make_async_copy(own_ref, near_own, sems.at[2]),
            pltpu.make_async_copy(swap_ref, far_own, sems.at[3]),
        ]
        for copy in copies:
            copy.start()
        for copy in copies:
            copy.wait()

    @pl.when(core == 0)
    def _():
        place_in(keys, own_keys, values, own_values)

    @pl.when(core == 1)
    def _():
        place_in(values, own_values, keys, own_keys)

    for copy in asking:
        copy.wait()
    targets = outs
    if carried:
        before, taken, passed = refs[9:]
        taking = []
        for step in range(CHIPS):
            taking.append(
                pltpu.make_async_copy(befores[step], before.at[step], taken.at[step])
            )
            taking[-1].start()
        targets = [out.at[1] for out in outs]

    low = low_lanes(HALF)
    lane = lax.broadcasted_iota(jnp.int32, (1, LANES), 1)
    dims = (((1,), (1,)), ((), ()))
    rows = 2 * BLOCK
    group = 8

    def attend_group(at, carry):
        ahead = lax.rem(at // 2 + 1, CHIPS)
        source, first = lax.rem(z + ahead, CHIPS), (at % 2) * group
        blocks = [source * 2 * OWN + core * OWN + first + k for k in range(group)]
        slots = [
            [owner_ref[entry, block] * CAP + slot_ref[entry, block] for entry in range(MAXK)]
            for block in blocks
        ]
        left = []
        for k in range(group):
            query = queries[source, first + k].astype(F32)
            turned = pltpu.roll(query, HDIM, 1)
            zero = jnp.zeros_like(query)
            left.append(
                jnp.concatenate(
                    [
                        jnp.where(low, query, zero),
                        jnp.where(low, turned, zero),
                        jnp.where(low, zero, turned),
                        jnp.where(low, zero, query),
                    ],
                    axis=0,
                ).astype(BF16)
            )
        near = []
        for quad in range(group // 4):
            four = own_keys[source, pl.ds(first + 4 * quad, 4)].reshape(LANES, LANES)
            scores = lax.dot_general(
                jnp.concatenate(left[4 * quad : 4 * quad + 4], axis=0),
                four,
                dims,
                preferred_element_type=F32,
            )
            for j in range(4):
                near.append(
                    jnp.where(lane // HALF == j, scores[j * rows : (j + 1) * rows], MASKED)
                )
        far = []
        for k in range(group):
            far_keys = jnp.concatenate([keys[slot] for slot in slots[k]], axis=0)
            scores = lax.dot_general(left[k], far_keys, dims, preferred_element_type=F32)
            limit = count_ref[blocks[k]] * HALF
            far.append(
                [
                    jnp.where(lane < limit, scores[:, :LANES], MASKED),
                    jnp.where(lane + LANES < limit, scores[:, LANES:], MASKED),
                ]
            )
        tops = []
        for k in range(group):
            top = jnp.maximum(jnp.maximum(far[k][0], far[k][1]), near[k])
            top = jnp.max(jnp.maximum(top[:BLOCK], top[BLOCK:]), axis=1, keepdims=True)
            tops.append(jnp.concatenate([top, top], axis=0))
        far = [[jnp.exp2((part - tops[k]) * SCALE) for part in far[k]] for k in range(group)]
        near = [jnp.exp2((near[k] - tops[k]) * SCALE) for k in range(group)]
        summed = []
        for quad in range(group // 4):
            four = own_values[source, pl.ds(first + 4 * quad, 4)].reshape(LANES, LANES)
            weights = [near[4 * quad + j].astype(BF16) for j in range(4)]
            product = jnp.dot(
                jnp.concatenate(weights, axis=0), four, preferred_element_type=F32
            )
            summed += [product[j * rows : (j + 1) * rows] for j in range(4)]
        for k in range(group):
            far_values = jnp.concatenate([values[slot] for slot in slots[k]], axis=0)
            weights = jnp.concatenate([part.astype(BF16) for part in far[k]], axis=1)
            summed[k] = summed[k] + jnp.dot(weights, far_values, preferred_element_type=F32)
        for k in range(group):
            total = far[k][0] + far[k][1] + near[k]
            total = jnp.sum(total[:BLOCK] + total[BLOCK:], axis=1, keepdims=True)
            share = 1.0 / total
            share = jnp.where(low, share[:HALF], share[HALF:])
            straight = jnp.where(low, summed[k][:HALF], summed[k][3 * HALF :])
            crossed = jnp.where(low, summed[k][HALF : 2 * HALF], summed[k][2 * HALF : 3 * HALF])
            result = (straight + pltpu.roll(crossed, HDIM, 1)) * share
            made[source, first + k] = result.astype(BF16)
        for step in range(CHIPS):

            @pl.when(jnp.logical_and(at % 2 == 1, ahead == step))
            def _():
                pltpu.make_async_copy(made.at[source], targets[step], done.at[step]).start()

        return carry

    lax.fori_loop(0, CHIPS * OWN // group, attend_group, 0)
    if carried:
        passing = []
        for step in range(CHIPS):
            taking[step].wait()
            passing.append(
                pltpu.make_async_copy(before.at[step], outs[step].at[0], passed.at[step])
            )
            passing[-1].start()
        for copy in passing:
            copy.wait()
    for step in range(CHIPS):
        source = lax.rem(z + step, CHIPS)
        pltpu.make_async_copy(made.at[source], targets[step], done.at[step]).wait()


def attend(tables, place, queries, own, swapped, mine, other, chunk, before=()):
    slots = mine.shape[0]
    blocks = pltpu.VMEM((CHIPS, OWN) + TILE, BF16)
    return pl.pallas_call(
        functools.partial(attend_kernel, chunk, len(before)),
        in_specs=[SMEM] * 4 + [HBM] * (CHIPS + 4 + len(before)),
        out_specs=[HBM] * CHIPS,
        out_shape=[jax.ShapeDtypeStruct((2,) * (len(before) > 0) + (OWN,) + TILE, BF16)] * CHIPS,
        scratch_shapes=[
            blocks,
            blocks,
            pltpu.VMEM((slots,) + TILE, BF16),
            pltpu.VMEM((slots,) + TILE, BF16),
            blocks,
            blocks,
            pltpu.SemaphoreType.DMA((CHIPS,)),
            pltpu.SemaphoreType.DMA((4,)),
            pltpu.SemaphoreType.DMA((CHIPS,)),
        ]
        + [blocks, pltpu.SemaphoreType.DMA((CHIPS,)), pltpu.SemaphoreType.DMA((CHIPS,))]
        * (len(before) > 0),
        compiler_params=params(0),
        cost_estimate=pl.CostEstimate(
            flops=64 * 4 * 128 * 128 * 384, bytes_accessed=8 << 20, transcendentals=64 * 128 * 384
        ),
        name="attend",
    )(*tables, place, *queries, own, swapped, mine, other, *before)


def normed(values, gain):
    center = values - jnp.mean(values, axis=-1, keepdims=True)
    spread = jnp.mean(center * center, axis=-1, keepdims=True)
    return center * lax.rsqrt(spread + 1e-05) * gain


def mixed_rows(held, half, weight):
    at = slice(half * 8, half * 8 + 8)
    pieces = [unpack_pair(held[2 * pair, at], held[2 * pair + 1, at]) for pair in range(2)]
    return jnp.dot(jnp.concatenate(pieces, axis=1), weight, preferred_element_type=F32)


def gather_parts(place_ref, parts, held, sems):
    copies = []
    for step in range(CHIPS):
        source = lax.rem(place_ref[0] + CHIPS - step, CHIPS)
        copies.append(pltpu.make_async_copy(parts[step], held.at[source], sems.at[step]))
        copies[-1].start()
    return copies


def gains_kernel(attn_ref, ffn_ref, out_ref):
    out_ref[0, :] = attn_ref[...]
    out_ref[1, :] = ffn_ref[...]


def stack_gains(gain_attn, gain_ffn):
    return pl.pallas_call(
        gains_kernel,
        in_specs=[VMEM, VMEM],
        out_specs=VMEM,
        out_shape=jax.ShapeDtypeStruct((2,) + gain_attn.shape, F32),
        compiler_params=params(0),
        name="gains",
    )(gain_attn, gain_ffn)


def finish_kernel(place_ref, feat_ref, *refs):
    parts, refs = refs[: 2 * CHIPS], refs[2 * CHIPS :]
    out_w_ref, up_ref, down_ref, gain_ref, result_ref, *scratch = refs
    held, feats, out_w, up, down, made, arrive, sems = scratch
    rows = feat_ref.shape[0] // 2
    halves = [slice(half * rows, (half + 1) * rows) for half in range(2)]
    arriving = []
    for which in range(CHUNKS):
        if which < CHUNKS - 1:
            some = [part.at[which] for part in parts[:CHIPS]]
        else:
            some = parts[CHIPS:]
        arriving += gather_parts(place_ref, some, held.at[which], arrive.at[which])
    copies = [
        pltpu.make_async_copy(out_w_ref, out_w, sems.at[0]),
        pltpu.make_async_copy(feat_ref.at[halves[0]], feats.at[halves[0]], sems.at[1]),
        pltpu.make_async_copy(feat_ref.at[halves[1]], feats.at[halves[1]], sems.at[2]),
        pltpu.make_async_copy(up_ref, up, sems.at[3]),
        pltpu.make_async_copy(down_ref, down, sems.at[4]),
    ]
    for copy in copies:
        copy.start()
    for copy in arriving:
        copy.wait()
    copies[0].wait()
    firsts = []
    for half, at in enumerate(halves):
        added = mixed_rows(held.at[0], half, out_w[:COLS, :])
        for which in range(1, CHUNKS):
            weight = out_w[which * COLS : (which + 1) * COLS, :]
            added = added + mixed_rows(held.at[which], half, weight)
        copies[1 + half].wait()
        mixed = feats[at, :].astype(F32) + added
        firsts.append(normed(mixed, gain_ref[0:1, :]).astype(BF16))
    rows = rows // 2
    firsts = [first[at : at + rows] for first in firsts for at in (0, rows)]
    for half, first in enumerate(firsts):
        at = slice(half * rows, (half + 1) * rows)
        if half == 0:
            copies[3].wait()
        hidden = jnp.maximum(jnp.dot(first, up[...], preferred_element_type=F32), 0.0).astype(BF16)
        if half == 0:
            copies[4].wait()
        total = first.astype(F32) + jnp.dot(hidden, down[...], preferred_element_type=F32)
        made[at, :] = normed(total, gain_ref[1:2, :]).astype(BF16)
        copies.append(pltpu.make_async_copy(made.at[at], result_ref.at[at], sems.at[5 + half]))
        copies[-1].start()
    for copy in copies[5:]:
        copy.wait()


def finish(place, features, backs, w_out, w_up, w_down, gains):
    rows, width = features.shape
    return pl.pallas_call(
        finish_kernel,
        in_specs=[SMEM] + [HBM] * (2 * CHIPS + 4) + [VMEM],
        out_specs=HBM,
        out_shape=jax.ShapeDtypeStruct((rows, width), BF16),
        scratch_shapes=[
            pltpu.VMEM((CHUNKS, CHIPS, OWN) + TILE, BF16),
            pltpu.VMEM((rows, width), BF16),
            pltpu.VMEM(w_out.shape, BF16),
            pltpu.VMEM(w_up.shape, BF16),
            pltpu.VMEM(w_down.shape, BF16),
            pltpu.VMEM((rows, width), BF16),
            pltpu.SemaphoreType.DMA((CHUNKS, CHIPS)),
            pltpu.SemaphoreType.DMA((9,)),
        ],
        compiler_params=params(0),
        name="finish",
    )(place, features, *[part for back in backs for part in back], w_out, w_up, w_down, gains)


def swap(array):
    return lax.ppermute(array, "head", [(i, i ^ 1) for i in range(2 * CHIPS)])


def along_z(parts):
    moved = list(parts)
    for step in (2, 1, 3):
        moved[step] = lax.ppermute(
            parts[step], "head", [(i, (i + 2 * step) % (2 * CHIPS)) for i in range(2 * CHIPS)]
        )
    return moved


def per_device(
    features, w_query, w_key, w_value, w_out, w_up, w_down, gain_attn, gain_ffn,
    send_list, edge_owner, edge_slot, edge_count,
):
    head = lax.axis_index("head").astype(jnp.int32)
    place = jnp.stack([head // 2, head % 2])
    groups = send_list.shape[1]
    owners, slots = edge_owner.T, edge_slot.T
    far = swap(features)
    collected = []
    for c in range(CHUNKS):
        if c == 0:
            whole = project_first(features, w_key, w_value)
            whole = lax.all_to_all(whole, "head", split_axis=0, concat_axis=0, tiled=True)
            parts = [whole.reshape((-1,) + TILE)]
        else:
            parts = project_keys_values(place, features, far, w_key, w_value, c)
            parts = along_z(parts)
        collected.append(collect(send_list, place, parts))
    queries = along_z(project_queries(place, features, w_query))
    mines = []
    for c in range(CHUNKS):
        sent = collected[c][0].reshape((groups, CAP) + TILE)
        got = lax.all_to_all(sent, "node", split_axis=0, concat_axis=0, tiled=True)
        mines.append(got.reshape((groups * CAP,) + TILE))
    backs = []
    for c in range(CHUNKS):
        swapped = swap(collected[c][2])
        other = swap(mines[c])
        tables = (owners, slots, edge_count)
        before = done if c == 1 else ()
        done = attend(tables, place, queries, collected[c][1], swapped, mines[c], other, c, before)
        if c > 0:
            backs.append(along_z(done))
    gains = stack_gains(gain_attn, gain_ffn)
    return finish(place, features, backs, w_out, w_up, w_down, gains)


def solution(mesh):
    return jax.shard_map(
        per_device,
        mesh=mesh,
        in_specs=(
            P(("node", "head"), None),
            P(), P(), P(), P(), P(), P(), P(), P(),
            P("node", None, None),
            P("node", None),
            P("node", None),
            P("node"),
        ),
        out_specs=P(("node", "head"), None),
        check_vma=False,
    )
```

```python
import functools
import math

import jax
import jax.numpy as jnp
from jax import lax
from jax.experimental import pallas as pl
from jax.experimental.pallas import tpu as pltpu
from jax.sharding import PartitionSpec as P


HDIM = 64
BLOCK = 64
MAXK = 8
CAP = 16
HALF = BLOCK // 2
LANES = 2 * HDIM
CHUNKS = 3
CHIPS = 4
COLS = CHIPS * HDIM
OWN = 16
SCALE = 1.4426950408889634 / math.sqrt(HDIM)
MASKED = -8e30
F32 = jnp.float32
BF16 = jnp.bfloat16
VMEM = pl.BlockSpec(memory_space=pltpu.VMEM)
SMEM = pl.BlockSpec(memory_space=pltpu.SMEM)
HBM = pl.BlockSpec(memory_space=pltpu.HBM)
TILE = (HALF, LANES)


def low_lanes(rows):
    return lax.broadcasted_iota(jnp.int32, (rows, LANES), 1) < HDIM


def pack_pair(both):
    blocks = both.shape[0] // BLOCK
    split = both.reshape(blocks, 2, HALF, LANES)
    first = split[:, 0].reshape(blocks * HALF, LANES)
    second = split[:, 1].reshape(blocks * HALF, LANES)
    low = low_lanes(blocks * HALF)
    even = jnp.where(low, first, pltpu.roll(second, HDIM, 1))
    odd = jnp.where(low, pltpu.roll(first, HDIM, 1), second)
    return [part.reshape(blocks, HALF, LANES).astype(BF16) for part in (even, odd)]


def unpack_pair(even, odd):
    blocks = even.shape[0]
    even = even.reshape(blocks * HALF, LANES).astype(F32)
    odd = odd.reshape(blocks * HALF, LANES).astype(F32)
    low = low_lanes(blocks * HALF)
    first = jnp.where(low, even, pltpu.roll(odd, HDIM, 1)).reshape(blocks, 1, HALF, LANES)
    second = jnp.where(low, pltpu.roll(even, HDIM, 1), odd).reshape(blocks, 1, HALF, LANES)
    return jnp.concatenate([first, second], axis=1).reshape(blocks * BLOCK, LANES).astype(BF16)


def params(room):
    return pltpu.CompilerParams(vmem_limit_bytes=67_043_328 - room)


def fetch_weight(chunk, core, key_ref, value_ref, weight, sem):
    def fetch(source):
        copy = pltpu.make_async_copy(source.at[:, chunk * COLS : (chunk + 1) * COLS], weight, sem)
        copy.start()
        copy.wait()

    @pl.when(core == 0)
    def _():
        fetch(key_ref)

    @pl.when(core == 1)
    def _():
        fetch(value_ref)


def pack_rows(feat_ref, weight, packed, first):
    for half in range(2):
        made = jnp.dot(
            feat_ref[half * 512 : half * 512 + 512, :], weight[...], preferred_element_type=F32
        )
        for pair in range(2):
            both = pack_pair(made[:, pair * LANES : (pair + 1) * LANES])
            for side in range(2):
                packed[2 * pair + side, pl.ds(first + half * 8, 8)] = both[side]


def first_kernel(feat_ref, key_ref, value_ref, *refs):
    out_ref, feats, weights, made, sems, done = refs
    halves = [slice(half * 512, half * 512 + 512) for half in range(2)]
    fetches = [
        pltpu.make_async_copy(key_ref.at[:, :COLS], weights.at[0], sems.at[0]),
        pltpu.make_async_copy(feat_ref.at[halves[0]], feats.at[halves[0]], sems.at[1]),
        pltpu.make_async_copy(feat_ref.at[halves[1]], feats.at[halves[1]], sems.at[2]),
        pltpu.make_async_copy(value_ref.at[:, :COLS], weights.at[1], sems.at[3]),
    ]
    for copy in fetches:
        copy.start()
    copies = []
    fetches[0].wait()
    for kind in range(2):
        if kind == 1:
            fetches[3].wait()
        for half, at in enumerate(halves):
            if kind == 0:
                fetches[1 + half].wait()
            rows = jnp.dot(feats[at, :], weights[kind], preferred_element_type=F32)
            for pair in range(2):
                both = pack_pair(rows[:, pair * LANES : (pair + 1) * LANES])
                for side in range(2):
                    dest = 2 * (2 * pair + side) + kind
                    made[dest, half * 8 : half * 8 + 8] = both[side]
        for z in range(CHIPS):
            dest = 2 * z + kind
            copies.append(pltpu.make_async_copy(made.at[dest], out_ref.at[dest], done.at[dest]))
            copies[-1].start()
    for copy in copies:
        copy.wait()


def project_first(features, w_key, w_value):
    rows, width = features.shape
    return pl.pallas_call(
        first_kernel,
        in_specs=[HBM] * 3,
        out_specs=HBM,
        out_shape=jax.ShapeDtypeStruct((2 * CHIPS, OWN) + TILE, BF16),
        scratch_shapes=[
            pltpu.VMEM((rows, width), BF16),
            pltpu.VMEM((2, width, COLS), BF16),
            pltpu.VMEM((2 * CHIPS, OWN) + TILE, BF16),
            pltpu.SemaphoreType.DMA((4,)),
            pltpu.SemaphoreType.DMA((2 * CHIPS,)),
        ],
        compiler_params=params(0),
        cost_estimate=pl.CostEstimate(
            flops=4 * rows * width * COLS, bytes_accessed=4 << 20, transcendentals=0
        ),
        name="first_keys_values",
    )(features, w_key, w_value)


def keys_values_kernel(chunk, place_ref, near_ref, far_ref, key_ref, value_ref, *refs):
    outs, (weight, packed, sem) = refs[:CHIPS], refs[CHIPS:]
    z, core = place_ref[0], place_ref[1]
    fetch_weight(chunk, core, key_ref, value_ref, weight, sem)
    pack_rows(near_ref, weight, packed, core * OWN)
    pack_rows(far_ref, weight, packed, (1 - core) * OWN)
    for step in range(CHIPS):
        outs[step][...] = packed[lax.rem(z + step, CHIPS)]


def project_keys_values(place, near, far, w_key, w_value, chunk):
    rows, width = near.shape
    return pl.pallas_call(
        functools.partial(keys_values_kernel, chunk),
        in_specs=[SMEM, VMEM, VMEM, HBM, HBM],
        out_specs=[VMEM] * CHIPS,
        out_shape=[jax.ShapeDtypeStruct((2 * OWN,) + TILE, BF16)] * CHIPS,
        scratch_shapes=[
            pltpu.VMEM((width, COLS), BF16),
            pltpu.VMEM((CHIPS, 2 * OWN) + TILE, BF16),
            pltpu.SemaphoreType.DMA,
        ],
        compiler_params=params(0),
        cost_estimate=pl.CostEstimate(
            flops=4 * rows * width * COLS, bytes_accessed=5 << 20, transcendentals=0
        ),
        name="keys_values",
    )(place, near, far, w_key, w_value)


def queries_kernel(place_ref, feat_ref, query_ref, *refs):
    outs, (packed,) = refs[:CHIPS], refs[CHIPS:]
    z = place_ref[0]
    for chunk in range(CHUNKS):
        for half in range(2):
            made = jnp.dot(
                feat_ref[half * 512 : half * 512 + 512, :],
                query_ref[:, chunk * COLS : (chunk + 1) * COLS],
                preferred_element_type=F32,
            )
            for pair in range(2):
                both = pack_pair(made[:, pair * LANES : (pair + 1) * LANES])
                for side in range(2):
                    packed[2 * pair + side, chunk, half * 8 : half * 8 + 8] = both[side]
    for step in range(CHIPS):
        outs[step][...] = packed[lax.rem(z + step, CHIPS)]


def project_queries(place, features, w_query):
    rows, width = features.shape
    return pl.pallas_call(
        queries_kernel,
        in_specs=[SMEM, VMEM, VMEM],
        out_specs=[VMEM] * CHIPS,
        out_shape=[jax.ShapeDtypeStruct((CHUNKS, OWN) + TILE, BF16)] * CHIPS,
        scratch_shapes=[pltpu.VMEM((CHIPS, CHUNKS, OWN) + TILE, BF16)],
        compiler_params=params(0),
        cost_estimate=pl.CostEstimate(
            flops=2 * rows * width * width, bytes_accessed=5 << 20, transcendentals=0
        ),
        name="queries",
    )(place, features, w_query)


def collect_kernel(count, list_ref, place_ref, *refs):
    parts, (out_ref, own_ref, swap_ref, *scratch) = refs[:count], refs[count:]
    z, core = place_ref[0], place_ref[1]
    if count == 1:
        held, (picked, sems) = parts[0], scratch
    else:
        held, picked, sems = scratch
        for step in range(CHIPS):
            source = lax.rem(z + CHIPS - step, CHIPS)
            held[pl.ds(source * 2 * OWN, 2 * OWN)] = parts[step][...]
    quarter = picked.shape[0] // CAP // 4

    def body(step, carry):
        for extra in range(CAP):
            picked[step * CAP + extra] = held[list_ref[0, step, extra]]
        return carry

    copies = []
    for part in range(4):
        lax.fori_loop(part * quarter, (part + 1) * quarter, body, 0)
        at = pl.ds(part * quarter * CAP, quarter * CAP)
        copies.append(pltpu.make_async_copy(picked.at[at], out_ref.at[at], sems.at[part]))
        copies[-1].start()
    for source in range(CHIPS):
        for which, target in enumerate((own_ref, swap_ref)):
            side = core if which == 0 else 1 - core
            at = pl.ds(source * 2 * OWN + side * OWN, OWN)
            copies.append(
                pltpu.make_async_copy(
                    held.at[at], target.at[source], sems.at[4 + 2 * source + which]
                )
            )
            copies[-1].start()
    for copy in copies:
        copy.wait()


def collect(send_list, place, parts):
    slots = send_list.shape[1] * send_list.shape[2]
    own = jax.ShapeDtypeStruct((CHIPS, OWN) + TILE, BF16)
    return pl.pallas_call(
        functools.partial(collect_kernel, len(parts)),
        in_specs=[SMEM, SMEM] + [VMEM] * len(parts),
        out_specs=[HBM] * 3,
        out_shape=[jax.ShapeDtypeStruct((slots,) + TILE, BF16), own, own],
        scratch_shapes=[pltpu.VMEM((CHIPS * 2 * OWN,) + TILE, BF16)] * (len(parts) > 1)
        + [pltpu.VMEM((slots,) + TILE, BF16), pltpu.SemaphoreType.DMA((4 + 2 * CHIPS,))],
        compiler_params=params(0),
        cost_estimate=pl.CostEstimate(flops=0, bytes_accessed=5 << 20, transcendentals=0),
        name="collect",
    )(send_list, place, *parts)


def attend_kernel(chunk, carried, owner_ref, slot_ref, count_ref, place_ref, *refs):
    parts, (own_ref, swap_ref, mine_ref, other_ref) = refs[:CHIPS], refs[CHIPS : CHIPS + 4]
    befores, refs = refs[CHIPS + 4 : CHIPS + 4 + carried], refs[CHIPS + 4 + carried :]
    outs, refs = refs[:CHIPS], refs[CHIPS:]
    queries, made, keys, values, own_keys, own_values, asked, sems, done = refs[:9]
    z, core = place_ref[0], place_ref[1]

    asking = []
    for step in range(CHIPS):
        source = lax.rem(z + CHIPS - step, CHIPS)
        asking.append(
            pltpu.make_async_copy(parts[step].at[chunk], queries.at[source], asked.at[step])
        )
        asking[-1].start()

    def place_in(near, near_own, far, far_own):
        copies = [
            pltpu.make_async_copy(mine_ref, near, sems.at[0]),
            pltpu.make_async_copy(other_ref, far, sems.at[1]),
            pltpu.make_async_copy(own_ref, near_own, sems.at[2]),
            pltpu.make_async_copy(swap_ref, far_own, sems.at[3]),
        ]
        for copy in copies:
            copy.start()
        for copy in copies:
            copy.wait()

    @pl.when(core == 0)
    def _():
        place_in(keys, own_keys, values, own_values)

    @pl.when(core == 1)
    def _():
        place_in(values, own_values, keys, own_keys)

    for copy in asking:
        copy.wait()
    targets = outs
    if carried:
        before, taken, passed = refs[9:]
        taking = []
        for step in range(CHIPS):
            taking.append(
                pltpu.make_async_copy(befores[step], before.at[step], taken.at[step])
            )
            taking[-1].start()
        targets = [out.at[1] for out in outs]

    low = low_lanes(HALF)
    lane = lax.broadcasted_iota(jnp.int32, (1, LANES), 1)
    dims = (((1,), (1,)), ((), ()))
    rows = 2 * BLOCK
    group = 8

    def attend_group(at, carry):
        ahead = lax.rem(at // 2 + 1, CHIPS)
        source, first = lax.rem(z + ahead, CHIPS), (at % 2) * group
        blocks = [source * 2 * OWN + core * OWN + first + k for k in range(group)]
        slots = [
            [owner_ref[entry, block] * CAP + slot_ref[entry, block] for entry in range(MAXK)]
            for block in blocks
        ]
        left = []
        for k in range(group):
            query = queries[source, first + k].astype(F32)
            turned = pltpu.roll(query, HDIM, 1)
            zero = jnp.zeros_like(query)
            left.append(
                jnp.concatenate(
                    [
                        jnp.where(low, query, zero),
                        jnp.where(low, turned, zero),
                        jnp.where(low, zero, turned),
                        jnp.where(low, zero, query),
                    ],
                    axis=0,
                ).astype(BF16)
            )
        near = []
        for quad in range(group // 4):
            four = own_keys[source, pl.ds(first + 4 * quad, 4)].reshape(LANES, LANES)
            scores = lax.dot_general(
                jnp.concatenate(left[4 * quad : 4 * quad + 4], axis=0),
                four,
                dims,
                preferred_element_type=F32,
            )
            for j in range(4):
                near.append(
                    jnp.where(lane // HALF == j, scores[j * rows : (j + 1) * rows], MASKED)
                )
        far = []
        for k in range(group):
            far_keys = jnp.concatenate([keys[slot] for slot in slots[k]], axis=0)
            scores = lax.dot_general(left[k], far_keys, dims, preferred_element_type=F32)
            limit = count_ref[blocks[k]] * HALF
            far.append(
                [
                    jnp.where(lane < limit, scores[:, :LANES], MASKED),
                    jnp.where(lane + LANES < limit, scores[:, LANES:], MASKED),
                ]
            )
        tops = []
        for k in range(group):
            top = jnp.maximum(jnp.maximum(far[k][0], far[k][1]), near[k])
            top = jnp.max(jnp.maximum(top[:BLOCK], top[BLOCK:]), axis=1, keepdims=True)
            tops.append(jnp.concatenate([top, top], axis=0))
        far = [[jnp.exp2((part - tops[k]) * SCALE) for part in far[k]] for k in range(group)]
        near = [jnp.exp2((near[k] - tops[k]) * SCALE) for k in range(group)]
        summed = []
        for quad in range(group // 4):
            four = own_values[source, pl.ds(first + 4 * quad, 4)].reshape(LANES, LANES)
            weights = [near[4 * quad + j].astype(BF16) for j in range(4)]
            product = jnp.dot(
                jnp.concatenate(weights, axis=0), four, preferred_element_type=F32
            )
            summed += [product[j * rows : (j + 1) * rows] for j in range(4)]
        for k in range(group):
            far_values = jnp.concatenate([values[slot] for slot in slots[k]], axis=0)
            weights = jnp.concatenate([part.astype(BF16) for part in far[k]], axis=1)
            summed[k] = summed[k] + jnp.dot(weights, far_values, preferred_element_type=F32)
        for k in range(group):
            total = far[k][0] + far[k][1] + near[k]
            total = jnp.sum(total[:BLOCK] + total[BLOCK:], axis=1, keepdims=True)
            share = 1.0 / total
            share = jnp.where(low, share[:HALF], share[HALF:])
            straight = jnp.where(low, summed[k][:HALF], summed[k][3 * HALF :])
            crossed = jnp.where(low, summed[k][HALF : 2 * HALF], summed[k][2 * HALF : 3 * HALF])
            result = (straight + pltpu.roll(crossed, HDIM, 1)) * share
            made[source, first + k] = result.astype(BF16)
        for step in range(CHIPS):

            @pl.when(jnp.logical_and(at % 2 == 1, ahead == step))
            def _():
                pltpu.make_async_copy(made.at[source], targets[step], done.at[step]).start()

        return carry

    lax.fori_loop(0, CHIPS * OWN // group, attend_group, 0)
    if carried:
        passing = []
        for step in range(CHIPS):
            taking[step].wait()
            passing.append(
                pltpu.make_async_copy(before.at[step], outs[step].at[0], passed.at[step])
            )
            passing[-1].start()
        for copy in passing:
            copy.wait()
    for step in range(CHIPS):
        source = lax.rem(z + step, CHIPS)
        pltpu.make_async_copy(made.at[source], targets[step], done.at[step]).wait()


def attend(tables, place, queries, own, swapped, mine, other, chunk, before=()):
    slots = mine.shape[0]
    blocks = pltpu.VMEM((CHIPS, OWN) + TILE, BF16)
    return pl.pallas_call(
        functools.partial(attend_kernel, chunk, len(before)),
        in_specs=[SMEM] * 4 + [HBM] * (CHIPS + 4 + len(before)),
        out_specs=[HBM] * CHIPS,
        out_shape=[jax.ShapeDtypeStruct((2,) * (len(before) > 0) + (OWN,) + TILE, BF16)] * CHIPS,
        scratch_shapes=[
            blocks,
            blocks,
            pltpu.VMEM((slots,) + TILE, BF16),
            pltpu.VMEM((slots,) + TILE, BF16),
            blocks,
            blocks,
            pltpu.SemaphoreType.DMA((CHIPS,)),
            pltpu.SemaphoreType.DMA((4,)),
            pltpu.SemaphoreType.DMA((CHIPS,)),
        ]
        + [blocks, pltpu.SemaphoreType.DMA((CHIPS,)), pltpu.SemaphoreType.DMA((CHIPS,))]
        * (len(before) > 0),
        compiler_params=params(0),
        cost_estimate=pl.CostEstimate(
            flops=64 * 4 * 128 * 128 * 384, bytes_accessed=8 << 20, transcendentals=64 * 128 * 384
        ),
        name="attend",
    )(*tables, place, *queries, own, swapped, mine, other, *before)


def normed(values, gain):
    center = values - jnp.mean(values, axis=-1, keepdims=True)
    spread = jnp.mean(center * center, axis=-1, keepdims=True)
    return center * lax.rsqrt(spread + 1e-05) * gain


def mixed_rows(held, half, weight):
    at = slice(half * 8, half * 8 + 8)
    pieces = [unpack_pair(held[2 * pair, at], held[2 * pair + 1, at]) for pair in range(2)]
    return jnp.dot(jnp.concatenate(pieces, axis=1), weight, preferred_element_type=F32)


def gather_parts(place_ref, parts, held, sems):
    copies = []
    for step in range(CHIPS):
        source = lax.rem(place_ref[0] + CHIPS - step, CHIPS)
        copies.append(pltpu.make_async_copy(parts[step], held.at[source], sems.at[step]))
        copies[-1].start()
    return copies


def gains_kernel(attn_ref, ffn_ref, out_ref):
    out_ref[0, :] = attn_ref[...]
    out_ref[1, :] = ffn_ref[...]


def stack_gains(gain_attn, gain_ffn):
    return pl.pallas_call(
        gains_kernel,
        in_specs=[VMEM, VMEM],
        out_specs=VMEM,
        out_shape=jax.ShapeDtypeStruct((2,) + gain_attn.shape, F32),
        compiler_params=params(0),
        name="gains",
    )(gain_attn, gain_ffn)


def mix_kernel(place_ref, feat_ref, *refs):
    parts, (weight_ref, out_ref, *scratch) = refs[:CHIPS], refs[CHIPS:]
    held, feats, weight, made, arrive, sems = scratch
    rows = feat_ref.shape[0] // 2
    arriving = []
    for which in range(CHUNKS - 1):
        some = [part.at[which] for part in parts]
        arriving += gather_parts(place_ref, some, held.at[which], arrive.at[which])
    fetches = [
        pltpu.make_async_copy(weight_ref.at[: (CHUNKS - 1) * COLS], weight, sems.at[0]),
        pltpu.make_async_copy(feat_ref, feats, sems.at[1]),
    ]
    for copy in fetches:
        copy.start()
    for copy in arriving + fetches:
        copy.wait()
    copies = []
    for half in range(2):
        at = slice(half * rows, (half + 1) * rows)
        mixed = feats[at, :].astype(F32)
        for which in range(CHUNKS - 1):
            part = weight[which * COLS : (which + 1) * COLS, :]
            mixed = mixed + mixed_rows(held.at[which], half, part)
        made[at, :] = mixed
        copies.append(pltpu.make_async_copy(made.at[at], out_ref.at[at], sems.at[2 + half]))
        copies[-1].start()
    for copy in copies:
        copy.wait()


def mix(place, features, back, w_out):
    rows, width = features.shape
    early = (CHUNKS - 1) * COLS
    return pl.pallas_call(
        mix_kernel,
        in_specs=[SMEM] + [HBM] * (CHIPS + 2),
        out_specs=HBM,
        out_shape=jax.ShapeDtypeStruct((rows, width), F32),
        scratch_shapes=[
            pltpu.VMEM((CHUNKS - 1, CHIPS, OWN) + TILE, BF16),
            pltpu.VMEM((rows, width), BF16),
            pltpu.VMEM((early, width), BF16),
            pltpu.VMEM((rows, width), F32),
            pltpu.SemaphoreType.DMA((CHUNKS - 1, CHIPS)),
            pltpu.SemaphoreType.DMA((4,)),
        ],
        compiler_params=params(0),
        cost_estimate=pl.CostEstimate(
            flops=2 * rows * early * width, bytes_accessed=7 << 20, transcendentals=0
        ),
        name="mix",
    )(place, features, *back, w_out)


def finish_kernel(place_ref, mixed_ref, *refs):
    parts, refs = refs[:CHIPS], refs[CHIPS:]
    out_w_ref, up_ref, down_ref, gain_ref, result_ref, *scratch = refs
    held, early, out_w, up, down, made, arrive, sems = scratch
    rows = mixed_ref.shape[0] // 2
    halves = [slice(half * rows, (half + 1) * rows) for half in range(2)]
    arriving = gather_parts(place_ref, parts, held, arrive)
    copies = [
        pltpu.make_async_copy(out_w_ref.at[(CHUNKS - 1) * COLS :], out_w, sems.at[0]),
        pltpu.make_async_copy(mixed_ref.at[halves[0]], early.at[halves[0]], sems.at[1]),
        pltpu.make_async_copy(mixed_ref.at[halves[1]], early.at[halves[1]], sems.at[2]),
        pltpu.make_async_copy(up_ref, up, sems.at[3]),
        pltpu.make_async_copy(down_ref, down, sems.at[4]),
    ]
    for copy in copies:
        copy.start()
    for copy in arriving:
        copy.wait()
    copies[0].wait()
    firsts = []
    for half, at in enumerate(halves):
        added = mixed_rows(held, half, out_w[...])
        copies[1 + half].wait()
        firsts.append(normed(early[at, :] + added, gain_ref[0:1, :]).astype(BF16))
    rows = rows // 2
    firsts = [first[at : at + rows] for first in firsts for at in (0, rows)]
    for half, first in enumerate(firsts):
        at = slice(half * rows, (half + 1) * rows)
        if half == 0:
            copies[3].wait()
        hidden = jnp.maximum(jnp.dot(first, up[...], preferred_element_type=F32), 0.0).astype(BF16)
        if half == 0:
            copies[4].wait()
        total = first.astype(F32) + jnp.dot(hidden, down[...], preferred_element_type=F32)
        made[at, :] = normed(total, gain_ref[1:2, :]).astype(BF16)
        copies.append(pltpu.make_async_copy(made.at[at], result_ref.at[at], sems.at[5 + half]))
        copies[-1].start()
    for copy in copies[5:]:
        copy.wait()


def finish(place, mixed, back, w_out, w_up, w_down, gains):
    rows, width = mixed.shape
    return pl.pallas_call(
        finish_kernel,
        in_specs=[SMEM] + [HBM] * (CHIPS + 4) + [VMEM],
        out_specs=HBM,
        out_shape=jax.ShapeDtypeStruct((rows, width), BF16),
        scratch_shapes=[
            pltpu.VMEM((CHIPS, OWN) + TILE, BF16),
            pltpu.VMEM((rows, width), F32),
            pltpu.VMEM((COLS, width), BF16),
            pltpu.VMEM(w_up.shape, BF16),
            pltpu.VMEM(w_down.shape, BF16),
            pltpu.VMEM((rows, width), BF16),
            pltpu.SemaphoreType.DMA((CHIPS,)),
            pltpu.SemaphoreType.DMA((9,)),
        ],
        compiler_params=params(0),
        name="finish",
    )(place, mixed, *back, w_out, w_up, w_down, gains)


def swap(array):
    return lax.ppermute(array, "head", [(i, i ^ 1) for i in range(2 * CHIPS)])


def along_z(parts):
    moved = list(parts)
    for step in (2, 1, 3):
        moved[step] = lax.ppermute(
            parts[step], "head", [(i, (i + 2 * step) % (2 * CHIPS)) for i in range(2 * CHIPS)]
        )
    return moved


def per_device(
    features, w_query, w_key, w_value, w_out, w_up, w_down, gain_attn, gain_ffn,
    send_list, edge_owner, edge_slot, edge_count,
):
    head = lax.axis_index("head").astype(jnp.int32)
    place = jnp.stack([head // 2, head % 2])
    groups = send_list.shape[1]
    owners, slots = edge_owner.T, edge_slot.T
    far = swap(features)
    collected = []
    for c in range(CHUNKS):
        if c == 0:
            whole = project_first(features, w_key, w_value)
            whole = lax.all_to_all(whole, "head", split_axis=0, concat_axis=0, tiled=True)
            parts = [whole.reshape((-1,) + TILE)]
        else:
            parts = project_keys_values(place, features, far, w_key, w_value, c)
            parts = along_z(parts)
        collected.append(collect(send_list, place, parts))
    queries = along_z(project_queries(place, features, w_query))
    mines = []
    for c in range(CHUNKS):
        sent = collected[c][0].reshape((groups, CAP) + TILE)
        got = lax.all_to_all(sent, "node", split_axis=0, concat_axis=0, tiled=True)
        mines.append(got.reshape((groups * CAP,) + TILE))
    backs = []
    for c in range(CHUNKS):
        swapped = swap(collected[c][2])
        other = swap(mines[c])
        tables = (owners, slots, edge_count)
        before = done if c == 1 else ()
        done = attend(tables, place, queries, collected[c][1], swapped, mines[c], other, c, before)
        if c > 0:
            backs.append(along_z(done))
    gains = stack_gains(gain_attn, gain_ffn)
    mixed = mix(place, features, backs[0], w_out)
    return finish(place, mixed, backs[1], w_out, w_up, w_down, gains)


def solution(mesh):
    return jax.shard_map(
        per_device,
        mesh=mesh,
        in_specs=(
            P(("node", "head"), None),
            P(), P(), P(), P(), P(), P(), P(), P(),
            P("node", None, None),
            P("node", None),
            P("node", None),
            P("node"),
        ),
        out_specs=P(("node", "head"), None),
        check_vma=False,
    )
```

```python
import functools
import math

import jax
import jax.numpy as jnp
from jax import lax
from jax.experimental import pallas as pl
from jax.experimental.pallas import tpu as pltpu
from jax.sharding import PartitionSpec as P


HDIM = 64
BLOCK = 64
MAXK = 8
CAP = 16
HALF = BLOCK // 2
LANES = 2 * HDIM
CHUNKS = 3
CHIPS = 4
COLS = CHIPS * HDIM
OWN = 16
SCALE = 1.4426950408889634 / math.sqrt(HDIM)
MASKED = -8e30
F32 = jnp.float32
BF16 = jnp.bfloat16
VMEM = pl.BlockSpec(memory_space=pltpu.VMEM)
SMEM = pl.BlockSpec(memory_space=pltpu.SMEM)
HBM = pl.BlockSpec(memory_space=pltpu.HBM)
TILE = (HALF, LANES)


def low_lanes(rows):
    return lax.broadcasted_iota(jnp.int32, (rows, LANES), 1) < HDIM


def pack_pair(both):
    blocks = both.shape[0] // BLOCK
    split = both.reshape(blocks, 2, HALF, LANES)
    first = split[:, 0].reshape(blocks * HALF, LANES)
    second = split[:, 1].reshape(blocks * HALF, LANES)
    low = low_lanes(blocks * HALF)
    even = jnp.where(low, first, pltpu.roll(second, HDIM, 1))
    odd = jnp.where(low, pltpu.roll(first, HDIM, 1), second)
    return [part.reshape(blocks, HALF, LANES).astype(BF16) for part in (even, odd)]


def unpack_pair(even, odd):
    blocks = even.shape[0]
    even = even.reshape(blocks * HALF, LANES).astype(F32)
    odd = odd.reshape(blocks * HALF, LANES).astype(F32)
    low = low_lanes(blocks * HALF)
    first = jnp.where(low, even, pltpu.roll(odd, HDIM, 1)).reshape(blocks, 1, HALF, LANES)
    second = jnp.where(low, pltpu.roll(even, HDIM, 1), odd).reshape(blocks, 1, HALF, LANES)
    return jnp.concatenate([first, second], axis=1).reshape(blocks * BLOCK, LANES).astype(BF16)


def params(room):
    return pltpu.CompilerParams(vmem_limit_bytes=67_043_328 - room)


def fetch_weight(chunk, core, key_ref, value_ref, weight, sem):
    def fetch(source):
        copy = pltpu.make_async_copy(source.at[:, chunk * COLS : (chunk + 1) * COLS], weight, sem)
        copy.start()
        copy.wait()

    @pl.when(core == 0)
    def _():
        fetch(key_ref)

    @pl.when(core == 1)
    def _():
        fetch(value_ref)


def pack_rows(feat_ref, weight, packed, first):
    for half in range(2):
        made = jnp.dot(
            feat_ref[half * 512 : half * 512 + 512, :], weight[...], preferred_element_type=F32
        )
        for pair in range(2):
            both = pack_pair(made[:, pair * LANES : (pair + 1) * LANES])
            for side in range(2):
                packed[2 * pair + side, pl.ds(first + half * 8, 8)] = both[side]


def first_kernel(feat_ref, key_ref, value_ref, *refs):
    out_ref, feats, weights, made, sems, done = refs
    halves = [slice(half * 512, half * 512 + 512) for half in range(2)]
    fetches = [
        pltpu.make_async_copy(key_ref.at[:, :COLS], weights.at[0], sems.at[0]),
        pltpu.make_async_copy(feat_ref.at[halves[0]], feats.at[halves[0]], sems.at[1]),
        pltpu.make_async_copy(feat_ref.at[halves[1]], feats.at[halves[1]], sems.at[2]),
        pltpu.make_async_copy(value_ref.at[:, :COLS], weights.at[1], sems.at[3]),
    ]
    for copy in fetches:
        copy.start()
    copies = []
    fetches[0].wait()
    for kind in range(2):
        if kind == 1:
            fetches[3].wait()
        for half, at in enumerate(halves):
            if kind == 0:
                fetches[1 + half].wait()
            rows = jnp.dot(feats[at, :], weights[kind], preferred_element_type=F32)
            for pair in range(2):
                both = pack_pair(rows[:, pair * LANES : (pair + 1) * LANES])
                for side in range(2):
                    dest = 2 * (2 * pair + side) + kind
                    made[dest, half * 8 : half * 8 + 8] = both[side]
        for z in range(CHIPS):
            dest = 2 * z + kind
            copies.append(pltpu.make_async_copy(made.at[dest], out_ref.at[dest], done.at[dest]))
            copies[-1].start()
    for copy in copies:
        copy.wait()


def project_first(features, w_key, w_value):
    rows, width = features.shape
    return pl.pallas_call(
        first_kernel,
        in_specs=[HBM] * 3,
        out_specs=HBM,
        out_shape=jax.ShapeDtypeStruct((2 * CHIPS, OWN) + TILE, BF16),
        scratch_shapes=[
            pltpu.VMEM((rows, width), BF16),
            pltpu.VMEM((2, width, COLS), BF16),
            pltpu.VMEM((2 * CHIPS, OWN) + TILE, BF16),
            pltpu.SemaphoreType.DMA((4,)),
            pltpu.SemaphoreType.DMA((2 * CHIPS,)),
        ],
        compiler_params=params(0),
        cost_estimate=pl.CostEstimate(
            flops=4 * rows * width * COLS, bytes_accessed=4 << 20, transcendentals=0
        ),
        name="first_keys_values",
    )(features, w_key, w_value)


def keys_values_kernel(chunk, place_ref, near_ref, far_ref, key_ref, value_ref, *refs):
    outs, (weight, packed, sem) = refs[:CHIPS], refs[CHIPS:]
    z, core = place_ref[0], place_ref[1]
    fetch_weight(chunk, core, key_ref, value_ref, weight, sem)
    pack_rows(near_ref, weight, packed, core * OWN)
    pack_rows(far_ref, weight, packed, (1 - core) * OWN)
    for step in range(CHIPS):
        outs[step][...] = packed[lax.rem(z + step, CHIPS)]


def project_keys_values(place, near, far, w_key, w_value, chunk):
    rows, width = near.shape
    return pl.pallas_call(
        functools.partial(keys_values_kernel, chunk),
        in_specs=[SMEM, VMEM, VMEM, HBM, HBM],
        out_specs=[VMEM] * CHIPS,
        out_shape=[jax.ShapeDtypeStruct((2 * OWN,) + TILE, BF16)] * CHIPS,
        scratch_shapes=[
            pltpu.VMEM((width, COLS), BF16),
            pltpu.VMEM((CHIPS, 2 * OWN) + TILE, BF16),
            pltpu.SemaphoreType.DMA,
        ],
        compiler_params=params(0),
        cost_estimate=pl.CostEstimate(
            flops=4 * rows * width * COLS, bytes_accessed=5 << 20, transcendentals=0
        ),
        name="keys_values",
    )(place, near, far, w_key, w_value)


def queries_kernel(place_ref, feat_ref, query_ref, *refs):
    outs, (packed,) = refs[:CHIPS], refs[CHIPS:]
    z = place_ref[0]
    for chunk in range(CHUNKS):
        for half in range(2):
            made = jnp.dot(
                feat_ref[half * 512 : half * 512 + 512, :],
                query_ref[:, chunk * COLS : (chunk + 1) * COLS],
                preferred_element_type=F32,
            )
            for pair in range(2):
                both = pack_pair(made[:, pair * LANES : (pair + 1) * LANES])
                for side in range(2):
                    packed[2 * pair + side, chunk, half * 8 : half * 8 + 8] = both[side]
    for step in range(CHIPS):
        outs[step][...] = packed[lax.rem(z + step, CHIPS)]


def project_queries(place, features, w_query):
    rows, width = features.shape
    return pl.pallas_call(
        queries_kernel,
        in_specs=[SMEM, VMEM, VMEM],
        out_specs=[VMEM] * CHIPS,
        out_shape=[jax.ShapeDtypeStruct((CHUNKS, OWN) + TILE, BF16)] * CHIPS,
        scratch_shapes=[pltpu.VMEM((CHIPS, CHUNKS, OWN) + TILE, BF16)],
        compiler_params=params(0),
        cost_estimate=pl.CostEstimate(
            flops=2 * rows * width * width, bytes_accessed=5 << 20, transcendentals=0
        ),
        name="queries",
    )(place, features, w_query)


def collect_kernel(count, list_ref, place_ref, *refs):
    parts, (out_ref, own_ref, swap_ref, *scratch) = refs[:count], refs[count:]
    z, core = place_ref[0], place_ref[1]
    if count == 1:
        held, (picked, sems) = parts[0], scratch
    else:
        held, picked, sems = scratch
        for step in range(CHIPS):
            source = lax.rem(z + CHIPS - step, CHIPS)
            held[pl.ds(source * 2 * OWN, 2 * OWN)] = parts[step][...]
    quarter = picked.shape[0] // CAP // 4

    def body(step, carry):
        for extra in range(CAP):
            picked[step * CAP + extra] = held[list_ref[0, step, extra]]
        return carry

    copies = []
    for part in range(4):
        lax.fori_loop(part * quarter, (part + 1) * quarter, body, 0)
        at = pl.ds(part * quarter * CAP, quarter * CAP)
        copies.append(pltpu.make_async_copy(picked.at[at], out_ref.at[at], sems.at[part]))
        copies[-1].start()
    for source in range(CHIPS):
        for which, target in enumerate((own_ref, swap_ref)):
            side = core if which == 0 else 1 - core
            at = pl.ds(source * 2 * OWN + side * OWN, OWN)
            copies.append(
                pltpu.make_async_copy(
                    held.at[at], target.at[source], sems.at[4 + 2 * source + which]
                )
            )
            copies[-1].start()
    for copy in copies:
        copy.wait()


def collect(send_list, place, parts):
    slots = send_list.shape[1] * send_list.shape[2]
    own = jax.ShapeDtypeStruct((CHIPS, OWN) + TILE, BF16)
    return pl.pallas_call(
        functools.partial(collect_kernel, len(parts)),
        in_specs=[SMEM, SMEM] + [VMEM] * len(parts),
        out_specs=[HBM] * 3,
        out_shape=[jax.ShapeDtypeStruct((slots,) + TILE, BF16), own, own],
        scratch_shapes=[pltpu.VMEM((CHIPS * 2 * OWN,) + TILE, BF16)] * (len(parts) > 1)
        + [pltpu.VMEM((slots,) + TILE, BF16), pltpu.SemaphoreType.DMA((4 + 2 * CHIPS,))],
        compiler_params=params(0),
        cost_estimate=pl.CostEstimate(flops=0, bytes_accessed=5 << 20, transcendentals=0),
        name="collect",
    )(send_list, place, *parts)


def attend_kernel(chunk, carried, owner_ref, slot_ref, count_ref, place_ref, *refs):
    parts, (own_ref, swap_ref, mine_ref, other_ref) = refs[:CHIPS], refs[CHIPS : CHIPS + 4]
    befores, refs = refs[CHIPS + 4 : CHIPS + 4 + carried], refs[CHIPS + 4 + carried :]
    outs, refs = refs[:CHIPS], refs[CHIPS:]
    queries, made, keys, values, own_keys, own_values, asked, sems, done = refs[:9]
    z, core = place_ref[0], place_ref[1]

    asking = []
    for step in range(CHIPS):
        source = lax.rem(z + CHIPS - step, CHIPS)
        asking.append(
            pltpu.make_async_copy(parts[step].at[chunk], queries.at[source], asked.at[step])
        )
        asking[-1].start()

    def place_in(near, near_own, far, far_own):
        copies = [
            pltpu.make_async_copy(mine_ref, near, sems.at[0]),
            pltpu.make_async_copy(other_ref, far, sems.at[1]),
            pltpu.make_async_copy(own_ref, near_own, sems.at[2]),
            pltpu.make_async_copy(swap_ref, far_own, sems.at[3]),
        ]
        for copy in copies:
            copy.start()
        for copy in copies:
            copy.wait()

    @pl.when(core == 0)
    def _():
        place_in(keys, own_keys, values, own_values)

    @pl.when(core == 1)
    def _():
        place_in(values, own_values, keys, own_keys)

    for copy in asking:
        copy.wait()
    targets = outs
    if carried:
        before, taken, passed = refs[9:]
        taking = []
        for step in range(CHIPS):
            taking.append(
                pltpu.make_async_copy(befores[step], before.at[step], taken.at[step])
            )
            taking[-1].start()
        targets = [out.at[1] for out in outs]

    low = low_lanes(HALF)
    lane = lax.broadcasted_iota(jnp.int32, (1, LANES), 1)
    dims = (((1,), (1,)), ((), ()))
    rows = 2 * BLOCK
    group = OWN

    def attend_group(at, carry):
        ahead = lax.rem(at + 1, CHIPS)
        source, first = lax.rem(z + ahead, CHIPS), 0
        blocks = [source * 2 * OWN + core * OWN + first + k for k in range(group)]
        slots = [
            [owner_ref[entry, block] * CAP + slot_ref[entry, block] for entry in range(MAXK)]
            for block in blocks
        ]
        left = []
        for k in range(group):
            query = queries[source, first + k].astype(F32)
            turned = pltpu.roll(query, HDIM, 1)
            zero = jnp.zeros_like(query)
            left.append(
                jnp.concatenate(
                    [
                        jnp.where(low, query, zero),
                        jnp.where(low, turned, zero),
                        jnp.where(low, zero, turned),
                        jnp.where(low, zero, query),
                    ],
                    axis=0,
                ).astype(BF16)
            )
        near = []
        for quad in range(group // 4):
            four = own_keys[source, pl.ds(first + 4 * quad, 4)].reshape(LANES, LANES)
            scores = lax.dot_general(
                jnp.concatenate(left[4 * quad : 4 * quad + 4], axis=0),
                four,
                dims,
                preferred_element_type=F32,
            )
            for j in range(4):
                near.append(
                    jnp.where(lane // HALF == j, scores[j * rows : (j + 1) * rows], MASKED)
                )
        far = []
        for k in range(group):
            far_keys = jnp.concatenate([keys[slot] for slot in slots[k]], axis=0)
            scores = lax.dot_general(left[k], far_keys, dims, preferred_element_type=F32)
            limit = count_ref[blocks[k]] * HALF
            far.append(
                [
                    jnp.where(lane < limit, scores[:, :LANES], MASKED),
                    jnp.where(lane + LANES < limit, scores[:, LANES:], MASKED),
                ]
            )
        tops = []
        for k in range(group):
            top = jnp.maximum(jnp.maximum(far[k][0], far[k][1]), near[k])
            top = jnp.max(jnp.maximum(top[:BLOCK], top[BLOCK:]), axis=1, keepdims=True)
            tops.append(jnp.concatenate([top, top], axis=0))
        far = [[jnp.exp2((part - tops[k]) * SCALE) for part in far[k]] for k in range(group)]
        near = [jnp.exp2((near[k] - tops[k]) * SCALE) for k in range(group)]
        summed = []
        for quad in range(group // 4):
            four = own_values[source, pl.ds(first + 4 * quad, 4)].reshape(LANES, LANES)
            weights = [near[4 * quad + j].astype(BF16) for j in range(4)]
            product = jnp.dot(
                jnp.concatenate(weights, axis=0), four, preferred_element_type=F32
            )
            summed += [product[j * rows : (j + 1) * rows] for j in range(4)]
        for k in range(group):
            far_values = jnp.concatenate([values[slot] for slot in slots[k]], axis=0)
            weights = jnp.concatenate([part.astype(BF16) for part in far[k]], axis=1)
            summed[k] = summed[k] + jnp.dot(weights, far_values, preferred_element_type=F32)
        for k in range(group):
            total = far[k][0] + far[k][1] + near[k]
            total = jnp.sum(total[:BLOCK] + total[BLOCK:], axis=1, keepdims=True)
            share = 1.0 / total
            share = jnp.where(low, share[:HALF], share[HALF:])
            straight = jnp.where(low, summed[k][:HALF], summed[k][3 * HALF :])
            crossed = jnp.where(low, summed[k][HALF : 2 * HALF], summed[k][2 * HALF : 3 * HALF])
            result = (straight + pltpu.roll(crossed, HDIM, 1)) * share
            made[source, first + k] = result.astype(BF16)
        for step in range(CHIPS):

            @pl.when(ahead == step)
            def _():
                pltpu.make_async_copy(made.at[source], targets[step], done.at[step]).start()

        return carry

    lax.fori_loop(0, CHIPS * OWN // group, attend_group, 0)
    if carried:
        passing = []
        for step in range(CHIPS):
            taking[step].wait()
            passing.append(
                pltpu.make_async_copy(before.at[step], outs[step].at[0], passed.at[step])
            )
            passing[-1].start()
        for copy in passing:
            copy.wait()
    for step in range(CHIPS):
        source = lax.rem(z + step, CHIPS)
        pltpu.make_async_copy(made.at[source], targets[step], done.at[step]).wait()


def attend(tables, place, queries, own, swapped, mine, other, chunk, before=()):
    slots = mine.shape[0]
    blocks = pltpu.VMEM((CHIPS, OWN) + TILE, BF16)
    return pl.pallas_call(
        functools.partial(attend_kernel, chunk, len(before)),
        in_specs=[SMEM] * 4 + [HBM] * (CHIPS + 4 + len(before)),
        out_specs=[HBM] * CHIPS,
        out_shape=[jax.ShapeDtypeStruct((2,) * (len(before) > 0) + (OWN,) + TILE, BF16)] * CHIPS,
        scratch_shapes=[
            blocks,
            blocks,
            pltpu.VMEM((slots,) + TILE, BF16),
            pltpu.VMEM((slots,) + TILE, BF16),
            blocks,
            blocks,
            pltpu.SemaphoreType.DMA((CHIPS,)),
            pltpu.SemaphoreType.DMA((4,)),
            pltpu.SemaphoreType.DMA((CHIPS,)),
        ]
        + [blocks, pltpu.SemaphoreType.DMA((CHIPS,)), pltpu.SemaphoreType.DMA((CHIPS,))]
        * (len(before) > 0),
        compiler_params=params(0),
        cost_estimate=pl.CostEstimate(
            flops=64 * 4 * 128 * 128 * 384, bytes_accessed=8 << 20, transcendentals=64 * 128 * 384
        ),
        name="attend",
    )(*tables, place, *queries, own, swapped, mine, other, *before)


def normed(values, gain):
    center = values - jnp.mean(values, axis=-1, keepdims=True)
    spread = jnp.mean(center * center, axis=-1, keepdims=True)
    return center * lax.rsqrt(spread + 1e-05) * gain


def mixed_rows(held, half, weight):
    at = slice(half * 8, half * 8 + 8)
    pieces = [unpack_pair(held[2 * pair, at], held[2 * pair + 1, at]) for pair in range(2)]
    return jnp.dot(jnp.concatenate(pieces, axis=1), weight, preferred_element_type=F32)


def gather_parts(place_ref, parts, held, sems):
    copies = []
    for step in range(CHIPS):
        source = lax.rem(place_ref[0] + CHIPS - step, CHIPS)
        copies.append(pltpu.make_async_copy(parts[step], held.at[source], sems.at[step]))
        copies[-1].start()
    return copies


def gains_kernel(attn_ref, ffn_ref, out_ref):
    out_ref[0, :] = attn_ref[...]
    out_ref[1, :] = ffn_ref[...]


def stack_gains(gain_attn, gain_ffn):
    return pl.pallas_call(
        gains_kernel,
        in_specs=[VMEM, VMEM],
        out_specs=VMEM,
        out_shape=jax.ShapeDtypeStruct((2,) + gain_attn.shape, F32),
        compiler_params=params(0),
        name="gains",
    )(gain_attn, gain_ffn)


def mix_kernel(place_ref, feat_ref, *refs):
    parts, (weight_ref, out_ref, *scratch) = refs[:CHIPS], refs[CHIPS:]
    held, feats, weight, made, arrive, sems = scratch
    rows = feat_ref.shape[0] // 2
    arriving = []
    for which in range(CHUNKS - 1):
        some = [part.at[which] for part in parts]
        arriving += gather_parts(place_ref, some, held.at[which], arrive.at[which])
    fetches = [
        pltpu.make_async_copy(weight_ref.at[: (CHUNKS - 1) * COLS], weight, sems.at[0]),
        pltpu.make_async_copy(feat_ref, feats, sems.at[1]),
    ]
    for copy in fetches:
        copy.start()
    for copy in arriving + fetches:
        copy.wait()
    copies = []
    for half in range(2):
        at = slice(half * rows, (half + 1) * rows)
        mixed = feats[at, :].astype(F32)
        for which in range(CHUNKS - 1):
            part = weight[which * COLS : (which + 1) * COLS, :]
            mixed = mixed + mixed_rows(held.at[which], half, part)
        made[at, :] = mixed
        copies.append(pltpu.make_async_copy(made.at[at], out_ref.at[at], sems.at[2 + half]))
        copies[-1].start()
    for copy in copies:
        copy.wait()


def mix(place, features, back, w_out):
    rows, width = features.shape
    early = (CHUNKS - 1) * COLS
    return pl.pallas_call(
        mix_kernel,
        in_specs=[SMEM] + [HBM] * (CHIPS + 2),
        out_specs=HBM,
        out_shape=jax.ShapeDtypeStruct((rows, width), F32),
        scratch_shapes=[
            pltpu.VMEM((CHUNKS - 1, CHIPS, OWN) + TILE, BF16),
            pltpu.VMEM((rows, width), BF16),
            pltpu.VMEM((early, width), BF16),
            pltpu.VMEM((rows, width), F32),
            pltpu.SemaphoreType.DMA((CHUNKS - 1, CHIPS)),
            pltpu.SemaphoreType.DMA((4,)),
        ],
        compiler_params=params(0),
        cost_estimate=pl.CostEstimate(
            flops=2 * rows * early * width, bytes_accessed=7 << 20, transcendentals=0
        ),
        name="mix",
    )(place, features, *back, w_out)


def finish_kernel(place_ref, mixed_ref, *refs):
    parts, refs = refs[:CHIPS], refs[CHIPS:]
    out_w_ref, up_ref, down_ref, gain_ref, result_ref, *scratch = refs
    held, early, out_w, up, down, made, arrive, sems = scratch
    rows = mixed_ref.shape[0] // 2
    halves = [slice(half * rows, (half + 1) * rows) for half in range(2)]
    arriving = gather_parts(place_ref, parts, held, arrive)
    copies = [
        pltpu.make_async_copy(out_w_ref.at[(CHUNKS - 1) * COLS :], out_w, sems.at[0]),
        pltpu.make_async_copy(mixed_ref.at[halves[0]], early.at[halves[0]], sems.at[1]),
        pltpu.make_async_copy(mixed_ref.at[halves[1]], early.at[halves[1]], sems.at[2]),
        pltpu.make_async_copy(up_ref, up, sems.at[3]),
        pltpu.make_async_copy(down_ref, down, sems.at[4]),
    ]
    for copy in copies:
        copy.start()
    for copy in arriving:
        copy.wait()
    copies[0].wait()
    firsts = []
    for half, at in enumerate(halves):
        added = mixed_rows(held, half, out_w[...])
        copies[1 + half].wait()
        firsts.append(normed(early[at, :] + added, gain_ref[0:1, :]).astype(BF16))
    rows = rows // 2
    firsts = [first[at : at + rows] for first in firsts for at in (0, rows)]
    for half, first in enumerate(firsts):
        at = slice(half * rows, (half + 1) * rows)
        if half == 0:
            copies[3].wait()
        hidden = jnp.maximum(jnp.dot(first, up[...], preferred_element_type=F32), 0.0).astype(BF16)
        if half == 0:
            copies[4].wait()
        total = first.astype(F32) + jnp.dot(hidden, down[...], preferred_element_type=F32)
        made[at, :] = normed(total, gain_ref[1:2, :]).astype(BF16)
        copies.append(pltpu.make_async_copy(made.at[at], result_ref.at[at], sems.at[5 + half]))
        copies[-1].start()
    for copy in copies[5:]:
        copy.wait()


def finish(place, mixed, back, w_out, w_up, w_down, gains):
    rows, width = mixed.shape
    return pl.pallas_call(
        finish_kernel,
        in_specs=[SMEM] + [HBM] * (CHIPS + 4) + [VMEM],
        out_specs=HBM,
        out_shape=jax.ShapeDtypeStruct((rows, width), BF16),
        scratch_shapes=[
            pltpu.VMEM((CHIPS, OWN) + TILE, BF16),
            pltpu.VMEM((rows, width), F32),
            pltpu.VMEM((COLS, width), BF16),
            pltpu.VMEM(w_up.shape, BF16),
            pltpu.VMEM(w_down.shape, BF16),
            pltpu.VMEM((rows, width), BF16),
            pltpu.SemaphoreType.DMA((CHIPS,)),
            pltpu.SemaphoreType.DMA((9,)),
        ],
        compiler_params=params(0),
        name="finish",
    )(place, mixed, *back, w_out, w_up, w_down, gains)


def swap(array):
    return lax.ppermute(array, "head", [(i, i ^ 1) for i in range(2 * CHIPS)])


def along_z(parts):
    moved = list(parts)
    for step in (2, 1, 3):
        moved[step] = lax.ppermute(
            parts[step], "head", [(i, (i + 2 * step) % (2 * CHIPS)) for i in range(2 * CHIPS)]
        )
    return moved


def per_device(
    features, w_query, w_key, w_value, w_out, w_up, w_down, gain_attn, gain_ffn,
    send_list, edge_owner, edge_slot, edge_count,
):
    head = lax.axis_index("head").astype(jnp.int32)
    place = jnp.stack([head // 2, head % 2])
    groups = send_list.shape[1]
    owners, slots = edge_owner.T, edge_slot.T
    far = swap(features)
    collected = []
    for c in range(CHUNKS):
        if c == 0:
            whole = project_first(features, w_key, w_value)
            whole = lax.all_to_all(whole, "head", split_axis=0, concat_axis=0, tiled=True)
            parts = [whole.reshape((-1,) + TILE)]
        else:
            parts = project_keys_values(place, features, far, w_key, w_value, c)
            parts = along_z(parts)
        collected.append(collect(send_list, place, parts))
    queries = along_z(project_queries(place, features, w_query))
    mines = []
    for c in range(CHUNKS):
        sent = collected[c][0].reshape((groups, CAP) + TILE)
        got = lax.all_to_all(sent, "node", split_axis=0, concat_axis=0, tiled=True)
        mines.append(got.reshape((groups * CAP,) + TILE))
    backs = []
    for c in range(CHUNKS):
        swapped = swap(collected[c][2])
        other = swap(mines[c])
        tables = (owners, slots, edge_count)
        before = done if c == 1 else ()
        done = attend(tables, place, queries, collected[c][1], swapped, mines[c], other, c, before)
        if c > 0:
            backs.append(along_z(done))
    gains = stack_gains(gain_attn, gain_ffn)
    mixed = mix(place, features, backs[0], w_out)
    return finish(place, mixed, backs[1], w_out, w_up, w_down, gains)


def solution(mesh):
    return jax.shard_map(
        per_device,
        mesh=mesh,
        in_specs=(
            P(("node", "head"), None),
            P(), P(), P(), P(), P(), P(), P(), P(),
            P("node", None, None),
            P("node", None),
            P("node", None),
            P("node"),
        ),
        out_specs=P(("node", "head"), None),
        check_vma=False,
    )
```

```python
import functools
import math

import jax
import jax.numpy as jnp
from jax import lax
from jax.experimental import pallas as pl
from jax.experimental.pallas import tpu as pltpu
from jax.sharding import PartitionSpec as P


HDIM = 64
BLOCK = 64
MAXK = 8
CAP = 16
HALF = BLOCK // 2
LANES = 2 * HDIM
CHUNKS = 3
CHIPS = 4
COLS = CHIPS * HDIM
OWN = 16
SCALE = 1.4426950408889634 / math.sqrt(HDIM)
MASKED = -8e30
F32 = jnp.float32
BF16 = jnp.bfloat16
VMEM = pl.BlockSpec(memory_space=pltpu.VMEM)
SMEM = pl.BlockSpec(memory_space=pltpu.SMEM)
HBM = pl.BlockSpec(memory_space=pltpu.HBM)
TILE = (HALF, LANES)


def low_lanes(rows):
    return lax.broadcasted_iota(jnp.int32, (rows, LANES), 1) < HDIM


def pack_pair(both):
    blocks = both.shape[0] // BLOCK
    split = both.reshape(blocks, 2, HALF, LANES)
    first = split[:, 0].reshape(blocks * HALF, LANES)
    second = split[:, 1].reshape(blocks * HALF, LANES)
    low = low_lanes(blocks * HALF)
    even = jnp.where(low, first, pltpu.roll(second, HDIM, 1))
    odd = jnp.where(low, pltpu.roll(first, HDIM, 1), second)
    return [part.reshape(blocks, HALF, LANES).astype(BF16) for part in (even, odd)]


def unpack_pair(even, odd):
    blocks = even.shape[0]
    even = even.reshape(blocks * HALF, LANES).astype(F32)
    odd = odd.reshape(blocks * HALF, LANES).astype(F32)
    low = low_lanes(blocks * HALF)
    first = jnp.where(low, even, pltpu.roll(odd, HDIM, 1)).reshape(blocks, 1, HALF, LANES)
    second = jnp.where(low, pltpu.roll(even, HDIM, 1), odd).reshape(blocks, 1, HALF, LANES)
    return jnp.concatenate([first, second], axis=1).reshape(blocks * BLOCK, LANES).astype(BF16)


def params(room):
    return pltpu.CompilerParams(vmem_limit_bytes=67_043_328 - room)


def fetch_weight(chunk, core, key_ref, value_ref, weight, sem):
    def fetch(source):
        copy = pltpu.make_async_copy(source.at[:, chunk * COLS : (chunk + 1) * COLS], weight, sem)
        copy.start()
        copy.wait()

    @pl.when(core == 0)
    def _():
        fetch(key_ref)

    @pl.when(core == 1)
    def _():
        fetch(value_ref)


def pack_rows(feat_ref, weight, packed, first):
    for half in range(2):
        made = jnp.dot(
            feat_ref[half * 512 : half * 512 + 512, :], weight[...], preferred_element_type=F32
        )
        for pair in range(2):
            both = pack_pair(made[:, pair * LANES : (pair + 1) * LANES])
            for side in range(2):
                packed[2 * pair + side, pl.ds(first + half * 8, 8)] = both[side]


def first_kernel(feat_ref, key_ref, value_ref, *refs):
    out_ref, feats, weights, made, sems, done = refs
    halves = [slice(half * 512, half * 512 + 512) for half in range(2)]
    fetches = [
        pltpu.make_async_copy(key_ref.at[:, :COLS], weights.at[0], sems.at[0]),
        pltpu.make_async_copy(feat_ref.at[halves[0]], feats.at[halves[0]], sems.at[1]),
        pltpu.make_async_copy(feat_ref.at[halves[1]], feats.at[halves[1]], sems.at[2]),
        pltpu.make_async_copy(value_ref.at[:, :COLS], weights.at[1], sems.at[3]),
    ]
    for copy in fetches:
        copy.start()
    copies = []
    fetches[0].wait()
    for kind in range(2):
        if kind == 1:
            fetches[3].wait()
        for half, at in enumerate(halves):
            if kind == 0:
                fetches[1 + half].wait()
            rows = jnp.dot(feats[at, :], weights[kind], preferred_element_type=F32)
            for pair in range(2):
                both = pack_pair(rows[:, pair * LANES : (pair + 1) * LANES])
                for side in range(2):
                    dest = 2 * (2 * pair + side) + kind
                    made[dest, half * 8 : half * 8 + 8] = both[side]
        for z in range(CHIPS):
            dest = 2 * z + kind
            copies.append(pltpu.make_async_copy(made.at[dest], out_ref.at[dest], done.at[dest]))
            copies[-1].start()
    for copy in copies:
        copy.wait()


def project_first(features, w_key, w_value):
    rows, width = features.shape
    return pl.pallas_call(
        first_kernel,
        in_specs=[HBM] * 3,
        out_specs=HBM,
        out_shape=jax.ShapeDtypeStruct((2 * CHIPS, OWN) + TILE, BF16),
        scratch_shapes=[
            pltpu.VMEM((rows, width), BF16),
            pltpu.VMEM((2, width, COLS), BF16),
            pltpu.VMEM((2 * CHIPS, OWN) + TILE, BF16),
            pltpu.SemaphoreType.DMA((4,)),
            pltpu.SemaphoreType.DMA((2 * CHIPS,)),
        ],
        compiler_params=params(0),
        cost_estimate=pl.CostEstimate(
            flops=4 * rows * width * COLS, bytes_accessed=4 << 20, transcendentals=0
        ),
        name="first_keys_values",
    )(features, w_key, w_value)


def keys_values_kernel(chunk, place_ref, near_ref, far_ref, key_ref, value_ref, *refs):
    outs, (weight, packed, sem) = refs[:CHIPS], refs[CHIPS:]
    z, core = place_ref[0], place_ref[1]
    fetch_weight(chunk, core, key_ref, value_ref, weight, sem)
    pack_rows(near_ref, weight, packed, core * OWN)
    pack_rows(far_ref, weight, packed, (1 - core) * OWN)
    for step in range(CHIPS):
        outs[step][...] = packed[lax.rem(z + step, CHIPS)]


def project_keys_values(place, near, far, w_key, w_value, chunk):
    rows, width = near.shape
    return pl.pallas_call(
        functools.partial(keys_values_kernel, chunk),
        in_specs=[SMEM, VMEM, VMEM, HBM, HBM],
        out_specs=[VMEM] * CHIPS,
        out_shape=[jax.ShapeDtypeStruct((2 * OWN,) + TILE, BF16)] * CHIPS,
        scratch_shapes=[
            pltpu.VMEM((width, COLS), BF16),
            pltpu.VMEM((CHIPS, 2 * OWN) + TILE, BF16),
            pltpu.SemaphoreType.DMA,
        ],
        compiler_params=params(0),
        cost_estimate=pl.CostEstimate(
            flops=4 * rows * width * COLS, bytes_accessed=5 << 20, transcendentals=0
        ),
        name="keys_values",
    )(place, near, far, w_key, w_value)


def queries_kernel(place_ref, feat_ref, query_ref, *refs):
    outs, (packed,) = refs[:CHIPS], refs[CHIPS:]
    z = place_ref[0]
    for chunk in range(CHUNKS):
        for half in range(2):
            made = jnp.dot(
                feat_ref[half * 512 : half * 512 + 512, :],
                query_ref[:, chunk * COLS : (chunk + 1) * COLS],
                preferred_element_type=F32,
            )
            for pair in range(2):
                both = pack_pair(made[:, pair * LANES : (pair + 1) * LANES])
                for side in range(2):
                    packed[2 * pair + side, chunk, half * 8 : half * 8 + 8] = both[side]
    for step in range(CHIPS):
        outs[step][...] = packed[lax.rem(z + step, CHIPS)]


def project_queries(place, features, w_query):
    rows, width = features.shape
    return pl.pallas_call(
        queries_kernel,
        in_specs=[SMEM, VMEM, VMEM],
        out_specs=[VMEM] * CHIPS,
        out_shape=[jax.ShapeDtypeStruct((CHUNKS, OWN) + TILE, BF16)] * CHIPS,
        scratch_shapes=[pltpu.VMEM((CHIPS, CHUNKS, OWN) + TILE, BF16)],
        compiler_params=params(0),
        cost_estimate=pl.CostEstimate(
            flops=2 * rows * width * width, bytes_accessed=5 << 20, transcendentals=0
        ),
        name="queries",
    )(place, features, w_query)


def collect_kernel(count, list_ref, place_ref, *refs):
    parts, (out_ref, own_ref, swap_ref, *scratch) = refs[:count], refs[count:]
    z, core = place_ref[0], place_ref[1]
    if count == 1:
        held, (picked, sems) = parts[0], scratch
    else:
        held, picked, sems = scratch
        for step in range(CHIPS):
            source = lax.rem(z + CHIPS - step, CHIPS)
            held[pl.ds(source * 2 * OWN, 2 * OWN)] = parts[step][...]
    quarter = picked.shape[0] // CAP // 4

    def body(step, carry):
        for extra in range(CAP):
            picked[step * CAP + extra] = held[list_ref[0, step, extra]]
        return carry

    copies = []
    for part in range(4):
        lax.fori_loop(part * quarter, (part + 1) * quarter, body, 0)
        at = pl.ds(part * quarter * CAP, quarter * CAP)
        copies.append(pltpu.make_async_copy(picked.at[at], out_ref.at[at], sems.at[part]))
        copies[-1].start()
    for source in range(CHIPS):
        for which, target in enumerate((own_ref, swap_ref)):
            side = core if which == 0 else 1 - core
            at = pl.ds(source * 2 * OWN + side * OWN, OWN)
            copies.append(
                pltpu.make_async_copy(
                    held.at[at], target.at[source], sems.at[4 + 2 * source + which]
                )
            )
            copies[-1].start()
    for copy in copies:
        copy.wait()


def collect(send_list, place, parts):
    slots = send_list.shape[1] * send_list.shape[2]
    own = jax.ShapeDtypeStruct((CHIPS, OWN) + TILE, BF16)
    return pl.pallas_call(
        functools.partial(collect_kernel, len(parts)),
        in_specs=[SMEM, SMEM] + [VMEM] * len(parts),
        out_specs=[HBM] * 3,
        out_shape=[jax.ShapeDtypeStruct((slots,) + TILE, BF16), own, own],
        scratch_shapes=[pltpu.VMEM((CHIPS * 2 * OWN,) + TILE, BF16)] * (len(parts) > 1)
        + [pltpu.VMEM((slots,) + TILE, BF16), pltpu.SemaphoreType.DMA((4 + 2 * CHIPS,))],
        compiler_params=params(0),
        cost_estimate=pl.CostEstimate(flops=0, bytes_accessed=5 << 20, transcendentals=0),
        name="collect",
    )(send_list, place, *parts)


def attend_kernel(chunk, carried, owner_ref, slot_ref, count_ref, place_ref, *refs):
    parts, (own_ref, swap_ref, mine_ref, other_ref) = refs[:CHIPS], refs[CHIPS : CHIPS + 4]
    befores, refs = refs[CHIPS + 4 : CHIPS + 4 + carried], refs[CHIPS + 4 + carried :]
    outs, refs = refs[:CHIPS], refs[CHIPS:]
    queries, made, keys, values, own_keys, own_values, asked, sems, done = refs[:9]
    z, core = place_ref[0], place_ref[1]

    asking = []
    for step in range(CHIPS):
        source = lax.rem(z + CHIPS - step, CHIPS)
        asking.append(
            pltpu.make_async_copy(parts[step].at[chunk], queries.at[source], asked.at[step])
        )
        asking[-1].start()

    def place_in(near, near_own, far, far_own):
        copies = [
            pltpu.make_async_copy(mine_ref, near, sems.at[0]),
            pltpu.make_async_copy(other_ref, far, sems.at[1]),
            pltpu.make_async_copy(own_ref, near_own, sems.at[2]),
            pltpu.make_async_copy(swap_ref, far_own, sems.at[3]),
        ]
        for copy in copies:
            copy.start()
        for copy in copies:
            copy.wait()

    @pl.when(core == 0)
    def _():
        place_in(keys, own_keys, values, own_values)

    @pl.when(core == 1)
    def _():
        place_in(values, own_values, keys, own_keys)

    for copy in asking:
        copy.wait()
    targets = outs
    if carried:
        before, taken, passed = refs[9:]
        taking = []
        for step in range(CHIPS):
            taking.append(
                pltpu.make_async_copy(befores[step], before.at[step], taken.at[step])
            )
            taking[-1].start()
        targets = [out.at[1] for out in outs]

    low = low_lanes(HALF)
    lane = lax.broadcasted_iota(jnp.int32, (1, LANES), 1)
    dims = (((1,), (1,)), ((), ()))
    rows = 2 * BLOCK
    group = OWN

    def attend_group(at, carry):
        ahead = lax.rem(at + 1, CHIPS)
        source, first = lax.rem(z + ahead, CHIPS), 0
        blocks = [source * 2 * OWN + core * OWN + first + k for k in range(group)]
        slots = [
            [owner_ref[entry, block] * CAP + slot_ref[entry, block] for entry in range(MAXK)]
            for block in blocks
        ]
        left = []
        for k in range(group):
            query = queries[source, first + k].astype(F32)
            turned = pltpu.roll(query, HDIM, 1)
            zero = jnp.zeros_like(query)
            left.append(
                jnp.concatenate(
                    [
                        jnp.where(low, query, zero),
                        jnp.where(low, turned, zero),
                        jnp.where(low, zero, turned),
                        jnp.where(low, zero, query),
                    ],
                    axis=0,
                ).astype(BF16)
            )
        near = []
        for quad in range(group // 4):
            four = own_keys[source, pl.ds(first + 4 * quad, 4)].reshape(LANES, LANES)
            scores = lax.dot_general(
                jnp.concatenate(left[4 * quad : 4 * quad + 4], axis=0),
                four,
                dims,
                preferred_element_type=F32,
            )
            for j in range(4):
                near.append(
                    jnp.where(lane // HALF == j, scores[j * rows : (j + 1) * rows], MASKED)
                )
        far = []
        for k in range(group):
            far_keys = jnp.concatenate([keys[slot] for slot in slots[k]], axis=0)
            scores = lax.dot_general(left[k], far_keys, dims, preferred_element_type=F32)
            limit = count_ref[blocks[k]] * HALF
            far.append(
                [
                    jnp.where(lane < limit, scores[:, :LANES], MASKED),
                    jnp.where(lane + LANES < limit, scores[:, LANES:], MASKED),
                ]
            )
        tops = []
        for k in range(group):
            top = jnp.maximum(jnp.maximum(far[k][0], far[k][1]), near[k])
            top = jnp.max(jnp.maximum(top[:BLOCK], top[BLOCK:]), axis=1, keepdims=True)
            tops.append(jnp.concatenate([top, top], axis=0))
        far = [[jnp.exp2((part - tops[k]) * SCALE) for part in far[k]] for k in range(group)]
        near = [jnp.exp2((near[k] - tops[k]) * SCALE) for k in range(group)]
        summed = []
        for quad in range(group // 4):
            four = own_values[source, pl.ds(first + 4 * quad, 4)].reshape(LANES, LANES)
            weights = [near[4 * quad + j].astype(BF16) for j in range(4)]
            product = jnp.dot(
                jnp.concatenate(weights, axis=0), four, preferred_element_type=F32
            )
            summed += [product[j * rows : (j + 1) * rows] for j in range(4)]
        for k in range(group):
            far_values = jnp.concatenate([values[slot] for slot in slots[k]], axis=0)
            weights = jnp.concatenate([part.astype(BF16) for part in far[k]], axis=1)
            summed[k] = summed[k] + jnp.dot(weights, far_values, preferred_element_type=F32)
        for k in range(group):
            total = far[k][0] + far[k][1] + near[k]
            total = jnp.sum(total[:BLOCK] + total[BLOCK:], axis=1, keepdims=True)
            share = 1.0 / total
            share = jnp.where(low, share[:HALF], share[HALF:])
            straight = jnp.where(low, summed[k][:HALF], summed[k][3 * HALF :])
            crossed = jnp.where(low, summed[k][HALF : 2 * HALF], summed[k][2 * HALF : 3 * HALF])
            result = (straight + pltpu.roll(crossed, HDIM, 1)) * share
            made[source, first + k] = result.astype(BF16)
        for step in range(CHIPS):

            @pl.when(ahead == step)
            def _():
                pltpu.make_async_copy(made.at[source], targets[step], done.at[step]).start()

        return carry

    lax.fori_loop(0, CHIPS * OWN // group, attend_group, 0)
    if carried:
        passing = []
        for step in range(CHIPS):
            taking[step].wait()
            passing.append(
                pltpu.make_async_copy(before.at[step], outs[step].at[0], passed.at[step])
            )
            passing[-1].start()
        for copy in passing:
            copy.wait()
    for step in range(CHIPS):
        source = lax.rem(z + step, CHIPS)
        pltpu.make_async_copy(made.at[source], targets[step], done.at[step]).wait()


def attend(tables, place, queries, own, swapped, mine, other, chunk, before=()):
    slots = mine.shape[0]
    blocks = pltpu.VMEM((CHIPS, OWN) + TILE, BF16)
    return pl.pallas_call(
        functools.partial(attend_kernel, chunk, len(before)),
        in_specs=[SMEM] * 4 + [HBM] * (CHIPS + 4 + len(before)),
        out_specs=[HBM] * CHIPS,
        out_shape=[jax.ShapeDtypeStruct((2,) * (len(before) > 0) + (OWN,) + TILE, BF16)] * CHIPS,
        scratch_shapes=[
            blocks,
            blocks,
            pltpu.VMEM((slots,) + TILE, BF16),
            pltpu.VMEM((slots,) + TILE, BF16),
            blocks,
            blocks,
            pltpu.SemaphoreType.DMA((CHIPS,)),
            pltpu.SemaphoreType.DMA((4,)),
            pltpu.SemaphoreType.DMA((CHIPS,)),
        ]
        + [blocks, pltpu.SemaphoreType.DMA((CHIPS,)), pltpu.SemaphoreType.DMA((CHIPS,))]
        * (len(before) > 0),
        compiler_params=params(0),
        cost_estimate=pl.CostEstimate(
            flops=64 * 4 * 128 * 128 * 384, bytes_accessed=8 << 20, transcendentals=64 * 128 * 384
        ),
        name="attend",
    )(*tables, place, *queries, own, swapped, mine, other, *before)


def normed(values, gain):
    center = values - jnp.mean(values, axis=-1, keepdims=True)
    spread = jnp.mean(center * center, axis=-1, keepdims=True)
    return center * lax.rsqrt(spread + 1e-05) * gain


def mixed_rows(held, half, weight):
    at = slice(half * 8, half * 8 + 8)
    pieces = [unpack_pair(held[2 * pair, at], held[2 * pair + 1, at]) for pair in range(2)]
    return jnp.dot(jnp.concatenate(pieces, axis=1), weight, preferred_element_type=F32)


def gather_parts(place_ref, parts, held, sems):
    copies = []
    for step in range(CHIPS):
        source = lax.rem(place_ref[0] + CHIPS - step, CHIPS)
        copies.append(pltpu.make_async_copy(parts[step], held.at[source], sems.at[step]))
        copies[-1].start()
    return copies


def gains_kernel(attn_ref, ffn_ref, out_ref):
    out_ref[0, :] = attn_ref[...]
    out_ref[1, :] = ffn_ref[...]


def stack_gains(gain_attn, gain_ffn):
    return pl.pallas_call(
        gains_kernel,
        in_specs=[VMEM, VMEM],
        out_specs=VMEM,
        out_shape=jax.ShapeDtypeStruct((2,) + gain_attn.shape, F32),
        compiler_params=params(0),
        name="gains",
    )(gain_attn, gain_ffn)


def mix_kernel(place_ref, feat_ref, *refs):
    parts, (weight_ref, out_ref, *scratch) = refs[:CHIPS], refs[CHIPS:]
    held, feats, weight, made, arrive, sems = scratch
    rows = feat_ref.shape[0] // 2
    arriving = []
    for which in range(CHUNKS - 1):
        some = [part.at[which] for part in parts]
        arriving += gather_parts(place_ref, some, held.at[which], arrive.at[which])
    fetches = [
        pltpu.make_async_copy(weight_ref.at[: (CHUNKS - 1) * COLS], weight, sems.at[0]),
        pltpu.make_async_copy(feat_ref, feats, sems.at[1]),
    ]
    for copy in fetches:
        copy.start()
    for copy in arriving + fetches:
        copy.wait()
    copies = []
    for half in range(2):
        at = slice(half * rows, (half + 1) * rows)
        mixed = feats[at, :].astype(F32)
        for which in range(CHUNKS - 1):
            part = weight[which * COLS : (which + 1) * COLS, :]
            mixed = mixed + mixed_rows(held.at[which], half, part)
        made[at, :] = mixed
        copies.append(pltpu.make_async_copy(made.at[at], out_ref.at[at], sems.at[2 + half]))
        copies[-1].start()
    for copy in copies:
        copy.wait()


def mix(place, features, back, w_out):
    rows, width = features.shape
    early = (CHUNKS - 1) * COLS
    return pl.pallas_call(
        mix_kernel,
        in_specs=[SMEM] + [HBM] * (CHIPS + 2),
        out_specs=HBM,
        out_shape=jax.ShapeDtypeStruct((rows, width), F32),
        scratch_shapes=[
            pltpu.VMEM((CHUNKS - 1, CHIPS, OWN) + TILE, BF16),
            pltpu.VMEM((rows, width), BF16),
            pltpu.VMEM((early, width), BF16),
            pltpu.VMEM((rows, width), F32),
            pltpu.SemaphoreType.DMA((CHUNKS - 1, CHIPS)),
            pltpu.SemaphoreType.DMA((4,)),
        ],
        compiler_params=params(0),
        cost_estimate=pl.CostEstimate(
            flops=2 * rows * early * width, bytes_accessed=7 << 20, transcendentals=0
        ),
        name="mix",
    )(place, features, *back, w_out)


def finish_kernel(place_ref, mixed_ref, *refs):
    parts, refs = refs[:CHIPS], refs[CHIPS:]
    out_w_ref, up_ref, down_ref, gain_ref, result_ref, *scratch = refs
    held, early, out_w, up, down, made, arrive, sems = scratch
    rows = mixed_ref.shape[0] // 2
    halves = [slice(half * rows, (half + 1) * rows) for half in range(2)]
    arriving = gather_parts(place_ref, parts, held, arrive)
    copies = [
        pltpu.make_async_copy(out_w_ref.at[(CHUNKS - 1) * COLS :], out_w, sems.at[0]),
        pltpu.make_async_copy(mixed_ref.at[halves[0]], early.at[halves[0]], sems.at[1]),
        pltpu.make_async_copy(mixed_ref.at[halves[1]], early.at[halves[1]], sems.at[2]),
        pltpu.make_async_copy(up_ref, up, sems.at[3]),
        pltpu.make_async_copy(down_ref, down, sems.at[4]),
    ]
    for which in (0, 1, 3, 4, 2):
        copies[which].start()
    for copy in arriving:
        copy.wait()
    copies[0].wait()
    rows = rows // 2
    for half, at in enumerate(halves):
        added = mixed_rows(held, half, out_w[...])
        copies[1 + half].wait()
        whole = normed(early[at, :] + added, gain_ref[0:1, :]).astype(BF16)
        for part in range(2):
            first = whole[part * rows : (part + 1) * rows]
            row = (half * 2 + part) * rows
            if half + part == 0:
                copies[3].wait()
            hidden = jnp.dot(first, up[...], preferred_element_type=F32)
            hidden = jnp.maximum(hidden, 0.0).astype(BF16)
            if half + part == 0:
                copies[4].wait()
            total = first.astype(F32) + jnp.dot(hidden, down[...], preferred_element_type=F32)
            made[row : row + rows, :] = normed(total, gain_ref[1:2, :]).astype(BF16)
            copies.append(
                pltpu.make_async_copy(
                    made.at[row : row + rows],
                    result_ref.at[row : row + rows],
                    sems.at[5 + half * 2 + part],
                )
            )
            copies[-1].start()
    for copy in copies[5:]:
        copy.wait()


def finish(place, mixed, back, w_out, w_up, w_down, gains):
    rows, width = mixed.shape
    return pl.pallas_call(
        finish_kernel,
        in_specs=[SMEM] + [HBM] * (CHIPS + 4) + [VMEM],
        out_specs=HBM,
        out_shape=jax.ShapeDtypeStruct((rows, width), BF16),
        scratch_shapes=[
            pltpu.VMEM((CHIPS, OWN) + TILE, BF16),
            pltpu.VMEM((rows, width), F32),
            pltpu.VMEM((COLS, width), BF16),
            pltpu.VMEM(w_up.shape, BF16),
            pltpu.VMEM(w_down.shape, BF16),
            pltpu.VMEM((rows, width), BF16),
            pltpu.SemaphoreType.DMA((CHIPS,)),
            pltpu.SemaphoreType.DMA((9,)),
        ],
        compiler_params=params(0),
        name="finish",
    )(place, mixed, *back, w_out, w_up, w_down, gains)


def swap(array):
    return lax.ppermute(array, "head", [(i, i ^ 1) for i in range(2 * CHIPS)])


def along_z(parts):
    moved = list(parts)
    for step in (2, 1, 3):
        moved[step] = lax.ppermute(
            parts[step], "head", [(i, (i + 2 * step) % (2 * CHIPS)) for i in range(2 * CHIPS)]
        )
    return moved


def per_device(
    features, w_query, w_key, w_value, w_out, w_up, w_down, gain_attn, gain_ffn,
    send_list, edge_owner, edge_slot, edge_count,
):
    head = lax.axis_index("head").astype(jnp.int32)
    place = jnp.stack([head // 2, head % 2])
    groups = send_list.shape[1]
    owners, slots = edge_owner.T, edge_slot.T
    far = swap(features)
    collected = []
    for c in range(CHUNKS):
        if c == 0:
            whole = project_first(features, w_key, w_value)
            whole = lax.all_to_all(whole, "head", split_axis=0, concat_axis=0, tiled=True)
            parts = [whole.reshape((-1,) + TILE)]
        else:
            parts = project_keys_values(place, features, far, w_key, w_value, c)
            parts = along_z(parts)
        collected.append(collect(send_list, place, parts))
    queries = along_z(project_queries(place, features, w_query))
    mines = []
    for c in range(CHUNKS):
        sent = collected[c][0].reshape((groups, CAP) + TILE)
        got = lax.all_to_all(sent, "node", split_axis=0, concat_axis=0, tiled=True)
        mines.append(got.reshape((groups * CAP,) + TILE))
    backs = []
    for c in range(CHUNKS):
        swapped = swap(collected[c][2])
        other = swap(mines[c])
        tables = (owners, slots, edge_count)
        before = done if c == 1 else ()
        done = attend(tables, place, queries, collected[c][1], swapped, mines[c], other, c, before)
        if c > 0:
            backs.append(along_z(done))
    gains = stack_gains(gain_attn, gain_ffn)
    mixed = mix(place, features, backs[0], w_out)
    return finish(place, mixed, backs[1], w_out, w_up, w_down, gains)


def solution(mesh):
    return jax.shard_map(
        per_device,
        mesh=mesh,
        in_specs=(
            P(("node", "head"), None),
            P(), P(), P(), P(), P(), P(), P(), P(),
            P("node", None, None),
            P("node", None),
            P("node", None),
            P("node"),
        ),
        out_specs=P(("node", "head"), None),
        check_vma=False,
    )
```
